32 devices in a mesh: dp: 2 (over x), expert: 4 (over y, core), mp: 4 (over z).
Axes of the slice: x: 2, y: 2, z: 4, core: 2. Of those that a mesh axis runs over, the one named last changes fastest.
Arguments:
- inputs: bfloat16 [8192, 512], P(('dp', 'expert')), may hold values from -6 to 6
- teacher: bfloat16 [8192, 512], P(('dp', 'expert'), 'mp'), may hold values from -6 to 6
- top_experts: int32 [8192, 2], P(('dp', 'expert')), may hold values from 0 to 7, all different within a row
- priority: int32 [8, 1024], P(('dp', 'expert')), may hold values from 0 to 1023, each once within a row
- valid_mask: int32 [8192], P(('dp', 'expert')), may hold values 0 or 1
- blocks: int32 [8, 1024], P(('dp', 'expert')), may hold values from 0 to 3, never falling along the last dimension, each value on 1 to 512 neighbouring positions
- query_weight: bfloat16 [512, 512], P(None, 'mp'), may hold values from -0.25 to 0.25
- key_weight: bfloat16 [512, 512], P(None, 'mp'), may hold values from -0.25 to 0.25
- value_weight: bfloat16 [512, 512], P(None, 'mp'), may hold values from -0.25 to 0.25
- out_weight: bfloat16 [512, 512], P('mp'), may hold values from -3.5 to 3.5
- router: float32 [512, 8], replicated, may hold values from -0.1875 to 0.1875
- expert_in: bfloat16 [8, 512, 2048], P(('dp', 'expert'), None, 'mp'), may hold values from -0.25 to 0.25
- expert_out: bfloat16 [8, 2048, 512], P(('dp', 'expert'), 'mp'), may hold values from -0.75 to 0.75
- first_gain: float32 [512], replicated, may hold values from 0.5 to 1.5
- first_bias: float32 [512], replicated, may hold values from -1.25 to 1.25
- second_gain: float32 [512], replicated, may hold values from 0.5 to 1.5
- second_bias: float32 [512], replicated, may hold values from -1.25 to 1.25
Outputs:
- output: bfloat16 [8192, 512], P(('dp', 'expert'), 'mp')
- sequence_loss: float32 [8], P(('dp', 'expert'))
- input_grad: float32 [8192, 512], P(('dp', 'expert'), 'mp')
- query_grad: float32 [512, 512], P(None, 'mp')
- key_grad: float32 [512, 512], P(None, 'mp')
- value_grad: float32 [512, 512], P(None, 'mp')
- out_grad: float32 [512, 512], P('mp')
- router_grad: float32 [512, 8], replicated
- expert_in_grad: float32 [8, 512, 2048], P(('dp', 'expert'), None, 'mp')
- expert_out_grad: float32 [8, 2048, 512], P(('dp', 'expert'), 'mp')
- first_gain_grad: float32 [512], replicated
- first_bias_grad: float32 [512], replicated
- second_gain_grad: float32 [512], replicated
- second_bias_grad: float32 [512], replicated
The draws below stay inside these ranges and needn't reach their ends.
Inputs may be any that keep to these rules, and one draw needn't show every extreme that they name: `top_experts`: the two experts of a token differ; every expert is named by some token. `priority`: each row is a permutation of the positions 0 to 1023. `blocks`: along each row the number never falls and starts at 0; each block holds 1 to 512 positions.
All inputs are finite; a program needn't handle non-finite values. No bound on the sum of `valid_mask` on one device may be relied on, other than what follows from the above.
Results may differ from the reference program's by a relative error of at most 0.01.
Values may be sent and summed in bfloat16 or wider, within the bound.
A program may use at most 128 MiB of HBM per device.

```python
import math
import jax
import jax.numpy as jnp
import numpy as np
from jax import lax

D = 512
HEADS = 8
HEAD_DIM = 64
FF = 2048
TOK_GRP = 1024
BLOCK = 256
GROUPS = 8
EXPERTS = 8
TOKENS = 8192
CAP = 268


def touch_ends(array, rng, low, largest):
    index_at = [jax.random.randint(jax.random.fold_in(rng, axis), (), 0, length) for axis, length in enumerate(array.shape)]
    main_axis = array.shape.index(max(array.shape))
    next_to = index_at[:main_axis] + [(index_at[main_axis] + 1) % array.shape[main_axis]] + index_at[main_axis + 1:]
    return array.at[tuple(index_at)].set(low).at[tuple(next_to)].set(largest)


def shard_levels(key, shape, shards, smallest, high):
    def one(axis_at, parts):
        heights = jax.random.uniform(jax.random.fold_in(jax.random.fold_in(key, 6), axis_at), (parts,), jnp.float32, smallest / len(shards), high / len(shards))
        return jnp.repeat(jnp.exp(heights), shape[axis_at] // parts).reshape((-1,) + (1,) * (len(shape) - axis_at - 1))

    level = one(*shards[0])
    for cut in shards[1:]:
        level = level * one(*cut)
    return level


def distinct(own_key, rows, number_of, top, lift):
    sequence = jax.random.permutation(jax.random.fold_in(own_key, 1), number_of)
    pull = sequence
    for power in range(3):
        pull = pull * pull // number_of
    pull = pull * lift // number_of
    chance = jax.random.randint(jax.random.fold_in(own_key, 2), (rows, number_of), 0, 4096) + pull
    holders = jax.random.permutation(jax.random.fold_in(own_key, 3), rows)[jnp.arange(number_of) % rows]
    chance = jnp.where(jnp.arange(rows)[:, None] == holders[None, :], 1 << 14, chance)
    score = chance * number_of + jnp.arange(number_of)
    return lax.top_k(score.astype(jnp.int32), top)[1].astype(jnp.int32)


def profile(amount, total, reach, skew):
    portions = [(1 << 20) // math.isqrt(grade ** skew) + 1 for grade in range(2, amount + 1)]
    rest, holding = total - reach - (amount - 1), [1] * (amount - 1)
    while rest > 0:
        movable = [i for i in range(amount - 1) if holding[i] < reach]
        mass, left = sum([portions[i] for i in movable]), rest
        for i in movable:
            addition = min(reach - holding[i], max(1, left * portions[i] // mass), rest)
            holding[i] = holding[i] + addition
            rest = rest - addition
    return np.array([reach] + holding)


def ragged(key, count, total, bound, skew):
    if count == 2:
        one = jax.random.randint(key, (), max(1, total - bound), min(bound, total - 1) + 1)
        return jnp.stack([one, total - one])
    sizes = jnp.asarray(profile(count, total, bound, skew), jnp.int32)
    couples = (count - 1) // 2
    giver, receiver = sizes[1:1 + 2 * couples:2], sizes[2:2 + 2 * couples:2]
    slack = jnp.minimum(giver - 1, bound - receiver)
    moved = jax.random.randint(jax.random.fold_in(key, 1), (couples,), 0, 1 << 20) % (slack + 1)
    sizes = sizes.at[1:1 + 2 * couples:2].set(giver - moved).at[2:2 + 2 * couples:2].set(receiver + moved)
    return sizes[jax.random.permutation(jax.random.fold_in(key, 2), count)]


def scatter_about(rng, shape, spread, most, split=(), kind=jnp.bfloat16):
    result = spread * jax.random.normal(rng, shape, jnp.float32)
    if split:
        result = result * shard_levels(rng, shape, split, -0.22, 0.18)
    return jnp.clip(result, -most, most).astype(kind)


def setup_inputs(seed: int = 0) -> dict:
    key_list = jax.random.split(jax.random.key(seed), 18)
    inputs = scatter_about(key_list[0], (TOKENS, D), 1.0, 6.0, ((0, 8),))
    teacher = scatter_about(key_list[1], (TOKENS, D), 1.0, 6.0, ((0, 8), (1, 4)))
    top_experts = distinct(key_list[2], TOKENS, EXPERTS, 2, 2048)
    priority = jax.vmap(lambda own: jax.random.permutation(own, TOK_GRP))(jax.random.split(key_list[3], GROUPS)).reshape((GROUPS, TOK_GRP)).astype(jnp.int32)
    valid_mask = touch_ends((jax.random.randint(key_list[4], (TOKENS,), 0, 8) < 7).astype(jnp.int32), jax.random.fold_in(key_list[4], 1), 0, 1)
    blocks = jax.vmap(lambda own: jnp.searchsorted(jnp.cumsum(ragged(own, TOK_GRP // BLOCK, TOK_GRP, 2 * BLOCK, 1)), jnp.arange(TOK_GRP), side="right"))(jax.random.split(key_list[5], GROUPS)).reshape((GROUPS, TOK_GRP)).astype(jnp.int32)
    query_weight = scatter_about(key_list[6], (D, D), D ** -0.5, 0.25, ((1, 4),))
    key_weight = scatter_about(key_list[7], (D, D), D ** -0.5, 0.25, ((1, 4),))
    value_weight = scatter_about(key_list[8], (D, D), D ** -0.5, 0.25, ((1, 4),))
    out_weight = scatter_about(key_list[9], (D, D), (0.4 * TOK_GRP ** 0.5 * D ** -0.5), 3.5, ((0, 4),))
    router = scatter_about(key_list[10], (D, EXPERTS), (2 * D) ** -0.5, 0.1875, (), jnp.float32)
    expert_in = scatter_about(key_list[11], (EXPERTS, D, FF), D ** -0.5, 0.25, ((0, 8), (2, 4)))
    expert_out = scatter_about(key_list[12], (EXPERTS, FF, D), (0.75 * EXPERTS * FF ** -0.5), 0.75, ((0, 8), (1, 4)))
    first_gain = jnp.clip(1.0 + 0.1 * jax.random.normal(key_list[13], (D,), jnp.float32), 0.5, 1.5)
    first_bias = scatter_about(key_list[14], (D,), 0.2, 1.25, (), jnp.float32)
    second_gain = jnp.clip(1.0 + 0.1 * jax.random.normal(key_list[15], (D,), jnp.float32), 0.5, 1.5)
    second_bias = scatter_about(key_list[16], (D,), 0.2, 1.25, (), jnp.float32)
    return {"inputs": inputs, "teacher": teacher, "top_experts": top_experts, "priority": priority, "valid_mask": valid_mask, "blocks": blocks, "query_weight": query_weight, "key_weight": key_weight, "value_weight": value_weight, "out_weight": out_weight, "router": router, "expert_in": expert_in, "expert_out": expert_out, "first_gain": first_gain, "first_bias": first_bias, "second_gain": second_gain, "second_bias": second_bias}


@jax.custom_vjp
def low(v):
    return lax.optimization_barrier(v.astype(jnp.bfloat16)).astype(jnp.float32)

@jax.custom_vjp
def low_back(v):
    return v

def low_keep(v):
    return (low(v), None)

def low_pass(kept, grad):
    return (grad,)

def back_keep(v):
    return (v, None)

def back_low(kept, grad):
    return (low(grad),)
low.defvjp(low_keep, low_pass)
low_back.defvjp(back_keep, back_low)
EPSILON = 1e-06
HIGHEST = lax.Precision.HIGHEST

def normalize(values, gain_row, bias_row):
    center = values - lax.optimization_barrier(jnp.mean(values, axis=-1, keepdims=True))
    inverse = lax.rsqrt(lax.optimization_barrier(jnp.mean(center * center, axis=-1, keepdims=True)) + EPSILON)
    return center * inverse * gain_row + bias_row

def assign_slots(chosen, claim_order):
    length = chosen.shape[0]
    ordered = jnp.concatenate([chosen[claim_order, 0], chosen[claim_order, 1]])
    catalog = jnp.arange(EXPERTS, dtype=jnp.int32)
    onehot = (ordered[:, None] == catalog[None, :]).astype(jnp.int32)
    before = jnp.cumsum(onehot, axis=0) - onehot
    ranked = lax.optimization_barrier(jnp.sum(before * onehot, axis=1))
    owners = jnp.concatenate([claim_order, claim_order])
    columns = jnp.concatenate([jnp.zeros((length,), jnp.int32), jnp.ones((length,), jnp.int32)])
    slot_rank = jnp.zeros((length, 2), jnp.int32).at[owners, columns].set(ranked)
    retained = slot_rank < CAP
    slot_index = chosen * CAP + jnp.minimum(slot_rank, CAP - 1)
    drop_index = jnp.where(retained, slot_index, EXPERTS * CAP)
    numbers = jnp.broadcast_to(jnp.arange(length, dtype=jnp.int32)[:, None], (length, 2))
    token_of_slot = jnp.full((EXPERTS * CAP,), length, jnp.int32).at[drop_index].set(numbers, mode='drop')
    return (slot_index, retained, token_of_slot)

def attend(query_block, query_ids, key_heads, value_heads, key_ids):
    scores = jnp.einsum('hqd,hkd->hqk', query_block, key_heads, precision=HIGHEST)
    scores = low_back(scores)
    allowed = key_ids[None, None, :] <= query_ids[None, :, None]
    scores = jnp.where(allowed, scores, -1e+30)
    weights = low(jax.nn.softmax(scores, axis=-1))
    return jnp.einsum('hqk,hkd->hqd', weights, value_heads, precision=HIGHEST)

def group_forward(params, tokens_in, teacher_rows, valid_rows, block_ids, chosen, slot_index, retained, token_of_slot):
    query_weight, key_weight, value_weight, out_weight, router, expert_in, expert_out, first_gain, first_bias, second_gain, second_bias = params
    length = tokens_in.shape[0]
    normed = low(normalize(tokens_in, first_gain, first_bias))
    queries = low(low_back(jnp.dot(normed, query_weight, precision=HIGHEST) * 0.125))
    keys = low(low_back(jnp.dot(normed, key_weight, precision=HIGHEST)))
    values = low(low_back(jnp.dot(normed, value_weight, precision=HIGHEST)))

    def split_heads(matrix):
        return matrix.reshape(length, HEADS, HEAD_DIM).transpose(1, 0, 2)
    block_rows = min(512, length)
    block_total = length // block_rows
    query_blocks = split_heads(queries).reshape(HEADS, block_total, block_rows, HEAD_DIM).transpose(1, 0, 2, 3)
    id_blocks = block_ids.reshape(block_total, block_rows)
    key_heads = split_heads(keys)
    value_heads = split_heads(values)

    def one_block(paired):
        return attend(paired[0], paired[1], key_heads, value_heads, block_ids)
    mixture = lax.map(jax.checkpoint(one_block), (query_blocks, id_blocks))
    mixture = low(low_back(mixture.transpose(0, 2, 1, 3).reshape(length, D)))
    attended = low_back(jnp.dot(mixture, out_weight, precision=HIGHEST))
    hidden = tokens_in + attended
    normed_two = normalize(hidden, second_gain, second_bias)
    gates_all = jax.nn.softmax(jnp.dot(normed_two, router, precision=HIGHEST), axis=-1)
    sendable = jnp.concatenate([low(normed_two), jnp.zeros((1, D), jnp.float32)])
    dispatched = low_back(sendable[token_of_slot]).reshape(EXPERTS, CAP, D)
    inner = low_back(jnp.einsum('ecd,edf->ecf', dispatched, expert_in, precision=HIGHEST))
    activated = low(jax.nn.gelu(inner))
    returned = low_back(low(jnp.einsum('ecf,efd->ecd', activated, expert_out, precision=HIGHEST)))
    returned = returned.reshape(EXPERTS * CAP, D)
    gate_pair = jnp.take_along_axis(gates_all, chosen, axis=1) * retained.astype(jnp.float32)
    combined = lax.optimization_barrier(jnp.sum(gate_pair[:, :, None] * returned[slot_index], axis=1))
    final_rows = hidden + combined
    residue = final_rows - teacher_rows
    objective = 0.5 * jnp.sum(valid_rows[:, None] * residue * residue)
    return (final_rows, objective)

def reference(inputs, teacher, top_experts, priority, valid_mask, blocks, query_weight, key_weight, value_weight, out_weight, router, expert_in, expert_out, first_gain, first_bias, second_gain, second_bias):
    params = tuple((tensor.astype(jnp.float32) for tensor in (query_weight, key_weight, value_weight, out_weight, router, expert_in, expert_out, first_gain, first_bias, second_gain, second_bias)))
    grouped = (inputs.reshape(GROUPS, TOK_GRP, D).astype(jnp.float32), teacher.reshape(GROUPS, TOK_GRP, D).astype(jnp.float32), top_experts.reshape(GROUPS, TOK_GRP, 2), priority, valid_mask.reshape(GROUPS, TOK_GRP).astype(jnp.float32), blocks)

    def per_group(running, group_data):
        group_inputs, group_teacher, group_chosen, group_order, group_valid, group_blocks = group_data
        slot_index, retained, token_of_slot = assign_slots(group_chosen, group_order)

        def forward(weights, tokens_in):
            return group_forward(weights, tokens_in, group_teacher, group_valid, group_blocks, group_chosen, slot_index, retained, token_of_slot)
        (final_rows, objective), pullback = jax.vjp(forward, params, group_inputs)
        weight_grads, input_grad = pullback((jnp.zeros_like(final_rows), jnp.ones_like(objective)))
        running = jax.tree.map(lambda first, second: first + second, running, weight_grads)
        return (running, (final_rows.astype(jnp.bfloat16), objective / (TOK_GRP * D), input_grad))
    initial = jax.tree.map(jnp.zeros_like, params)
    running, (outputs, losses, input_grads) = lax.scan(per_group, initial, grouped)
    return (outputs.reshape(TOKENS, D), losses, input_grads.reshape(TOKENS, D), running[0], running[1], running[2], running[3], running[4], running[5], running[6], running[7], running[8], running[9], running[10])
```

```python
import functools

import jax
import jax.numpy as jnp
from jax import lax
from jax.experimental import pallas as pl
from jax.experimental.pallas import tpu as pltpu
from jax.sharding import PartitionSpec as P

HEAD_DIM = 64
EPSILON = 1e-06
HIGHEST = lax.Precision.HIGHEST
MESH = pl.DeviceIdType.MESH
F32 = jnp.float32
BF16 = jnp.bfloat16
I32 = jnp.int32
VMEM_LIMIT = 62 * 1024 * 1024


def standardize(values):
    center = values - jnp.mean(values, axis=-1, keepdims=True)
    inverse = lax.rsqrt(jnp.mean(center * center, axis=-1, keepdims=True) + EPSILON)
    return (center * inverse, inverse)


def dot(a, b, precision=None):
    return jnp.dot(a, b, preferred_element_type=F32, precision=precision)


def dot_nt(a, b, precision=None):
    return lax.dot_general(
        a, b, (((1,), (1,)), ((), ())), preferred_element_type=F32, precision=precision
    )


def dot_tn(a, b, precision=None):
    return lax.dot_general(
        a, b, (((0,), (0,)), ((), ())), preferred_element_type=F32, precision=precision
    )


def remote(src, dst, send, recv, device):
    return pltpu.make_async_remote_copy(
        src_ref=src, dst_ref=dst, send_sem=send, recv_sem=recv, device_id=device, device_id_type=MESH
    )


def lanes(f, width):
    return pl.ds(pl.multiple_of(f * width, width), width)


def rows_at(s, count, unit):
    return pl.ds(pl.multiple_of(s * count, unit), count)


def loop(low, high, body):
    def step(i, carry):
        body(i)
        return carry

    lax.fori_loop(low, high, step, 0)


class Place:
    def __init__(self, dims):
        self.dp, self.ex, self.mp = dims
        self.n = self.dp * self.ex
        self.me = lax.axis_index("dp") * self.ex + lax.axis_index("expert")
        self.z = lax.axis_index("mp")

    def ahead(self, k):
        return lax.rem(self.me + k, self.n)

    def behind(self, k):
        return lax.rem(self.me + self.n - k, self.n)

    def plane(self, p):
        return {"dp": p // self.ex, "expert": lax.rem(p, self.ex)}

    def zahead(self, j):
        return lax.rem(self.z + j, self.mp)

    def barrier(self):
        sem = pltpu.get_barrier_semaphore()

        def greet(k):
            pl.semaphore_signal(
                sem, inc=1, device_id=self.plane(self.ahead(k)), device_id_type=MESH
            )

        loop(1, self.n, greet)
        for j in range(1, self.mp):
            pl.semaphore_signal(
                sem, inc=1, device_id={"mp": self.zahead(j)}, device_id_type=MESH
            )
        pl.semaphore_wait(sem, self.n - 1 + self.mp - 1)


def feature_order(mp):
    return [i // 2 if i % 2 == 0 else mp - 1 - i // 2 for i in range(mp)]


TB = 256


def moe_kernel(
    dims,
    capacity,
    experts,
    x_ref,
    mix_ref,
    wo_ref,
    g2_ref,
    b2_ref,
    rt_ref,
    top_ref,
    pri_ref,
    val_ref,
    tea_ref,
    win_ref,
    wout_ref,
    out_ref,
    loss_ref,
    gho_ref,
    ga_ref,
    vec_ref,
    gwin_ref,
    gwout_ref,
    mixf,
    wof,
    hid,
    n2b,
    posc,
    sidc,
    sidr,
    gcol,
    grow_t,
    valc,
    disp,
    comb,
    gsl,
    gg,
    sbuf,
    rows,
    dgelu,
    act,
    obuf,
    ret,
    pbuf,
    rbuf,
    own,
    gf,
    grows,
    gi,
    msg,
    rmsg,
    s_a,
    r_a,
    s_d,
    r_d,
    s_r,
    r_r,
    s_p,
    r_p,
    s_g,
    r_g,
    s_d2,
    r_d2,
    s_r2,
    r_r2,
    s_p2,
    r_p2,
    s_g2,
    r_g2,
    s_m,
    r_m,
):
    place = Place(dims)
    n, mp, me, z = place.n, place.mp, place.me, place.z
    tokens, width = x_ref.shape
    share = width // mp
    blocks = tokens // TB
    slots = ret.shape[0]
    room = slots // n
    unit = 16
    order = feature_order(mp)
    mine = lanes(z, share)

    place.barrier()

    for c in range(blocks):
        for j in range(1, mp):
            remote(
                mix_ref.at[pl.ds(c * TB, TB)],
                mixf.at[pl.ds(c * TB, TB), mine],
                s_a.at[c, j],
                r_a.at[c, z],
                {"mp": place.zahead(j)},
            ).start()
    mixf[:, mine] = mix_ref[...]
    for j in range(mp):
        wof[rows_at(lax.rem(z + mp - j, mp), share, share), :] = wo_ref[j]

    lane_t = lax.broadcasted_iota(I32, (TB, tokens), 1)
    sub_t = lax.broadcasted_iota(I32, (TB, tokens), 0)
    lane_k = lax.broadcasted_iota(I32, (TB, 128), 1)

    def positions(b):
        at = rows_at(b, TB, TB)
        hit = (sub_t + b * TB) == pri_ref[...]
        pos = jnp.sum(jnp.where(hit, lane_t.astype(F32), 0.0), axis=1, keepdims=True)
        posc[at, :] = pos
        flat = jnp.transpose(jnp.broadcast_to(pos, (TB, 128)))
        sidr[2:3, at] = flat[0:1]
        vt = jnp.transpose(jnp.broadcast_to(val_ref[:, at].astype(F32), (128, TB)))
        valc[at, :] = vt[:, 0:1]

    loop(0, blocks, positions)

    lane_all = lax.broadcasted_iota(I32, (tokens, 128), 1)
    first = top_ref[:, 0:1]
    second = top_ref[:, 1:2]
    named = jnp.where(
        ((lane_all < experts) & (first == lane_all))
        | ((lane_all >= experts) & (second == lane_all - experts)),
        1.0,
        0.0,
    ).astype(BF16)
    total = jnp.sum(
        jnp.where(first == lane_all - experts, 1.0, 0.0), axis=0, keepdims=True
    )
    pos_row = sidr[2:3, :]

    def ranks(b):
        at = rows_at(b, TB, TB)
        earlier = jnp.where(pos_row < posc[at, :], 1.0, 0.0).astype(BF16)
        count = dot(earlier, named)
        e0 = top_ref[at, 0:1]
        e1 = top_ref[at, 1:2]
        r0 = jnp.sum(jnp.where(lane_k == e0, count, 0.0), axis=1, keepdims=True)
        r1 = jnp.sum(jnp.where(lane_k == e1 + experts, count + total, 0.0), axis=1, keepdims=True)
        id0 = jnp.where(r0 < capacity, e0.astype(F32) * room + r0, -1.0)
        id1 = jnp.where(r1 < capacity, e1.astype(F32) * room + r1, -1.0)
        both = jnp.where(lane_k == 0, id0, jnp.where(lane_k == 1, id1, 0.0))
        both = jnp.where(lane_k == 3, e0.astype(F32), jnp.where(lane_k == 4, e1.astype(F32), both))
        sidc[at, :] = both
        flat = jnp.transpose(both)
        sidr[0:2, at] = flat[0:2]
        sidr[3:5, at] = flat[3:5]

    loop(0, blocks, ranks)

    sub_e = lax.broadcasted_iota(I32, (experts, TB), 0)

    def second_norm(b):
        at = rows_at(b, TB, TB)
        for j in range(1, mp):
            src = place.zahead(j)
            remote(
                mix_ref.at[pl.ds(0, TB)],
                mixf.at[at, lanes(src, share)],
                s_a.at[0, 0],
                r_a.at[b, src],
                {"mp": src},
            ).wait_recv()
        hidden = x_ref[at, :].astype(F32) + dot(mixf[at, :], wof[...])
        hid[at, :] = hidden
        normal, _ = standardize(hidden)
        normed = normal * g2_ref[...] + b2_ref[...]
        n2b[at, :] = normed.astype(BF16)
        logits = dot_nt(rt_ref[...], normed, HIGHEST)
        logits = jnp.exp(logits - jnp.max(logits, axis=0, keepdims=True))
        gates = logits / jnp.sum(logits, axis=0, keepdims=True)
        grow_t[0:experts, at] = gates
        for j in range(2):
            chosen = sidr[3 + j : 4 + j, at].astype(I32)
            gate = jnp.sum(jnp.where(sub_e == chosen, gates, 0.0), axis=0, keepdims=True)
            gate = jnp.where(sidr[j : j + 1, at] >= 0.0, gate, 0.0)
            sidr[5 + j : 6 + j, at] = gate
            gcol[j, at, :] = jnp.transpose(jnp.broadcast_to(gate, (128, TB)))[:, 0:1]

    loop(0, blocks, second_norm)

    sub_c = lax.broadcasted_iota(I32, (room, tokens), 0).astype(F32)

    def fill(k):
        e = place.ahead(k)
        base = (e * room).astype(F32)
        hit0 = sidr[0:1, :] == sub_c + base
        hit1 = sidr[1:2, :] == sub_c + base
        pick = jnp.where(hit0 | hit1, 1.0, 0.0).astype(BF16)
        disp[e] = pick
        gsl[e] = jnp.sum(
            jnp.where(hit0, sidr[5:6, :], jnp.where(hit1, sidr[6:7, :], 0.0)), axis=1, keepdims=True
        )
        return e, dot(pick, n2b[...]).astype(BF16)

    def dispatch_copy(k):
        e = place.ahead(k)
        return remote(
            sbuf.at[rows_at(e, room, unit)],
            rows.at[rows_at(me, room, unit)],
            s_d.at[k],
            r_d.at[k],
            place.plane(e),
        )

    def dispatch(k):
        e, out = fill(k)
        sbuf[rows_at(e, room, unit), :] = out

        @pl.when(k >= 2)
        def _():
            dispatch_copy(k - 1).start()

    loop(1, n, dispatch)
    e, out = fill(n)
    rows[rows_at(e, room, unit), :] = out
    dispatch_copy(n - 1).start()

    def weigh(b):
        at = rows_at(b, TB, TB)
        slot = lax.broadcasted_iota(I32, (TB, slots), 1).astype(F32)
        comb[at, :] = jnp.where(
            sidc[at, 0:1] == slot,
            gcol[0, at, :],
            jnp.where(sidc[at, 1:2] == slot, gcol[1, at, :], 0.0),
        ).astype(BF16)

    loop(0, blocks, weigh)

    def arrived(buf, recv, send, src):
        remote(
            buf.at[rows_at(src, room, unit)],
            buf.at[rows_at(src, room, unit)],
            send,
            recv,
            place.plane(src),
        ).wait_recv()

    root = 0.7978845608028654
    cube = 0.044715

    def expert_in(k):
        s = place.behind(k)

        @pl.when(k > 0)
        def _():
            arrived(rows, r_d.at[k], s_d.at[k], s)

        at = rows_at(s, room, unit)
        inner = dot(rows[at, :], win_ref[...])
        square = inner * inner
        wave = jnp.tanh(root * inner * (1.0 + cube * square))
        half = 0.5 * (1.0 + wave)
        act[at, :] = (inner * half).astype(BF16)
        dgelu[at, :] = half + 0.5 * inner * (1.0 - wave * wave) * (
            root * (1.0 + 3.0 * cube * square)
        )

    loop(0, n, expert_in)

    def return_copy(sends, recvs, i, f, k):
        s = place.behind(k)
        return remote(
            obuf.at[rows_at(s, room, unit), lanes(f, share)],
            ret.at[rows_at(me, room, unit), lanes(f, share)],
            sends.at[i, k],
            recvs.at[i, k],
            place.plane(s),
        )

    def give_back(i, f, compute, sends, recvs):
        def send(k):
            s = place.behind(k)
            obuf[rows_at(s, room, unit), lanes(f, share)] = compute(s).astype(BF16)

            @pl.when(k >= 2)
            def _():
                return_copy(sends, recvs, i, f, k - 1).start()

        loop(1, n, send)
        ret[rows_at(me, room, unit), lanes(f, share)] = compute(me).astype(BF16)
        return_copy(sends, recvs, i, f, n - 1).start()

    for i, f in enumerate(order):
        give_back(
            i,
            f,
            lambda s, f=f: dot(act[rows_at(s, room, unit), :], wout_ref[:, f * share : (f + 1) * share]),
            s_r,
            r_r,
        )

    def gather_back(i, f, recvs, sends):
        def wait(k):
            src = place.ahead(k)
            remote(
                obuf.at[rows_at(src, room, unit), lanes(f, share)],
                ret.at[rows_at(src, room, unit), lanes(f, share)],
                sends.at[i, k],
                recvs.at[i, k],
                place.plane(src),
            ).wait_recv()

        loop(1, n, wait)

    def part_copy(sends, recvs, f):
        return remote(pbuf.at[f], rbuf.at[z], sends.at[f], recvs.at[z], {"mp": f})

    def reduce_back(sends_r, recvs_r, sends, recvs):
        for i, f in enumerate(order):
            gather_back(i, f, recvs_r, sends_r)

            def combine(b, f=f):
                at = rows_at(b, TB, TB)
                part = dot(comb[at, :], ret[:, f * share : (f + 1) * share])
                pbuf[f, at, :] = part.astype(BF16)

                @pl.when(z == f)
                def _():
                    own[at, :] = part

            loop(0, blocks, combine)

            @pl.when(z != f)
            def _(f=f):
                part_copy(sends, recvs, f).start()

        for j in range(1, mp):
            src = place.zahead(j)
            remote(pbuf.at[0], rbuf.at[src], sends.at[0], recvs.at[src], {"mp": src}).wait_recv()

    def wait_parts(sends, recvs):
        for f in range(mp):

            @pl.when(z != f)
            def _(f=f):
                part_copy(sends, recvs, f).wait_send()

    def summed(at):
        value = own[at, :]
        for j in range(1, mp):
            value = value + rbuf[place.zahead(j), at, :].astype(F32)
        return value

    def spread_copy(buf, sends, recvs, j):
        return remote(
            buf.at[:, mine], buf.at[:, mine], sends.at[j], recvs.at[z], {"mp": place.zahead(j)}
        )

    def spread_wait(buf, sends, recvs, src):
        remote(
            buf.at[:, mine], buf.at[:, lanes(src, share)], sends.at[0], recvs.at[src], {"mp": src}
        ).wait_recv()

    reduce_back(s_r, r_r, s_p, r_p)

    def finish(b, loss):
        at = rows_at(b, TB, TB)
        final = hid[at, mine] + summed(at)
        out_ref[at, :] = final.astype(BF16)
        residue = final - tea_ref[at, :].astype(F32)
        grad = valc[at, :] * residue
        gf[at, mine] = grad.astype(BF16)
        return loss + 0.5 * jnp.sum(grad * residue)

    loss = lax.fori_loop(0, blocks, finish, jnp.float32(0.0))
    for j in range(1, mp):
        spread_copy(gf, s_g, r_g, j).start()

    def wait_dispatch(k):
        dispatch_copy(k).wait_send()

    loop(1, n, wait_dispatch)

    def clear(e):
        gg[e] = jnp.zeros((room, 1), F32)

    loop(0, n, clear)

    def grad_copy(i, f, k):
        e = place.ahead(k)
        return remote(
            sbuf.at[rows_at(e, room, unit), lanes(f, share)],
            grows.at[rows_at(me, room, unit), lanes(f, share)],
            s_d2.at[i, k],
            r_d2.at[i, k],
            place.plane(e),
        )

    for i in range(mp):
        f = place.zahead(i)
        if i > 0:
            spread_wait(gf, s_g, r_g, f)

        def grad_rows(k, f=f):
            e = place.ahead(k)
            at = rows_at(e, room, unit)
            picked = dot(disp[e], gf[:, lanes(f, share)])
            gg[e] = gg[e] + jnp.sum(
                picked * ret[at, lanes(f, share)].astype(F32), axis=1, keepdims=True
            )
            return at, (gsl[e] * picked).astype(BF16)

        def grad_send(k, i=i, f=f):
            at, out = grad_rows(k)
            sbuf[at, lanes(f, share)] = out

            @pl.when(k >= 2)
            def _():
                grad_copy(i, f, k - 1).start()

        loop(1, n, grad_send)
        at, out = grad_rows(n)
        grows[at, lanes(f, share)] = out
        grad_copy(i, f, n - 1).start()

    def gate_row(e):
        msg[pl.ds(e, 1), :] = jnp.sum(disp[e].astype(F32) * gg[e], axis=0, keepdims=True)

    loop(0, experts, gate_row)
    msg[experts : experts + 8, :] = jnp.full((8, tokens), loss, F32)
    rmsg[z] = msg[...]
    for j in range(1, mp):
        remote(msg, rmsg.at[z], s_m.at[j], r_m.at[z], {"mp": place.zahead(j)}).start()

    def weigh_back(b):
        at = rows_at(b, TB, TB)
        slot = lax.broadcasted_iota(I32, (TB, slots), 1).astype(F32)
        comb[at, :] = jnp.where(
            (sidc[at, 0:1] == slot) | (sidc[at, 1:2] == slot), 1.0, 0.0
        ).astype(BF16)

    loop(0, blocks, weigh_back)

    def expert_back(k):
        s = place.behind(k)

        @pl.when(k > 0)
        def _():
            for i in range(mp):
                f = place.zahead(i)
                remote(
                    grows.at[rows_at(s, room, unit), lanes(f, share)],
                    grows.at[rows_at(s, room, unit), lanes(f, share)],
                    s_d2.at[i, k],
                    r_d2.at[i, k],
                    place.plane(s),
                ).wait_recv()

        at = rows_at(s, room, unit)
        gi[at, :] = (dot_nt(grows[at, :], wout_ref[...]) * dgelu[at, :]).astype(BF16)

    loop(0, n, expert_back)

    def wait_returns(sends, recvs):
        for i, f in enumerate(order):

            def wait(k, i=i, f=f):
                return_copy(sends, recvs, i, f, k).wait_send()

            loop(1, n, wait)

    wait_returns(s_r, r_r)

    for i, f in enumerate(order):
        give_back(
            i,
            f,
            lambda s, f=f: dot_nt(gi[rows_at(s, room, unit), :], win_ref[f * share : (f + 1) * share, :]),
            s_r2,
            r_r2,
        )

    def weight_grads(b):
        at = lanes(b, 128)
        gwin_ref[at, :] = dot_tn(rows[:, at], gi[...])

    loop(0, width // 128, weight_grads)

    def weight_grads_out(b):
        at = lanes(b, 128)
        gwout_ref[at, :] = dot_tn(act[:, at], grows[...])

    loop(0, gwout_ref.shape[0] // 128, weight_grads_out)

    wait_parts(s_p, r_p)
    reduce_back(s_r2, r_r2, s_p2, r_p2)

    ger = mixf

    def finish_back(b):
        at = rows_at(b, TB, TB)
        ger[at, mine] = summed(at).astype(BF16)

    loop(0, blocks, finish_back)
    for j in range(1, mp):
        spread_copy(ger, s_g2, r_g2, j).start()
    for j in range(1, mp):
        src = place.zahead(j)
        remote(msg, rmsg.at[src], s_m.at[0], r_m.at[src], {"mp": src}).wait_recv()
    grad_probs = rmsg[0]
    for j in range(1, mp):
        grad_probs = grad_probs + rmsg[j]
    msg2 = grad_probs[0:experts]
    loss_ref[...] = grad_probs[experts : experts + 8, 0:128] / (tokens * width)
    gates = grow_t[0:experts, :]
    grow_t[0:experts, :] = gates * (msg2 - jnp.sum(msg2 * gates, axis=0, keepdims=True))
    vec_ref[...] = jnp.zeros_like(vec_ref)
    for j in range(1, mp):
        spread_wait(ger, s_g2, r_g2, place.zahead(j))

    def norm_back(b):
        at = rows_at(b, TB, TB)
        normal, inverse = standardize(hid[at, :])
        normed = normal * g2_ref[...] + b2_ref[...]
        logits = grow_t[0:experts, at]
        vec_ref[8 : 8 + experts, :] += dot(logits, normed, HIGHEST)
        grad = dot_tn(logits, rt_ref[...], HIGHEST) + ger[at, :].astype(F32)
        vec_ref[2:3, :] += jnp.sum(grad * normal, axis=0, keepdims=True)
        vec_ref[3:4, :] += jnp.sum(grad, axis=0, keepdims=True)
        scaled = grad * g2_ref[...]
        out = gf[at, :].astype(F32) + inverse * (
            scaled
            - jnp.mean(scaled, axis=-1, keepdims=True)
            - normal * jnp.mean(scaled * normal, axis=-1, keepdims=True)
        )
        hid[at, :] = out
        ga_ref[at, :] = out.astype(BF16)
        gho_ref[at, :] = hid[at, mine]

    loop(0, blocks, norm_back)

    for c in range(blocks):
        for j in range(1, mp):
            remote(
                mix_ref.at[pl.ds(c * TB, TB)],
                mixf.at[pl.ds(c * TB, TB), mine],
                s_a.at[c, j],
                r_a.at[c, z],
                {"mp": place.zahead(j)},
            ).wait_send()
    for j in range(1, mp):
        spread_copy(gf, s_g, r_g, j).wait_send()
        spread_copy(ger, s_g2, r_g2, j).wait_send()
        remote(msg, rmsg.at[z], s_m.at[j], r_m.at[z], {"mp": place.zahead(j)}).wait_send()
    for i in range(mp):
        f = place.zahead(i)

        def wait_grad(k, i=i, f=f):
            grad_copy(i, f, k).wait_send()

        loop(1, n, wait_grad)
    wait_returns(s_r2, r_r2)
    wait_parts(s_p2, r_p2)


def moe(dims, capacity, experts, *args):
    x, mix = args[0], args[1]
    dp, ex, mp = dims
    n = dp * ex
    tokens, width = x.shape
    share = width // mp
    hidden = args[-1].shape[0]
    room = -(-capacity // 16) * 16
    while (room * n) % 128:
        room += 16
    slots = n * room
    msgs = experts + 8
    dma = pltpu.SemaphoreType.DMA
    vm = pltpu.VMEM
    scratch = [
        vm((tokens, width), BF16),
        vm((width, width), BF16),
        vm((tokens, width), F32),
        vm((tokens, width), BF16),
        vm((tokens, 1), F32),
        vm((tokens, 128), F32),
        vm((8, tokens), F32),
        vm((2, tokens, 1), F32),
        vm((experts, tokens), F32),
        vm((tokens, 1), F32),
        vm((n, room, tokens), BF16),
        vm((tokens, slots), BF16),
        vm((n, room, 1), F32),
        vm((n, room, 1), F32),
        vm((slots, width), BF16),
        vm((slots, width), BF16),
        vm((slots, hidden), F32),
        vm((slots, hidden), BF16),
        vm((slots, width), BF16),
        vm((slots, width), BF16),
        vm((mp, tokens, share), BF16),
        vm((mp, tokens, share), BF16),
        vm((tokens, share), F32),
        vm((tokens, width), BF16),
        vm((slots, width), BF16),
        vm((slots, hidden), BF16),
        vm((msgs, tokens), F32),
        vm((mp, msgs, tokens), F32),
        dma((tokens // TB, mp)),
        dma((tokens // TB, mp)),
        dma((n,)),
        dma((n,)),
        dma((mp, n)),
        dma((mp, n)),
        dma((mp,)),
        dma((mp,)),
        dma((mp,)),
        dma((mp,)),
        dma((mp, n)),
        dma((mp, n)),
        dma((mp, n)),
        dma((mp, n)),
        dma((mp,)),
        dma((mp,)),
        dma((mp,)),
        dma((mp,)),
        dma((mp,)),
        dma((mp,)),
    ]
    shapes = (
        jax.ShapeDtypeStruct((tokens, share), BF16),
        jax.ShapeDtypeStruct((8, 128), F32),
        jax.ShapeDtypeStruct((tokens, share), F32),
        jax.ShapeDtypeStruct((tokens, width), BF16),
        jax.ShapeDtypeStruct((8 + experts, width), F32),
        jax.ShapeDtypeStruct((width, hidden), F32),
        jax.ShapeDtypeStruct((hidden, width), F32),
    )
    spec = pl.BlockSpec(memory_space=pltpu.VMEM)
    return pl.pallas_call(
        functools.partial(moe_kernel, dims, capacity, experts),
        out_shape=shapes,
        in_specs=[spec] * len(args),
        out_specs=[spec] * len(shapes),
        scratch_shapes=scratch,
        compiler_params=pltpu.CompilerParams(
            collective_id=0, has_side_effects=True, vmem_limit_bytes=VMEM_LIMIT
        ),
        name="moe",
    )(*args)


def tail_kernel(
    dims,
    part_ref,
    small_ref,
    vz_ref,
    vec_ref,
    wpk_ref,
    gho_ref,
    x_ref,
    g1_ref,
    gin_ref,
    gw_ref,
    sum_ref,
    rpart,
    rsmall,
    rvz,
    vsend,
    rvec,
    rw,
    wred,
    wall,
    s_p,
    r_p,
    s_s,
    r_s,
    s_v,
    r_v,
    s_w,
    r_w,
    s_c,
    r_c,
    s_g,
    r_g,
):
    place = Place(dims)
    n, mp, me, z = place.n, place.mp, place.me, place.z
    tokens, width = x_ref.shape
    share = width // mp
    blocks = tokens // TB
    piece = wpk_ref.shape[0] // n
    mine = lanes(z, share)
    place.barrier()

    def z_copy(which, j):
        dst = place.zahead(j)
        device = {"mp": dst}
        if which == 0:
            return remote(vz_ref, rvz.at[z], s_v.at[j], r_v.at[z], device)
        if which == 1:
            return remote(small_ref, rsmall.at[z], s_s.at[j], r_s.at[z], device)
        return remote(
            part_ref.at[:, lanes(dst, share)], rpart.at[z], s_p.at[j], r_p.at[z], device
        )

    for which in range(3):
        for j in range(1, mp):
            z_copy(which, j).start()
    rvz[z] = vz_ref[...]
    rsmall[z] = small_ref[...]

    def w_copy(k):
        p = place.ahead(k)
        return remote(
            wpk_ref.at[rows_at(p, piece, 16)], rw.at[me], s_w.at[k], r_w.at[k], place.plane(p)
        )

    loop(1, n, lambda k: w_copy(k).start())
    rw[me] = wpk_ref[rows_at(me, piece, 16), :]

    for j in range(1, mp):
        src = place.zahead(j)
        remote(vz_ref, rvz.at[src], s_v.at[0], r_v.at[src], {"mp": src}).wait_recv()
    total = rvz[0]
    for j in range(1, mp):
        total = total + rvz[j]
    vsend[...] = vec_ref[...].astype(BF16)
    vsend[0:2, :] = total[0:2].astype(BF16)

    def v_copy(k):
        return remote(
            vsend, rvec.at[me], s_c.at[k], r_c.at[k], place.plane(place.ahead(k))
        )

    rvec[me] = vsend[...]
    loop(1, n, lambda k: v_copy(k).start())

    def w_wait(k):
        src = place.behind(k)
        remote(
            wpk_ref.at[rows_at(0, piece, 16)], rw.at[src], s_w.at[k], r_w.at[k], place.plane(src)
        ).wait_recv()

    loop(1, n, w_wait)
    acc = rw[0].astype(F32)
    for p in range(1, n):
        acc = acc + rw[p].astype(F32)
    wall[rows_at(me, piece, 16), :] = acc.astype(BF16)

    def g_copy(k):
        at = rows_at(me, piece, 16)
        return remote(wall.at[at], wall.at[at], s_g.at[k], r_g.at[k], place.plane(place.ahead(k)))

    loop(1, n, lambda k: g_copy(k).start())

    def v_wait(k):
        src = place.behind(k)
        remote(vsend, rvec.at[src], s_c.at[k], r_c.at[k], place.plane(src)).wait_recv()

    loop(1, n, v_wait)
    acc = rvec[0].astype(F32)
    for p in range(1, n):
        acc = acc + rvec[p].astype(F32)
    sum_ref[...] = acc

    for j in range(1, mp):
        src = place.zahead(j)
        remote(small_ref, rsmall.at[src], s_s.at[0], r_s.at[src], {"mp": src}).wait_recv()
    means = rsmall[0]
    for j in range(1, mp):
        means = means + rsmall[j]
    means = means / width
    for j in range(1, mp):
        src = place.zahead(j)
        remote(
            part_ref.at[:, mine], rpart.at[src], s_p.at[0], r_p.at[src], {"mp": src}
        ).wait_recv()

    gain = g1_ref[:, mine]
    for b in range(blocks):
        at = pl.ds(b * TB, TB)
        values = x_ref[at, :].astype(F32)
        center = jnp.mean(values, axis=-1, keepdims=True)
        spread = values - center
        inverse = lax.rsqrt(jnp.mean(spread * spread, axis=-1, keepdims=True) + EPSILON)
        normal = (x_ref[at, mine].astype(F32) - center) * inverse
        grad = part_ref[at, mine].astype(F32)
        for j in range(1, mp):
            grad = grad + rpart[place.zahead(j), at, :].astype(F32)
        flat = means[:, b * TB : (b + 1) * TB]
        turned = jnp.transpose(jnp.concatenate([flat, jnp.zeros((120, TB), F32)], axis=0))
        gin_ref[at, :] = gho_ref[at, :] + inverse * (
            grad * gain - turned[:, 0:1] - normal * turned[:, 1:2]
        )

    def g_wait(k):
        src = place.behind(k)
        at = rows_at(src, piece, 16)
        remote(wall.at[at], wall.at[at], s_g.at[k], r_g.at[k], place.plane(src)).wait_recv()

    loop(1, n, g_wait)
    gw_ref[...] = wall[...].astype(F32)

    for which in range(3):
        for j in range(1, mp):
            z_copy(which, j).wait_send()
    loop(1, n, lambda k: w_copy(k).wait_send())
    loop(1, n, lambda k: v_copy(k).wait_send())
    loop(1, n, lambda k: g_copy(k).wait_send())


def tail(dims, part, small, vz, vec, wpk, gho, x, g1):
    dp, ex, mp = dims
    n = dp * ex
    tokens, width = x.shape
    share = width // mp
    dma = pltpu.SemaphoreType.DMA
    vm = pltpu.VMEM
    args = (part, small, vz, vec, wpk, gho, x, g1)
    shapes = (
        jax.ShapeDtypeStruct((tokens, share), F32),
        jax.ShapeDtypeStruct(wpk.shape, F32),
        jax.ShapeDtypeStruct(vec.shape, F32),
    )
    scratch = [
        vm((mp, tokens, share), BF16),
        vm((mp,) + small.shape, F32),
        vm((mp,) + vz.shape, F32),
        vm(vec.shape, BF16),
        vm((n,) + vec.shape, BF16),
        vm((n, wpk.shape[0] // n, wpk.shape[1]), BF16),
        vm((8, 128), BF16),
        vm(wpk.shape, BF16),
    ]
    scratch += [dma((mp,))] * 6 + [dma((n,))] * 6
    spec = pl.BlockSpec(memory_space=pltpu.VMEM)
    return pl.pallas_call(
        functools.partial(tail_kernel, dims),
        out_shape=shapes,
        in_specs=[spec] * len(args),
        out_specs=[spec] * len(shapes),
        scratch_shapes=scratch,
        compiler_params=pltpu.CompilerParams(
            collective_id=1, has_side_effects=True, vmem_limit_bytes=VMEM_LIMIT
        ),
        name="tail",
    )(*args)


def per_device(
    dims,
    inputs,
    teacher,
    top_experts,
    priority,
    valid_mask,
    blocks,
    query_weight,
    key_weight,
    value_weight,
    out_weight,
    router,
    expert_in,
    expert_out,
    first_gain,
    first_bias,
    second_gain,
    second_bias,
):
    length, features = inputs.shape
    mp = dims[2]
    experts = router.shape[1]
    share_width = features // mp
    capacity = length * 2 * 21 // (20 * experts)
    head_count = query_weight.shape[1] // HEAD_DIM
    block_rows = min(512, length)
    block_total = length // block_rows
    block_ids = blocks[0]
    pieces = [out_weight] + [
        lax.ppermute(out_weight, "mp", [(i, (i + j) % mp) for i in range(mp)])
        for j in range(1, mp)
    ]
    out_pieces = jnp.stack(pieces)
    flat_inputs = inputs.astype(F32)
    normal_one, inverse_one = standardize(flat_inputs)
    normed = (normal_one * first_gain + first_bias).astype(BF16)
    query_rows = (dot(normed, query_weight) * 0.125).astype(BF16)
    query_rows = query_rows.reshape(length, head_count, HEAD_DIM)
    key_rows = dot(normed, key_weight).astype(BF16).reshape(length, head_count, HEAD_DIM)
    value_rows = dot(normed, value_weight).astype(BF16).reshape(length, head_count, HEAD_DIM)

    def scores_for(block_index):
        queries = lax.dynamic_slice_in_dim(query_rows, block_index * block_rows, block_rows, 0)
        query_ids = lax.dynamic_slice_in_dim(block_ids, block_index * block_rows, block_rows, 0)
        scores = jnp.einsum("qhd,khd->hqk", queries, key_rows, preferred_element_type=F32)
        allowed = block_ids[None, None, :] <= query_ids[None, :, None]
        return (queries, jnp.where(allowed, scores, -1e30))

    def forward_block(block_index):
        queries, scores = scores_for(block_index)
        peak_score = jnp.max(scores, axis=-1, keepdims=True)
        expanded = jnp.exp(scores - peak_score)
        totals = jnp.sum(expanded, axis=-1, keepdims=True)
        weights = (expanded / totals).astype(BF16)
        blended = jnp.einsum("hqk,khd->qhd", weights, value_rows, preferred_element_type=F32)
        return (blended, (peak_score + jnp.log(totals))[:, :, 0])

    mixed_blocks, log_totals = lax.map(forward_block, jnp.arange(block_total))
    mixture = mixed_blocks.reshape(length, head_count * HEAD_DIM).astype(BF16)

    output, loss, grad_hidden_own, grad_attended, vec, grad_in, grad_out = moe(
        dims,
        capacity,
        experts,
        inputs,
        mixture,
        out_pieces,
        second_gain[None],
        second_bias[None],
        router.T,
        top_experts,
        priority,
        valid_mask[None],
        teacher,
        expert_in[0],
        expert_out[0],
    )

    grad_out_weight = jnp.einsum("tf,td->fd", mixture, grad_attended, preferred_element_type=F32)
    grad_mixture = jnp.einsum(
        "td,fd->tf", grad_attended, out_weight, preferred_element_type=F32
    ).astype(BF16)
    grad_mixture = grad_mixture.reshape(length, head_count, HEAD_DIM)

    def backward_block(carry, block_pair):
        grad_keys, grad_values = carry
        block_index, log_block = block_pair
        queries, scores = scores_for(block_index)
        grad_mix = lax.dynamic_slice_in_dim(grad_mixture, block_index * block_rows, block_rows, 0)
        probability = jnp.exp(scores - log_block[:, :, None])
        probability_low = probability.astype(BF16)
        grad_weights = jnp.einsum("qhd,khd->hqk", grad_mix, value_rows, preferred_element_type=F32)
        centre = jnp.sum(grad_weights * probability, axis=-1, keepdims=True)
        grad_scores = (probability * (grad_weights - centre)).astype(BF16)
        grad_queries = jnp.einsum("hqk,khd->qhd", grad_scores, key_rows, preferred_element_type=F32)
        grad_keys = grad_keys + jnp.einsum(
            "hqk,qhd->khd", grad_scores, queries, preferred_element_type=F32
        )
        grad_values = grad_values + jnp.einsum(
            "hqk,qhd->khd", probability_low, grad_mix, preferred_element_type=F32
        )
        return ((grad_keys, grad_values), grad_queries)

    empty_heads = jnp.zeros((length, head_count, HEAD_DIM), F32)
    (grad_keys, grad_values), grad_query_blocks = lax.scan(
        backward_block, (empty_heads, empty_heads), (jnp.arange(block_total), log_totals)
    )
    grad_queries = grad_query_blocks.reshape(length, head_count * HEAD_DIM).astype(BF16) * 0.125
    grad_keys = grad_keys.reshape(length, head_count * HEAD_DIM).astype(BF16)
    grad_values = grad_values.reshape(length, head_count * HEAD_DIM).astype(BF16)
    grad_query_weight = jnp.einsum("td,tf->df", normed, grad_queries, preferred_element_type=F32)
    grad_key_weight = jnp.einsum("td,tf->df", normed, grad_keys, preferred_element_type=F32)
    grad_value_weight = jnp.einsum("td,tf->df", normed, grad_values, preferred_element_type=F32)
    grad_one = jnp.einsum("tf,df->td", grad_queries, query_weight, preferred_element_type=F32)
    grad_one = grad_one + jnp.einsum(
        "tf,df->td", grad_keys, key_weight, preferred_element_type=F32
    )
    grad_one = grad_one + jnp.einsum(
        "tf,df->td", grad_values, value_weight, preferred_element_type=F32
    )
    scaled_one = grad_one * first_gain
    small = jnp.zeros((8, length), F32)
    small = small.at[0].set(jnp.sum(scaled_one, axis=-1))
    small = small.at[1].set(jnp.sum(scaled_one * normal_one, axis=-1))
    vz = jnp.zeros((8, features), F32)
    vz = vz.at[0].set(jnp.sum(grad_one * normal_one, axis=0))
    vz = vz.at[1].set(jnp.sum(grad_one, axis=0))
    weights_packed = jnp.concatenate(
        [grad_query_weight, grad_key_weight, grad_value_weight]
        + [
            grad_out_weight[:, i * share_width : (i + 1) * share_width]
            for i in range(features // share_width)
        ]
    ).astype(BF16)
    grad_input, grad_weights, sums = tail(
        dims,
        grad_one.astype(BF16),
        small,
        vz,
        vec,
        weights_packed,
        grad_hidden_own,
        inputs,
        first_gain[None],
    )
    grad_wo = jnp.concatenate(
        [
            grad_weights[3 * features + i * share_width : 3 * features + (i + 1) * share_width]
            for i in range(features // share_width)
        ],
        axis=1,
    )
    return (
        output,
        loss[0, 0:1],
        grad_input,
        grad_weights[0:features],
        grad_weights[features : 2 * features],
        grad_weights[2 * features : 3 * features],
        grad_wo,
        sums[8 : 8 + experts].T,
        grad_in[None],
        grad_out[None],
        sums[0],
        sums[1],
        sums[2],
        sums[3],
    )


def solution(mesh):
    dims = (mesh.shape["dp"], mesh.shape["expert"], mesh.shape["mp"])
    both = ("dp", "expert")
    in_specs = (
        P(both, None),
        P(both, "mp"),
        P(both, None),
        P(both, None),
        P(both),
        P(both, None),
        P(None, "mp"),
        P(None, "mp"),
        P(None, "mp"),
        P("mp", None),
        P(),
        P(both, None, "mp"),
        P(both, "mp", None),
        P(),
        P(),
        P(),
        P(),
    )
    out_specs = (
        P(both, "mp"),
        P(both),
        P(both, "mp"),
        P(None, "mp"),
        P(None, "mp"),
        P(None, "mp"),
        P("mp", None),
        P(),
        P(both, None, "mp"),
        P(both, "mp", None),
        P(),
        P(),
        P(),
        P(),
    )
    return jax.shard_map(
        functools.partial(per_device, dims),
        mesh=mesh,
        in_specs=in_specs,
        out_specs=out_specs,
        check_vma=False,
    )
```

```python
import functools

import jax
import jax.numpy as jnp
from jax import lax
from jax.experimental import pallas as pl
from jax.experimental.pallas import tpu as pltpu
from jax.sharding import PartitionSpec as P

HEAD_DIM = 64
EPSILON = 1e-06
HIGHEST = lax.Precision.HIGHEST
MESH = pl.DeviceIdType.MESH
F32 = jnp.float32
BF16 = jnp.bfloat16
I32 = jnp.int32
VMEM_LIMIT = 67043328


def standardize(values):
    center = values - jnp.mean(values, axis=-1, keepdims=True)
    inverse = lax.rsqrt(jnp.mean(center * center, axis=-1, keepdims=True) + EPSILON)
    return (center * inverse, inverse)


def dot(a, b, precision=None):
    return jnp.dot(a, b, preferred_element_type=F32, precision=precision)


def dot_nt(a, b, precision=None):
    return lax.dot_general(
        a, b, (((1,), (1,)), ((), ())), preferred_element_type=F32, precision=precision
    )


def dot_tn(a, b, precision=None):
    return lax.dot_general(
        a, b, (((0,), (0,)), ((), ())), preferred_element_type=F32, precision=precision
    )


def remote(src, dst, send, recv, device):
    return pltpu.make_async_remote_copy(
        src_ref=src, dst_ref=dst, send_sem=send, recv_sem=recv, device_id=device, device_id_type=MESH
    )


def lanes(f, width):
    return pl.ds(pl.multiple_of(f * width, width), width)


def rows_at(s, count, unit):
    return pl.ds(pl.multiple_of(s * count, unit), count)


def loop(low, high, body):
    def step(i, carry):
        body(i)
        return carry

    lax.fori_loop(low, high, step, 0)


def peer_order(n):
    masks = sorted(range(1, n), key=lambda m: (-bin(m // 2).count("1"), m))
    return [0] + masks


class Place:
    def __init__(self, dims):
        self.dp, self.ex, self.mp = dims
        self.n = self.dp * self.ex
        self.me = lax.axis_index("dp") * self.ex + lax.axis_index("expert")
        self.z = lax.axis_index("mp")
        self.order = peer_order(self.n)

    def peer(self, k):
        mask = 0
        for i in range(1, self.n):
            mask = mask + jnp.where(k == i, self.order[i], 0)
        out = 0
        bit = 1
        while bit < self.n:
            out = out + bit * lax.rem(lax.div(self.me, bit) + lax.div(mask, bit), 2)
            bit *= 2
        return out

    def plane(self, p):
        return {"dp": lax.div(p, self.ex), "expert": lax.rem(p, self.ex)}

    def zahead(self, j):
        return lax.rem(self.z + j, self.mp)

    def greet(self):
        sem = pltpu.get_barrier_semaphore()

        def hello(k):
            pl.semaphore_signal(
                sem, inc=1, device_id=self.plane(self.peer(k)), device_id_type=MESH
            )

        loop(1, self.n, hello)
        for j in range(1, self.mp):
            pl.semaphore_signal(
                sem, inc=1, device_id={"mp": self.zahead(j)}, device_id_type=MESH
            )

    def meet(self):
        pl.semaphore_wait(pltpu.get_barrier_semaphore(), self.n - 1 + self.mp - 1)


def feature_order(mp):
    return [i // 2 if i % 2 == 0 else mp - 1 - i // 2 for i in range(mp)]


TB = 256


def layer_kernel(
    dims,
    capacity,
    experts,
    x_ref,
    blk_ref,
    wq_ref,
    wk_ref,
    wv_ref,
    wo_ref,
    g1_ref,
    b1_ref,
    g2_ref,
    b2_ref,
    rt_ref,
    top_ref,
    pri_ref,
    val_ref,
    tea_ref,
    win_ref,
    wout_ref,
    out_ref,
    loss_ref,
    gin_ref,
    gwq_ref,
    gwk_ref,
    gwv_ref,
    gwo_ref,
    vec_ref,
    gwin_ref,
    gwout_ref,
    a1,
    wcat,
    keys,
    values,
    turned,
    mixt,
    lse,
    kidc,
    gk,
    gv,
    gt,
    gflat,
    wpk,
    rw,
    wall,
    small,
    rsmall,
    vz,
    rvz,
    vsend,
    rvec,
    mixf,
    wof,
    hid,
    n2b,
    posc,
    topc,
    sidc,
    sidr,
    gcol,
    grow_t,
    valc,
    disp,
    comb,
    gsl,
    gg,
    sbuf,
    rows,
    dgelu,
    act,
    ret,
    pbuf,
    rbuf,
    own,
    gf,
    grows,
    gi,
    msg,
    rmsg,
    s_a,
    r_a,
    s_d,
    r_d,
    s_r,
    r_r,
    s_p,
    r_p,
    s_g,
    r_g,
    s_d2,
    r_d2,
    s_r2,
    r_r2,
    s_p2,
    r_p2,
    s_g2,
    r_g2,
    s_m,
    r_m,
    s_o,
    r_o,
    s_o2,
    r_o2,
    s_z,
    r_z,
    s_s,
    r_s,
    s_v,
    r_v,
    s_w,
    r_w,
    s_c,
    r_c,
    s_e,
    r_e,
):
    place = Place(dims)
    n, mp, me, z = place.n, place.mp, place.me, place.z
    tokens, width = x_ref.shape
    share = width // mp
    heads = share // HEAD_DIM
    blocks = tokens // TB
    slots = ret.shape[0]
    room = slots // n
    unit = 16
    order = feature_order(mp)
    mine = lanes(z, share)

    place.greet()

    wcat[:, 0:share] = wq_ref[...]
    wcat[:, share : 2 * share] = wk_ref[...]
    wcat[:, 2 * share : 3 * share] = wv_ref[...]

    def project(b):
        at = rows_at(b, TB, TB)
        normal, _ = standardize(x_ref[at, :].astype(F32))
        normed = (normal * g1_ref[...] + b1_ref[...]).astype(BF16)
        a1[at, :] = normed
        out = dot(normed, wcat[...])
        lane = lax.broadcasted_iota(I32, (TB, 3 * share), 1)
        out = out * jnp.where(lane < share, 0.125, 1.0)
        keys[at, :] = out[:, share : 2 * share].astype(BF16)
        values[at, :] = out[:, 2 * share : 3 * share].astype(BF16)
        turned[:, at] = jnp.transpose(out).astype(BF16)
        kidc[at, :] = jnp.transpose(jnp.broadcast_to(blk_ref[:, at].astype(F32), (128, TB)))[:, 0:1]

    loop(0, blocks, project)
    place.meet()

    piece = max(16, share // n)
    pieces = share // piece

    def own_piece(ref, s):
        return ref.at[rows_at(s * pieces + me, piece, 16), :]

    def out_weight_z(j):
        return remote(
            wo_ref.at[rows_at(me, piece, 16), :],
            own_piece(wof, z),
            s_o.at[j],
            r_o.at[z],
            {"mp": place.zahead(j)},
        )

    def out_weight_plane(s, k):
        return remote(
            own_piece(wof, s), own_piece(wof, s), s_o2.at[s, k], r_o2.at[s, k], place.plane(place.peer(k))
        )

    @pl.when(me < pieces)
    def _():
        for j in range(1, mp):
            out_weight_z(j).start()

    wof[rows_at(z, share, share), :] = wo_ref[...]

    def mixture_copy(b, j):
        at = rows_at(b, TB, TB)
        return remote(
            mixf.at[at, mine], mixf.at[at, mine], s_a.at[b, j], r_a.at[b, z], {"mp": place.zahead(j)}
        )

    head_row = lax.div(lax.broadcasted_iota(I32, (share, TB), 0), HEAD_DIM)
    head_lane = lax.div(lax.broadcasted_iota(I32, (TB, share), 1), HEAD_DIM)

    def only(value, where, h):
        return jnp.where(where == h, value, jnp.zeros_like(value))

    def masked_scores(at, h):
        scores = dot(keys[...], only(turned[0:share, at], head_row, h))
        return jnp.where(kidc[...] <= blk_ref[:, at].astype(F32), scores, -1e30)

    def attend(b):
        at = rows_at(b, TB, TB)
        mixed = []
        for h in range(heads):
            scores = masked_scores(at, h)
            peak = jnp.max(scores, axis=0, keepdims=True)
            raised = jnp.exp(scores - peak)
            total = jnp.sum(raised, axis=0, keepdims=True)
            lse[h : h + 1, at] = peak + jnp.log(total)
            probs = (raised * (1.0 / total)).astype(BF16)
            low = 2 * share + h * HEAD_DIM
            mixed.append(dot(turned[low : low + HEAD_DIM, :], probs))
        flat = jnp.concatenate(mixed, axis=0)
        mixt[:, at] = flat.astype(BF16)
        mixf[at, mine] = jnp.transpose(flat).astype(BF16)

        @pl.when(b >= 1)
        def _():
            for j in range(1, mp):
                mixture_copy(b - 1, j).start()

    loop(0, blocks, attend)
    for j in range(1, mp):
        mixture_copy(blocks - 1, j).start()

    @pl.when(me < pieces)
    def _():
        for j in range(1, mp):
            src = place.zahead(j)
            remote(
                wo_ref.at[rows_at(me, piece, 16), :], own_piece(wof, src), s_o.at[0], r_o.at[src], {"mp": src}
            ).wait_recv()
        for j in range(1, mp):
            src = place.zahead(j)
            loop(1, n, lambda k, src=src: out_weight_plane(src, k).start())

    def out_weight_wait():
        for j in range(1, mp):
            src = place.zahead(j)

            def wait(k, src=src):
                p = place.peer(k)

                @pl.when(p < pieces)
                def _():
                    at = rows_at(src * pieces + p, piece, 16)
                    remote(
                        wof.at[at, :], wof.at[at, :], s_o2.at[src, k], r_o2.at[src, k], place.plane(p)
                    ).wait_recv()

            loop(1, n, wait)

    lane_t = lax.broadcasted_iota(I32, (TB, tokens), 1)
    sub_t = lax.broadcasted_iota(I32, (TB, tokens), 0)
    lane_k = lax.broadcasted_iota(I32, (TB, 128), 1)

    def positions(b):
        at = rows_at(b, TB, TB)
        hit = (sub_t + b * TB) == pri_ref[...]
        pos = jnp.sum(jnp.where(hit, lane_t.astype(F32), 0.0), axis=1, keepdims=True)
        posc[at, :] = pos
        flat = jnp.transpose(jnp.broadcast_to(pos, (TB, 128)))
        sidr[2:3, at] = flat[0:1]
        vt = jnp.transpose(jnp.broadcast_to(val_ref[:, at].astype(F32), (128, TB)))
        valc[at, :] = vt[:, 0:1]
        named = jnp.concatenate(
            [top_ref[:, at].astype(F32), jnp.zeros((126, TB), F32)], axis=0
        )
        topc[at, :] = jnp.transpose(named)

    loop(0, blocks, positions)

    lane_all = lax.broadcasted_iota(I32, (tokens, 128), 1)
    first = topc[:, 0:1].astype(I32)
    second = topc[:, 1:2].astype(I32)
    named = jnp.where(
        ((lane_all < experts) & (first == lane_all))
        | ((lane_all >= experts) & (second == lane_all - experts)),
        1.0,
        0.0,
    ).astype(BF16)
    total = jnp.sum(
        jnp.where(first == lane_all - experts, 1.0, 0.0), axis=0, keepdims=True
    )
    pos_row = sidr[2:3, :]

    def ranks(b):
        at = rows_at(b, TB, TB)
        earlier = jnp.where(pos_row < posc[at, :], 1.0, 0.0).astype(BF16)
        count = dot(earlier, named)
        e0 = topc[at, 0:1].astype(I32)
        e1 = topc[at, 1:2].astype(I32)
        r0 = jnp.sum(jnp.where(lane_k == e0, count, 0.0), axis=1, keepdims=True)
        r1 = jnp.sum(jnp.where(lane_k == e1 + experts, count + total, 0.0), axis=1, keepdims=True)
        id0 = jnp.where(r0 < capacity, e0.astype(F32) * room + r0, -1.0)
        id1 = jnp.where(r1 < capacity, e1.astype(F32) * room + r1, -1.0)
        both = jnp.where(lane_k == 0, id0, jnp.where(lane_k == 1, id1, 0.0))
        sidc[at, :] = both
        flat = jnp.transpose(both)
        sidr[0:2, at] = flat[0:2]

    loop(0, blocks, ranks)

    out_weight_wait()
    sub_e = lax.broadcasted_iota(I32, (experts, TB), 0)

    def second_norm(b):
        at = rows_at(b, TB, TB)
        for j in range(1, mp):
            src = place.zahead(j)
            remote(
                mixf.at[at, mine], mixf.at[at, lanes(src, share)], s_a.at[0, 0], r_a.at[b, src], {"mp": src}
            ).wait_recv()
        hidden = x_ref[at, :].astype(F32) + dot(mixf[at, :], wof[...])
        hid[at, :] = hidden
        normal, _ = standardize(hidden)
        normed = normal * g2_ref[...] + b2_ref[...]
        n2b[at, :] = normed.astype(BF16)
        logits = dot_nt(rt_ref[...], normed, HIGHEST)
        logits = jnp.exp(logits - jnp.max(logits, axis=0, keepdims=True))
        gates = logits / jnp.sum(logits, axis=0, keepdims=True)
        grow_t[0:experts, at] = gates
        for j in range(2):
            chosen = top_ref[j : j + 1, at]
            gate = jnp.sum(jnp.where(sub_e == chosen, gates, 0.0), axis=0, keepdims=True)
            gate = jnp.where(sidr[j : j + 1, at] >= 0.0, gate, 0.0)
            sidr[5 + j : 6 + j, at] = gate
            gcol[j, at, :] = jnp.transpose(jnp.broadcast_to(gate, (128, TB)))[:, 0:1]

    loop(0, blocks, second_norm)

    sub_c = lax.broadcasted_iota(I32, (room, tokens), 0).astype(F32)

    def fill(k):
        e = place.peer(k)
        base = (e * room).astype(F32)
        hit0 = sidr[0:1, :] == sub_c + base
        hit1 = sidr[1:2, :] == sub_c + base
        pick = jnp.where(hit0 | hit1, 1.0, 0.0).astype(BF16)
        disp[e] = pick
        gsl[e] = jnp.sum(
            jnp.where(hit0, sidr[5:6, :], jnp.where(hit1, sidr[6:7, :], 0.0)), axis=1, keepdims=True
        )
        return e, dot(pick, n2b[...]).astype(BF16)

    def dispatch_copy(k):
        e = place.peer(k)
        return remote(
            sbuf.at[rows_at(e, room, unit)],
            rows.at[rows_at(me, room, unit)],
            s_d.at[k],
            r_d.at[k],
            place.plane(e),
        )

    def dispatch(k):
        e, out = fill(k)
        sbuf[rows_at(e, room, unit), :] = out

        @pl.when(k >= 2)
        def _():
            dispatch_copy(k - 1).start()

    loop(1, n, dispatch)
    e, out = fill(n)
    rows[rows_at(e, room, unit), :] = out
    dispatch_copy(n - 1).start()

    def weigh(b):
        at = rows_at(b, TB, TB)
        slot = lax.broadcasted_iota(I32, (TB, slots), 1).astype(F32)
        comb[at, :] = jnp.where(
            sidc[at, 0:1] == slot,
            gcol[0, at, :],
            jnp.where(sidc[at, 1:2] == slot, gcol[1, at, :], 0.0),
        ).astype(BF16)

    loop(0, blocks, weigh)

    def arrived(buf, recv, send, src):
        remote(
            buf.at[rows_at(src, room, unit)],
            buf.at[rows_at(src, room, unit)],
            send,
            recv,
            place.plane(src),
        ).wait_recv()

    root = 0.7978845608028654
    cube = 0.044715

    def expert_in(k):
        s = place.peer(k)

        @pl.when(k > 0)
        def _():
            arrived(rows, r_d.at[k], s_d.at[k], s)

        at = rows_at(s, room, unit)
        inner = dot(rows[at, :], win_ref[...])
        square = inner * inner
        wave = jnp.tanh(root * inner * (1.0 + cube * square))
        half = 0.5 * (1.0 + wave)
        act[at, :] = (inner * half).astype(BF16)
        dgelu[at, :] = half + 0.5 * inner * (1.0 - wave * wave) * (
            root * (1.0 + 3.0 * cube * square)
        )

    loop(0, n, expert_in)

    def return_copy(sends, recvs, i, f, k):
        s = place.peer(k)
        return remote(
            sbuf.at[rows_at(s, room, unit), lanes(f, share)],
            ret.at[rows_at(me, room, unit), lanes(f, share)],
            sends.at[i, k],
            recvs.at[i, k],
            place.plane(s),
        )

    def give_back(i, f, compute, sends, recvs):
        def send(k):
            s = place.peer(k)
            sbuf[rows_at(s, room, unit), lanes(f, share)] = compute(s).astype(BF16)

            @pl.when(k >= 2)
            def _():
                return_copy(sends, recvs, i, f, k - 1).start()

        loop(1, n, send)
        ret[rows_at(me, room, unit), lanes(f, share)] = compute(me).astype(BF16)
        return_copy(sends, recvs, i, f, n - 1).start()

    loop(1, n, lambda k: dispatch_copy(k).wait_send())

    def wait_returns(sends, recvs):
        for i, f in enumerate(order):

            def wait(k, i=i, f=f):
                return_copy(sends, recvs, i, f, k).wait_send()

            loop(1, n, wait)

    for i, f in enumerate(order):
        give_back(
            i,
            f,
            lambda s, f=f: dot(act[rows_at(s, room, unit), :], wout_ref[:, f * share : (f + 1) * share]),
            s_r,
            r_r,
        )

    def gather_back(i, f, recvs, sends):
        def wait(k):
            src = place.peer(k)
            remote(
                sbuf.at[rows_at(src, room, unit), lanes(f, share)],
                ret.at[rows_at(src, room, unit), lanes(f, share)],
                sends.at[i, k],
                recvs.at[i, k],
                place.plane(src),
            ).wait_recv()

        loop(1, n, wait)

    def part_copy(sends, recvs, f):
        return remote(pbuf.at[f], rbuf.at[z], sends.at[f], recvs.at[z], {"mp": f})

    def reduce_back(sends_r, recvs_r, sends, recvs):
        for i, f in enumerate(order):
            gather_back(i, f, recvs_r, sends_r)

            def combine(b, f=f):
                at = rows_at(b, TB, TB)
                part = dot(comb[at, :], ret[:, f * share : (f + 1) * share])
                pbuf[f, at, :] = part.astype(BF16)

                @pl.when(z == f)
                def _():
                    own[at, :] = part

            loop(0, blocks, combine)

            @pl.when(z != f)
            def _(f=f):
                part_copy(sends, recvs, f).start()

        for j in range(1, mp):
            src = place.zahead(j)
            remote(pbuf.at[0], rbuf.at[src], sends.at[0], recvs.at[src], {"mp": src}).wait_recv()

    def wait_parts(sends, recvs):
        for f in range(mp):

            @pl.when(z != f)
            def _(f=f):
                part_copy(sends, recvs, f).wait_send()

    def summed(at):
        value = own[at, :]
        for j in range(1, mp):
            value = value + rbuf[place.zahead(j), at, :].astype(F32)
        return value

    def spread_copy(buf, sends, recvs, j):
        return remote(
            buf.at[:, mine], buf.at[:, mine], sends.at[j], recvs.at[z], {"mp": place.zahead(j)}
        )

    def spread_wait(buf, sends, recvs, src):
        remote(
            buf.at[:, mine], buf.at[:, lanes(src, share)], sends.at[0], recvs.at[src], {"mp": src}
        ).wait_recv()

    reduce_back(s_r, r_r, s_p, r_p)

    def finish(b, loss):
        at = rows_at(b, TB, TB)
        final = hid[at, mine] + summed(at)
        out_ref[at, :] = final.astype(BF16)
        residue = final - tea_ref[at, :].astype(F32)
        grad = valc[at, :] * residue
        gf[at, mine] = grad.astype(BF16)
        return loss + 0.5 * jnp.sum(grad * residue)

    loss = lax.fori_loop(0, blocks, finish, jnp.float32(0.0))
    for j in range(1, mp):
        spread_copy(gf, s_g, r_g, j).start()

    wait_returns(s_r, r_r)

    def clear(e):
        gg[e] = jnp.zeros((room, 1), F32)

    loop(0, n, clear)

    def grad_copy(i, f, k):
        e = place.peer(k)
        return remote(
            sbuf.at[rows_at(e, room, unit), lanes(f, share)],
            grows.at[rows_at(me, room, unit), lanes(f, share)],
            s_d2.at[i, k],
            r_d2.at[i, k],
            place.plane(e),
        )

    for i in range(mp):
        f = place.zahead(i)
        if i > 0:
            spread_wait(gf, s_g, r_g, f)

        def grad_rows(k, f=f):
            e = place.peer(k)
            at = rows_at(e, room, unit)
            picked = dot(disp[e], gf[:, lanes(f, share)])
            gg[e] = gg[e] + jnp.sum(
                picked * ret[at, lanes(f, share)].astype(F32), axis=1, keepdims=True
            )
            return at, (gsl[e] * picked).astype(BF16)

        def grad_send(k, i=i, f=f):
            at, out = grad_rows(k)
            sbuf[at, lanes(f, share)] = out

            @pl.when(k >= 2)
            def _():
                grad_copy(i, f, k - 1).start()

        loop(1, n, grad_send)
        at, out = grad_rows(n)
        grows[at, lanes(f, share)] = out
        grad_copy(i, f, n - 1).start()

    def gate_row(e):
        msg[pl.ds(e, 1), :] = jnp.sum(disp[e].astype(F32) * gg[e], axis=0, keepdims=True)

    loop(0, experts, gate_row)
    msg[experts : experts + 8, :] = jnp.full((8, tokens), loss, F32)
    rmsg[z] = msg[...]
    for j in range(1, mp):
        remote(msg, rmsg.at[z], s_m.at[j], r_m.at[z], {"mp": place.zahead(j)}).start()

    def weigh_back(b):
        at = rows_at(b, TB, TB)
        slot = lax.broadcasted_iota(I32, (TB, slots), 1).astype(F32)
        comb[at, :] = jnp.where(
            (sidc[at, 0:1] == slot) | (sidc[at, 1:2] == slot), 1.0, 0.0
        ).astype(BF16)

    loop(0, blocks, weigh_back)

    def expert_back(k):
        s = place.peer(k)

        @pl.when(k > 0)
        def _():
            for i in range(mp):
                f = place.zahead(i)
                remote(
                    grows.at[rows_at(s, room, unit), lanes(f, share)],
                    grows.at[rows_at(s, room, unit), lanes(f, share)],
                    s_d2.at[i, k],
                    r_d2.at[i, k],
                    place.plane(s),
                ).wait_recv()

        at = rows_at(s, room, unit)
        gi[at, :] = (dot_nt(grows[at, :], wout_ref[...]) * dgelu[at, :]).astype(BF16)

    loop(0, n, expert_back)

    def wait_grads():
        for i in range(mp):
            f = place.zahead(i)

            def wait(k, i=i, f=f):
                grad_copy(i, f, k).wait_send()

            loop(1, n, wait)

    wait_grads()

    for i, f in enumerate(order):
        give_back(
            i,
            f,
            lambda s, f=f: dot_nt(gi[rows_at(s, room, unit), :], win_ref[f * share : (f + 1) * share, :]),
            s_r2,
            r_r2,
        )

    def weight_grads(b):
        at = lanes(b, 128)
        gwin_ref[at, :] = dot_tn(rows[:, at], gi[...])

    loop(0, width // 128, weight_grads)

    def weight_grads_out(b):
        at = lanes(b, 128)
        gwout_ref[at, :] = dot_tn(act[:, at], grows[...])

    loop(0, gwout_ref.shape[0] // 128, weight_grads_out)

    wait_parts(s_p, r_p)
    reduce_back(s_r2, r_r2, s_p2, r_p2)

    ger = mixf

    def ger_copy(b, j):
        at = rows_at(b, TB, TB)
        return remote(
            ger.at[at, mine], ger.at[at, mine], s_g2.at[b, j], r_g2.at[b, z], {"mp": place.zahead(j)}
        )

    def finish_back(b):
        at = rows_at(b, TB, TB)
        ger[at, mine] = summed(at).astype(BF16)

        @pl.when(b >= 1)
        def _():
            for j in range(1, mp):
                ger_copy(b - 1, j).start()

    for c in range(blocks):
        for j in range(1, mp):
            mixture_copy(c, j).wait_send()
    loop(0, blocks, finish_back)
    for j in range(1, mp):
        ger_copy(blocks - 1, j).start()

    for j in range(1, mp):
        src = place.zahead(j)
        remote(msg, rmsg.at[src], s_m.at[0], r_m.at[src], {"mp": src}).wait_recv()
    grad_probs = rmsg[0]
    for j in range(1, mp):
        grad_probs = grad_probs + rmsg[j]
    loss_ref[...] = grad_probs[experts : experts + 8, 0:128] / (tokens * width)
    grad_probs = grad_probs[0:experts]
    gates = grow_t[0:experts, :]
    grow_t[0:experts, :] = gates * (
        grad_probs - jnp.sum(grad_probs * gates, axis=0, keepdims=True)
    )
    vec_ref[...] = jnp.zeros_like(vec_ref)
    gk[...] = jnp.zeros_like(gk)
    gv[...] = jnp.zeros_like(gv)
    gwo_ref[...] = jnp.zeros_like(gwo_ref)

    def back(b):
        at = rows_at(b, TB, TB)
        for j in range(1, mp):
            src = place.zahead(j)
            remote(
                ger.at[at, mine], ger.at[at, lanes(src, share)], s_g2.at[0, 0], r_g2.at[b, src], {"mp": src}
            ).wait_recv()
        normal, inverse = standardize(hid[at, :])
        normed = normal * g2_ref[...] + b2_ref[...]
        logits = grow_t[0:experts, at]
        vec_ref[8 : 8 + experts, :] += dot(logits, normed, HIGHEST)
        grad = dot_tn(logits, rt_ref[...], HIGHEST) + ger[at, :].astype(F32)
        vec_ref[2:3, :] += jnp.sum(grad * normal, axis=0, keepdims=True)
        vec_ref[3:4, :] += jnp.sum(grad, axis=0, keepdims=True)
        scaled = grad * g2_ref[...]
        out = gf[at, :].astype(F32) + inverse * (
            scaled
            - jnp.mean(scaled, axis=-1, keepdims=True)
            - normal * jnp.mean(scaled * normal, axis=-1, keepdims=True)
        )
        hid[at, :] = out
        attended = out.astype(BF16)
        gwo_ref[...] += dot(mixt[:, at], attended)
        mix_t = dot_nt(wo_ref[...], attended)
        mix_low = jnp.transpose(mix_t).astype(BF16)
        mix_t = mix_t.astype(BF16)
        query = jnp.transpose(turned[0:share, at].astype(F32)).astype(BF16)
        grad_query = []
        for h in range(heads):
            probs = jnp.exp(masked_scores(at, h) - lse[h : h + 1, at])
            grad_probs = dot(values[...], only(mix_t, head_row, h))
            centre = jnp.sum(grad_probs * probs, axis=0, keepdims=True)
            grad_scores = (probs * (grad_probs - centre)).astype(BF16)
            low = share + h * HEAD_DIM
            grad_query.append(dot(turned[low : low + HEAD_DIM, :], grad_scores))
            gk[...] += dot(grad_scores, only(query, head_lane, h))
            gv[...] += dot(probs.astype(BF16), only(mix_low, head_lane, h))
        flat = jnp.concatenate(grad_query, axis=0)
        gt[0:share, at] = flat.astype(BF16) * 0.125
        gflat[at, 0:share] = jnp.transpose(flat).astype(BF16) * 0.125

    loop(0, blocks, back)

    part = n2b

    def part_z(b, j):
        at = rows_at(b, TB, TB)
        dst = place.zahead(j)
        return remote(
            part.at[at, lanes(dst, share)], rbuf.at[z, at, :], s_z.at[b, j], r_z.at[b, z], {"mp": dst}
        )

    vz[...] = jnp.zeros_like(vz)

    def first_back(b):
        at = rows_at(b, TB, TB)
        gflat[at, share : 2 * share] = gk[at, :].astype(BF16)
        gflat[at, 2 * share : 3 * share] = gv[at, :].astype(BF16)
        grad = dot_nt(gflat[at, :], wcat[...])
        part[at, :] = grad.astype(BF16)
        normal, _ = standardize(x_ref[at, :].astype(F32))
        scaled = grad * g1_ref[...]
        crossed = grad * normal
        lane = lax.broadcasted_iota(I32, (TB, 128), 1)
        sums = jnp.where(
            lane == 0,
            jnp.sum(scaled, axis=1, keepdims=True),
            jnp.where(lane == 1, jnp.sum(scaled * normal, axis=1, keepdims=True), 0.0),
        )
        small[:, at] = jnp.transpose(sums)[0:8]
        vz[0:1, :] += jnp.sum(crossed, axis=0, keepdims=True)
        vz[1:2, :] += jnp.sum(grad, axis=0, keepdims=True)

        @pl.when(b >= 1)
        def _():
            for j in range(1, mp):
                part_z(b - 1, j).start()

    loop(0, blocks, first_back)

    def vz_copy(j):
        return remote(vz, rvz.at[z], s_v.at[j], r_v.at[z], {"mp": place.zahead(j)})

    def small_copy(j):
        return remote(small, rsmall.at[z], s_s.at[j], r_s.at[z], {"mp": place.zahead(j)})

    for j in range(1, mp):
        vz_copy(j).start()
        part_z(blocks - 1, j).start()
        small_copy(j).start()
    rvz[z] = vz[...]
    rsmall[z] = small[...]

    def turn(b):
        at = rows_at(b, TB, TB)
        gt[share : 2 * share, at] = jnp.transpose(gk[at, :]).astype(BF16)
        gt[2 * share : 3 * share, at] = jnp.transpose(gv[at, :]).astype(BF16)

    loop(0, blocks, turn)
    wpk[0 : 3 * share, :] = dot(gt[...], a1[...]).astype(BF16)
    wpk[3 * share : 4 * share, :] = gwo_ref[...].astype(BF16)
    wrows = 4 * share // n

    def w_copy(k):
        p = place.peer(k)
        return remote(
            wpk.at[rows_at(p, wrows, 16)], rw.at[me], s_w.at[k], r_w.at[k], place.plane(p)
        )

    loop(1, n, lambda k: w_copy(k).start())
    rw[me] = wpk[rows_at(me, wrows, 16), :]

    for j in range(1, mp):
        src = place.zahead(j)
        remote(vz, rvz.at[src], s_v.at[0], r_v.at[src], {"mp": src}).wait_recv()
    total_vz = rvz[0]
    for j in range(1, mp):
        total_vz = total_vz + rvz[j]
    vsend[...] = vec_ref[...].astype(BF16)
    vsend[0:2, :] = total_vz[0:2].astype(BF16)

    def v_copy(k):
        return remote(vsend, rvec.at[me], s_c.at[k], r_c.at[k], place.plane(place.peer(k)))

    rvec[me] = vsend[...]
    loop(1, n, lambda k: v_copy(k).start())

    def w_wait(k):
        src = place.peer(k)
        remote(
            wpk.at[rows_at(0, wrows, 16)], rw.at[src], s_w.at[k], r_w.at[k], place.plane(src)
        ).wait_recv()

    loop(1, n, w_wait)
    acc = rw[0].astype(F32)
    for p in range(1, n):
        acc = acc + rw[p].astype(F32)
    wall[rows_at(me, wrows, 16), :] = acc.astype(BF16)

    def e_copy(k):
        at = rows_at(me, wrows, 16)
        return remote(wall.at[at], wall.at[at], s_e.at[k], r_e.at[k], place.plane(place.peer(k)))

    loop(1, n, lambda k: e_copy(k).start())

    def v_wait(k):
        src = place.peer(k)
        remote(vsend, rvec.at[src], s_c.at[k], r_c.at[k], place.plane(src)).wait_recv()

    loop(1, n, v_wait)
    acc = rvec[0].astype(F32)
    for p in range(1, n):
        acc = acc + rvec[p].astype(F32)
    vec_ref[...] = acc

    def e_wait(k):
        src = place.peer(k)
        at = rows_at(src, wrows, 16)
        remote(wall.at[at], wall.at[at], s_e.at[k], r_e.at[k], place.plane(src)).wait_recv()

    loop(1, n, e_wait)
    for i, ref in enumerate((gwq_ref, gwk_ref, gwv_ref)):
        ref[...] = jnp.transpose(wall[i * share : (i + 1) * share, :].astype(F32))
    gwo_ref[...] = wall[3 * share : 4 * share, :].astype(F32)

    for j in range(1, mp):
        src = place.zahead(j)
        remote(small, rsmall.at[src], s_s.at[0], r_s.at[src], {"mp": src}).wait_recv()
    means = rsmall[0]
    for j in range(1, mp):
        means = means + rsmall[j]
    small_sum = means / width
    rsmall[z] = small_sum

    def last(b):
        at = rows_at(b, TB, TB)
        for j in range(1, mp):
            src = place.zahead(j)
            remote(
                part.at[at, mine], rbuf.at[src, at, :], s_z.at[0, 0], r_z.at[b, src], {"mp": src}
            ).wait_recv()
        inputs = x_ref[at, :].astype(F32)
        center = jnp.mean(inputs, axis=-1, keepdims=True)
        spread = inputs - center
        inverse = lax.rsqrt(jnp.mean(spread * spread, axis=-1, keepdims=True) + EPSILON)
        normal = (x_ref[at, mine].astype(F32) - center) * inverse
        grad = part[at, mine].astype(F32)
        for j in range(1, mp):
            grad = grad + rbuf[place.zahead(j), at, :].astype(F32)
        flat = jnp.concatenate([rsmall[z, :, at], jnp.zeros((120, TB), F32)], axis=0)
        columns = jnp.transpose(flat)
        gin_ref[at, :] = hid[at, mine] + inverse * (
            grad * g1_ref[:, mine] - columns[:, 0:1] - normal * columns[:, 1:2]
        )

    loop(0, blocks, last)

    @pl.when(me < pieces)
    def _():
        for j in range(1, mp):
            out_weight_z(j).wait_send()
            src = place.zahead(j)
            loop(1, n, lambda k, src=src: out_weight_plane(src, k).wait_send())

    for j in range(1, mp):
        spread_copy(gf, s_g, r_g, j).wait_send()
        remote(msg, rmsg.at[z], s_m.at[j], r_m.at[z], {"mp": place.zahead(j)}).wait_send()
        vz_copy(j).wait_send()
        small_copy(j).wait_send()
        for b in range(blocks):
            ger_copy(b, j).wait_send()
            part_z(b, j).wait_send()
    wait_returns(s_r2, r_r2)
    wait_parts(s_p2, r_p2)
    loop(1, n, lambda k: w_copy(k).wait_send())
    loop(1, n, lambda k: v_copy(k).wait_send())
    loop(1, n, lambda k: e_copy(k).wait_send())


def layer(dims, capacity, experts, *args):
    x = args[0]
    dp, ex, mp = dims
    n = dp * ex
    tokens, width = x.shape
    share = width // mp
    hidden = args[-1].shape[0]
    room = -(-capacity // 16) * 16
    while (room * n) % 128:
        room += 16
    slots = n * room
    msgs = experts + 8
    blocks = tokens // TB
    dma = pltpu.SemaphoreType.DMA
    vm = pltpu.VMEM
    scratch = [
        vm((tokens, width), BF16),
        vm((width, 3 * share), BF16),
        vm((tokens, share), BF16),
        vm((tokens, share), BF16),
        vm((3 * share, tokens), BF16),
        vm((share, tokens), BF16),
        vm((8, tokens), F32),
        vm((tokens, 1), F32),
        vm((tokens, share), F32),
        vm((tokens, share), F32),
        vm((3 * share, tokens), BF16),
        vm((tokens, 3 * share), BF16),
        vm((4 * share, width), BF16),
        vm((n, 4 * share // n, width), BF16),
        vm((4 * share, width), BF16),
        vm((8, tokens), F32),
        vm((mp, 8, tokens), F32),
        vm((8, width), F32),
        vm((mp, 8, width), F32),
        vm((8 + experts, width), BF16),
        vm((n, 8 + experts, width), BF16),
        vm((tokens, width), BF16),
        vm((width, width), BF16),
        vm((tokens, width), F32),
        vm((tokens, width), BF16),
        vm((tokens, 1), F32),
        vm((tokens, 128), F32),
        vm((tokens, 128), F32),
        vm((8, tokens), F32),
        vm((2, tokens, 1), F32),
        vm((experts, tokens), F32),
        vm((tokens, 1), F32),
        vm((n, room, tokens), BF16),
        vm((tokens, slots), BF16),
        vm((n, room, 1), F32),
        vm((n, room, 1), F32),
        vm((slots, width), BF16),
        vm((slots, width), BF16),
        vm((slots, hidden), F32),
        vm((slots, hidden), BF16),
        vm((slots, width), BF16),
        vm((mp, tokens, share), BF16),
        vm((mp, tokens, share), BF16),
        vm((tokens, share), F32),
        vm((tokens, width), BF16),
        vm((slots, width), BF16),
        vm((slots, hidden), BF16),
        vm((msgs, tokens), F32),
        vm((mp, msgs, tokens), F32),
        dma((blocks, mp)),
        dma((blocks, mp)),
        dma((n,)),
        dma((n,)),
        dma((mp, n)),
        dma((mp, n)),
        dma((mp,)),
        dma((mp,)),
        dma((mp,)),
        dma((mp,)),
        dma((mp, n)),
        dma((mp, n)),
        dma((mp, n)),
        dma((mp, n)),
        dma((mp,)),
        dma((mp,)),
        dma((blocks, mp)),
        dma((blocks, mp)),
        dma((mp,)),
        dma((mp,)),
        dma((mp,)),
        dma((mp,)),
        dma((mp, n)),
        dma((mp, n)),
        dma((blocks, mp)),
        dma((blocks, mp)),
        dma((mp,)),
        dma((mp,)),
        dma((mp,)),
        dma((mp,)),
        dma((n,)),
        dma((n,)),
        dma((n,)),
        dma((n,)),
        dma((n,)),
        dma((n,)),
    ]
    shapes = (
        jax.ShapeDtypeStruct((tokens, share), BF16),
        jax.ShapeDtypeStruct((8, 128), F32),
        jax.ShapeDtypeStruct((tokens, share), F32),
        jax.ShapeDtypeStruct((width, share), F32),
        jax.ShapeDtypeStruct((width, share), F32),
        jax.ShapeDtypeStruct((width, share), F32),
        jax.ShapeDtypeStruct((share, width), F32),
        jax.ShapeDtypeStruct((8 + experts, width), F32),
        jax.ShapeDtypeStruct((width, hidden), F32),
        jax.ShapeDtypeStruct((hidden, width), F32),
    )
    spec = pl.BlockSpec(memory_space=pltpu.VMEM)
    return pl.pallas_call(
        functools.partial(layer_kernel, dims, capacity, experts),
        out_shape=shapes,
        in_specs=[spec] * len(args),
        out_specs=[spec] * len(shapes),
        scratch_shapes=scratch,
        compiler_params=pltpu.CompilerParams(
            collective_id=0, has_side_effects=True, vmem_limit_bytes=VMEM_LIMIT
        ),
        name="layer",
    )(*args)


def per_device(
    dims,
    inputs,
    teacher,
    top_experts,
    priority,
    valid_mask,
    blocks,
    query_weight,
    key_weight,
    value_weight,
    out_weight,
    router,
    expert_in,
    expert_out,
    first_gain,
    first_bias,
    second_gain,
    second_bias,
):
    experts = router.shape[1]
    capacity = inputs.shape[0] * 2 * 21 // (20 * experts)
    output, loss, grad_input, grad_q, grad_k, grad_v, grad_o, sums, grad_in, grad_out = layer(
        dims,
        capacity,
        experts,
        inputs,
        blocks,
        query_weight,
        key_weight,
        value_weight,
        out_weight,
        first_gain[None],
        first_bias[None],
        second_gain[None],
        second_bias[None],
        router.T,
        top_experts.T,
        priority,
        valid_mask[None],
        teacher,
        expert_in[0],
        expert_out[0],
    )
    return (
        output,
        loss[0, 0:1],
        grad_input,
        grad_q,
        grad_k,
        grad_v,
        grad_o,
        sums[8 : 8 + experts].T,
        grad_in[None],
        grad_out[None],
        sums[0],
        sums[1],
        sums[2],
        sums[3],
    )


def solution(mesh):
    dims = (mesh.shape["dp"], mesh.shape["expert"], mesh.shape["mp"])
    both = ("dp", "expert")
    in_specs = (
        P(both, None),
        P(both, "mp"),
        P(both, None),
        P(both, None),
        P(both),
        P(both, None),
        P(None, "mp"),
        P(None, "mp"),
        P(None, "mp"),
        P("mp", None),
        P(),
        P(both, None, "mp"),
        P(both, "mp", None),
        P(),
        P(),
        P(),
        P(),
    )
    out_specs = (
        P(both, "mp"),
        P(both),
        P(both, "mp"),
        P(None, "mp"),
        P(None, "mp"),
        P(None, "mp"),
        P("mp", None),
        P(),
        P(both, None, "mp"),
        P(both, "mp", None),
        P(),
        P(),
        P(),
        P(),
    )
    return jax.shard_map(
        functools.partial(per_device, dims),
        mesh=mesh,
        in_specs=in_specs,
        out_specs=out_specs,
        check_vma=False,
    )
```

```python
import functools

import jax
import jax.numpy as jnp
from jax import lax
from jax.experimental import pallas as pl
from jax.experimental.pallas import tpu as pltpu
from jax.sharding import PartitionSpec as P

HEAD_DIM = 64
EPSILON = 1e-06
HIGHEST = lax.Precision.HIGHEST
MESH = pl.DeviceIdType.MESH
F32 = jnp.float32
BF16 = jnp.bfloat16
I32 = jnp.int32
VMEM_LIMIT = 67043328


def standardize(values):
    center = values - jnp.mean(values, axis=-1, keepdims=True)
    inverse = lax.rsqrt(jnp.mean(center * center, axis=-1, keepdims=True) + EPSILON)
    return (center * inverse, inverse)


def dot(a, b, precision=None):
    return jnp.dot(a, b, preferred_element_type=F32, precision=precision)


def dot_nt(a, b, precision=None):
    return lax.dot_general(
        a, b, (((1,), (1,)), ((), ())), preferred_element_type=F32, precision=precision
    )


def dot_tn(a, b, precision=None):
    return lax.dot_general(
        a, b, (((0,), (0,)), ((), ())), preferred_element_type=F32, precision=precision
    )


def remote(src, dst, send, recv, device):
    return pltpu.make_async_remote_copy(
        src_ref=src, dst_ref=dst, send_sem=send, recv_sem=recv, device_id=device, device_id_type=MESH
    )


def lanes(f, width):
    return pl.ds(pl.multiple_of(f * width, width), width)


def rows_at(s, count, unit):
    return pl.ds(pl.multiple_of(s * count, unit), count)


def loop(low, high, body):
    def step(i, carry):
        body(i)
        return carry

    lax.fori_loop(low, high, step, 0)


def peer_order(n):
    masks = sorted(range(1, n), key=lambda m: (-bin(m // 2).count("1"), m))
    return [0] + masks


class Place:
    def __init__(self, dims):
        self.dp, self.ex, self.mp = dims
        self.n = self.dp * self.ex
        self.me = lax.axis_index("dp") * self.ex + lax.axis_index("expert")
        self.z = lax.axis_index("mp")
        self.order = peer_order(self.n)

    def peer(self, k):
        mask = 0
        for i in range(1, self.n):
            mask = mask + jnp.where(k == i, self.order[i], 0)
        out = 0
        bit = 1
        while bit < self.n:
            out = out + bit * lax.rem(lax.div(self.me, bit) + lax.div(mask, bit), 2)
            bit *= 2
        return out

    def plane(self, p):
        return {"dp": lax.div(p, self.ex), "expert": lax.rem(p, self.ex)}

    def zahead(self, j):
        return lax.rem(self.z + j, self.mp)

    def greet(self):
        sem = pltpu.get_barrier_semaphore()

        def hello(k):
            pl.semaphore_signal(
                sem, inc=1, device_id=self.plane(self.peer(k)), device_id_type=MESH
            )

        loop(1, self.n, hello)
        for j in range(1, self.mp):
            pl.semaphore_signal(
                sem, inc=1, device_id={"mp": self.zahead(j)}, device_id_type=MESH
            )

    def meet(self):
        pl.semaphore_wait(pltpu.get_barrier_semaphore(), self.n - 1 + self.mp - 1)


def feature_order(mp):
    return [i // 2 if i % 2 == 0 else mp - 1 - i // 2 for i in range(mp)]


TB = 256


def layer_kernel(
    dims,
    capacity,
    experts,
    x_ref,
    blk_ref,
    wq_ref,
    wk_ref,
    wv_ref,
    wo_ref,
    g1_ref,
    b1_ref,
    g2_ref,
    b2_ref,
    rt_ref,
    top_ref,
    pri_ref,
    val_ref,
    tea_ref,
    win_ref,
    wout_ref,
    out_ref,
    loss_ref,
    gin_ref,
    wall,
    vec_ref,
    gwin_hbm,
    gwout_hbm,
    gwin_ref,
    gwout_ref,
    gwo_ref,
    a1,
    wcat,
    keys,
    values,
    turned,
    mixt,
    lse,
    kidc,
    gk,
    gv,
    gt,
    gflat,
    wpk,
    rw,
    small,
    rsmall,
    vz,
    rvz,
    vsend,
    rvec,
    mixf,
    wof,
    hid,
    n2b,
    posc,
    topc,
    sidc,
    sidr,
    gcol,
    grow_t,
    valc,
    disp,
    comb,
    gsl,
    gg,
    sbuf,
    rows,
    dgelu,
    act,
    ret,
    pbuf,
    rbuf,
    own,
    gf,
    grows,
    gi,
    msg,
    rmsg,
    s_a,
    r_a,
    s_d,
    r_d,
    s_r,
    r_r,
    s_p,
    r_p,
    s_g,
    r_g,
    s_d2,
    r_d2,
    s_r2,
    r_r2,
    s_p2,
    r_p2,
    s_g2,
    r_g2,
    s_m,
    r_m,
    s_o,
    r_o,
    s_o2,
    r_o2,
    s_z,
    r_z,
    s_s,
    r_s,
    s_v,
    r_v,
    s_w,
    r_w,
    s_c,
    r_c,
    s_e,
    r_e,
    s_h,
):
    place = Place(dims)
    n, mp, me, z = place.n, place.mp, place.me, place.z
    tokens, width = x_ref.shape
    share = width // mp
    heads = share // HEAD_DIM
    blocks = tokens // TB
    slots = ret.shape[0]
    room = slots // n
    unit = 16
    order = feature_order(mp)
    mine = lanes(z, share)

    def near(dst):
        return jnp.abs(dst - z) < mp - 1

    def block_copy(buf, sends, recvs, at, b, j):
        return remote(
            buf.at[at, mine], buf.at[at, mine], sends.at[b, j], recvs.at[b, z], {"mp": place.zahead(j)}
        )

    def for_near(action):
        for j in (2, 1, 3) if mp == 4 else range(1, mp):

            @pl.when(near(place.zahead(j)))
            def _(j=j):
                action(j)

    def spread_block(buf, sends, recvs, at, b):
        for_near(lambda j: block_copy(buf, sends, recvs, at, b, j).start())

    def pass_copy(buf, sends, recvs, at, b, src, dst):
        return remote(
            buf.at[at, lanes(src, share)],
            buf.at[at, lanes(src, share)],
            sends.at[b, 0],
            recvs.at[b, src],
            {"mp": dst},
        )

    passers = ((mp - 2, 0, mp - 1), (1, mp - 1, 0))

    def pass_block(buf, sends, recvs, at, b):
        for rank, src, dst in passers:

            @pl.when(z == rank)
            def _(src=src, dst=dst):
                copy = pass_copy(buf, sends, recvs, at, b, src, dst)
                copy.wait_recv()
                copy.start()

    def passed(src):
        return ((z == mp - 2) & (src == 0)) | ((z == 1) & (src == mp - 1))

    def wait_block(buf, sends, recvs, at, b, src):
        @pl.when(jnp.logical_not(passed(src)))
        def _():
            remote(
                buf.at[at, mine], buf.at[at, lanes(src, share)], sends.at[b, 0], recvs.at[b, src], {"mp": src}
            ).wait_recv()

    def sent_block(buf, sends, recvs, at, b):
        for_near(lambda j: block_copy(buf, sends, recvs, at, b, j).wait_send())
        for rank, src, dst in passers:

            @pl.when(z == rank)
            def _(src=src, dst=dst):
                pass_copy(buf, sends, recvs, at, b, src, dst).wait_send()

    place.greet()

    wcat[:, 0:share] = wq_ref[...]
    wcat[:, share : 2 * share] = wk_ref[...]
    wcat[:, 2 * share : 3 * share] = wv_ref[...]

    def project(b):
        at = rows_at(b, TB, TB)
        normal, _ = standardize(x_ref[at, :].astype(F32))
        normed = (normal * g1_ref[...] + b1_ref[...]).astype(BF16)
        a1[at, :] = normed
        out = dot(normed, wcat[...])
        lane = lax.broadcasted_iota(I32, (TB, 3 * share), 1)
        out = out * jnp.where(lane < share, 0.125, 1.0)
        keys[at, :] = out[:, share : 2 * share].astype(BF16)
        values[at, :] = out[:, 2 * share : 3 * share].astype(BF16)
        turned[:, at] = jnp.transpose(out).astype(BF16)
        kidc[at, :] = jnp.transpose(jnp.broadcast_to(blk_ref[:, at].astype(F32), (128, TB)))[:, 0:1]

    loop(0, blocks, project)
    place.meet()

    piece = max(16, share // n)
    pieces = share // piece

    def own_piece(ref, s):
        return ref.at[rows_at(s * pieces + me, piece, 16), :]

    def out_weight_z(j):
        return remote(
            wo_ref.at[rows_at(me, piece, 16), :],
            own_piece(wof, z),
            s_o.at[j],
            r_o.at[z],
            {"mp": place.zahead(j)},
        )

    def out_weight_plane(s, k):
        return remote(
            own_piece(wof, s), own_piece(wof, s), s_o2.at[s, k], r_o2.at[s, k], place.plane(place.peer(k))
        )

    @pl.when(me < pieces)
    def _():
        for j in range(1, mp):
            out_weight_z(j).start()

    wof[rows_at(z, share, share), :] = wo_ref[...]

    head_row = lax.div(lax.broadcasted_iota(I32, (share, TB), 0), HEAD_DIM)
    head_lane = lax.div(lax.broadcasted_iota(I32, (TB, share), 1), HEAD_DIM)

    def only(value, where, h):
        return jnp.where(where == h, value, jnp.zeros_like(value))

    def masked_scores(at, h):
        scores = dot(keys[...], only(turned[0:share, at], head_row, h))
        return jnp.where(kidc[...] <= blk_ref[:, at].astype(F32), scores, -1e30)

    def attend(b):
        at = rows_at(b, TB, TB)
        mixed = []
        for h in range(heads):
            scores = masked_scores(at, h)
            peak = jnp.max(scores, axis=0, keepdims=True)
            raised = jnp.exp(scores - peak)
            total = jnp.sum(raised, axis=0, keepdims=True)
            lse[h : h + 1, at] = peak + jnp.log(total)
            probs = (raised * (1.0 / total)).astype(BF16)
            low = 2 * share + h * HEAD_DIM
            mixed.append(dot(turned[low : low + HEAD_DIM, :], probs))
        flat = jnp.concatenate(mixed, axis=0)
        mixt[:, at] = flat.astype(BF16)
        mixf[at, mine] = jnp.transpose(flat).astype(BF16)

        @pl.when(b >= 1)
        def _():
            spread_block(mixf, s_a, r_a, rows_at(b - 1, TB, TB), b - 1)

    loop(0, blocks, attend)
    spread_block(mixf, s_a, r_a, rows_at(blocks - 1, TB, TB), blocks - 1)

    @pl.when(me < pieces)
    def _():
        for j in range(1, mp):
            src = place.zahead(j)
            remote(
                wo_ref.at[rows_at(me, piece, 16), :], own_piece(wof, src), s_o.at[0], r_o.at[src], {"mp": src}
            ).wait_recv()
        for j in range(1, mp):
            src = place.zahead(j)
            loop(1, n, lambda k, src=src: out_weight_plane(src, k).start())

    def out_weight_wait():
        for j in range(1, mp):
            src = place.zahead(j)

            def wait(k, src=src):
                p = place.peer(k)

                @pl.when(p < pieces)
                def _():
                    at = rows_at(src * pieces + p, piece, 16)
                    remote(
                        wof.at[at, :], wof.at[at, :], s_o2.at[src, k], r_o2.at[src, k], place.plane(p)
                    ).wait_recv()

            loop(1, n, wait)

    lane_t = lax.broadcasted_iota(I32, (TB, tokens), 1)
    sub_t = lax.broadcasted_iota(I32, (TB, tokens), 0)
    lane_k = lax.broadcasted_iota(I32, (TB, 128), 1)

    def positions(b):
        at = rows_at(b, TB, TB)
        hit = (sub_t + b * TB) == pri_ref[...]
        pos = jnp.sum(jnp.where(hit, lane_t.astype(F32), 0.0), axis=1, keepdims=True)
        posc[at, :] = pos
        flat = jnp.transpose(jnp.broadcast_to(pos, (TB, 128)))
        sidr[2:3, at] = flat[0:1]
        vt = jnp.transpose(jnp.broadcast_to(val_ref[:, at].astype(F32), (128, TB)))
        valc[at, :] = vt[:, 0:1]
        named = jnp.concatenate(
            [top_ref[:, at].astype(F32), jnp.zeros((126, TB), F32)], axis=0
        )
        topc[at, :] = jnp.transpose(named)

    pass_block(mixf, s_a, r_a, rows_at(0, TB, TB), 0)
    loop(0, blocks, positions)

    lane_all = lax.broadcasted_iota(I32, (tokens, 128), 1)
    first = topc[:, 0:1].astype(I32)
    second = topc[:, 1:2].astype(I32)
    named = jnp.where(
        ((lane_all < experts) & (first == lane_all))
        | ((lane_all >= experts) & (second == lane_all - experts)),
        1.0,
        0.0,
    ).astype(BF16)
    total = jnp.sum(
        jnp.where(first == lane_all - experts, 1.0, 0.0), axis=0, keepdims=True
    )
    pos_row = sidr[2:3, :]

    def ranks(b):
        at = rows_at(b, TB, TB)
        earlier = jnp.where(pos_row < posc[at, :], 1.0, 0.0).astype(BF16)
        count = dot(earlier, named)
        e0 = topc[at, 0:1].astype(I32)
        e1 = topc[at, 1:2].astype(I32)
        r0 = jnp.sum(jnp.where(lane_k == e0, count, 0.0), axis=1, keepdims=True)
        r1 = jnp.sum(jnp.where(lane_k == e1 + experts, count + total, 0.0), axis=1, keepdims=True)
        id0 = jnp.where(r0 < capacity, e0.astype(F32) * room + r0, -1.0)
        id1 = jnp.where(r1 < capacity, e1.astype(F32) * room + r1, -1.0)
        both = jnp.where(lane_k == 0, id0, jnp.where(lane_k == 1, id1, 0.0))
        sidc[at, :] = both
        flat = jnp.transpose(both)
        sidr[0:2, at] = flat[0:2]

    pass_block(mixf, s_a, r_a, rows_at(1, TB, TB), 1)
    loop(0, blocks, ranks)

    out_weight_wait()
    sub_e = lax.broadcasted_iota(I32, (experts, TB), 0)

    def second_norm(b):
        at = rows_at(b, TB, TB)
        for j in range(1, mp):
            src = place.zahead(j)
            wait_block(mixf, s_a, r_a, at, b, src)
        hidden = x_ref[at, :].astype(F32) + dot(mixf[at, :], wof[...])
        hid[at, :] = hidden
        normal, _ = standardize(hidden)
        normed = normal * g2_ref[...] + b2_ref[...]
        n2b[at, :] = normed.astype(BF16)
        logits = dot_nt(rt_ref[...], normed, HIGHEST)
        logits = jnp.exp(logits - jnp.max(logits, axis=0, keepdims=True))
        gates = logits / jnp.sum(logits, axis=0, keepdims=True)
        grow_t[0:experts, at] = gates
        for j in range(2):
            chosen = top_ref[j : j + 1, at]
            gate = jnp.sum(jnp.where(sub_e == chosen, gates, 0.0), axis=0, keepdims=True)
            gate = jnp.where(sidr[j : j + 1, at] >= 0.0, gate, 0.0)
            sidr[5 + j : 6 + j, at] = gate
            gcol[j, at, :] = jnp.transpose(jnp.broadcast_to(gate, (128, TB)))[:, 0:1]

        @pl.when(b + 2 < blocks)
        def _():
            pass_block(mixf, s_a, r_a, rows_at(b + 2, TB, TB), b + 2)

    loop(0, blocks, second_norm)

    sub_c = lax.broadcasted_iota(I32, (room, tokens), 0).astype(F32)

    def fill(k):
        e = place.peer(k)
        base = (e * room).astype(F32)
        hit0 = sidr[0:1, :] == sub_c + base
        hit1 = sidr[1:2, :] == sub_c + base
        pick = jnp.where(hit0 | hit1, 1.0, 0.0).astype(BF16)
        disp[e] = pick
        gsl[e] = jnp.sum(
            jnp.where(hit0, sidr[5:6, :], jnp.where(hit1, sidr[6:7, :], 0.0)), axis=1, keepdims=True
        )
        return e, dot(pick, n2b[...]).astype(BF16)

    def dispatch_copy(k):
        e = place.peer(k)
        return remote(
            sbuf.at[rows_at(e, room, unit)],
            rows.at[rows_at(me, room, unit)],
            s_d.at[k],
            r_d.at[k],
            place.plane(e),
        )

    def dispatch(k):
        e, out = fill(k)
        sbuf[rows_at(e, room, unit), :] = out

        @pl.when(k >= 2)
        def _():
            dispatch_copy(k - 1).start()

    loop(1, n, dispatch)
    e, out = fill(n)
    rows[rows_at(e, room, unit), :] = out
    dispatch_copy(n - 1).start()

    def weigh(b):
        at = rows_at(b, TB, TB)
        slot = lax.broadcasted_iota(I32, (TB, slots), 1).astype(F32)
        comb[at, :] = jnp.where(
            sidc[at, 0:1] == slot,
            gcol[0, at, :],
            jnp.where(sidc[at, 1:2] == slot, gcol[1, at, :], 0.0),
        ).astype(BF16)

    loop(0, blocks, weigh)

    def arrived(buf, recv, send, src):
        remote(
            buf.at[rows_at(src, room, unit)],
            buf.at[rows_at(src, room, unit)],
            send,
            recv,
            place.plane(src),
        ).wait_recv()

    root = 0.7978845608028654
    cube = 0.044715

    def expert_in(k):
        s = place.peer(k)

        @pl.when(k > 0)
        def _():
            arrived(rows, r_d.at[k], s_d.at[k], s)

        at = rows_at(s, room, unit)
        inner = dot(rows[at, :], win_ref[...])
        square = inner * inner
        wave = jnp.tanh(root * inner * (1.0 + cube * square))
        half = 0.5 * (1.0 + wave)
        act[at, :] = (inner * half).astype(BF16)
        dgelu[at, :] = half + 0.5 * inner * (1.0 - wave * wave) * (
            root * (1.0 + 3.0 * cube * square)
        )

    loop(0, n, expert_in)

    def return_copy(sends, recvs, i, f, k):
        s = place.peer(k)
        return remote(
            sbuf.at[rows_at(s, room, unit), lanes(f, share)],
            ret.at[rows_at(me, room, unit), lanes(f, share)],
            sends.at[i, k],
            recvs.at[i, k],
            place.plane(s),
        )

    def give_back(i, f, compute, sends, recvs):
        def send(k):
            s = place.peer(k)
            sbuf[rows_at(s, room, unit), lanes(f, share)] = compute(s).astype(BF16)

            @pl.when(k >= 2)
            def _():
                return_copy(sends, recvs, i, f, k - 1).start()

        loop(1, n, send)
        ret[rows_at(me, room, unit), lanes(f, share)] = compute(me).astype(BF16)
        return_copy(sends, recvs, i, f, n - 1).start()

    loop(1, n, lambda k: dispatch_copy(k).wait_send())

    def wait_returns(sends, recvs):
        for i, f in enumerate(order):

            def wait(k, i=i, f=f):
                return_copy(sends, recvs, i, f, k).wait_send()

            loop(1, n, wait)

    for i, f in enumerate(order):
        give_back(
            i,
            f,
            lambda s, f=f: dot(act[rows_at(s, room, unit), :], wout_ref[:, f * share : (f + 1) * share]),
            s_r,
            r_r,
        )

    def gather_back(i, f, recvs, sends):
        def wait(k):
            src = place.peer(k)
            remote(
                sbuf.at[rows_at(src, room, unit), lanes(f, share)],
                ret.at[rows_at(src, room, unit), lanes(f, share)],
                sends.at[i, k],
                recvs.at[i, k],
                place.plane(src),
            ).wait_recv()

        loop(1, n, wait)

    def part_copy(sends, recvs, f):
        return remote(pbuf.at[f], rbuf.at[z], sends.at[f], recvs.at[z], {"mp": f})

    def reduce_back(sends_r, recvs_r, sends, recvs):
        for i, f in enumerate(order):
            gather_back(i, f, recvs_r, sends_r)

            def combine(b, f=f):
                at = rows_at(b, TB, TB)
                part = dot(comb[at, :], ret[:, f * share : (f + 1) * share])
                pbuf[f, at, :] = part.astype(BF16)

                @pl.when(z == f)
                def _():
                    own[at, :] = part

            loop(0, blocks, combine)

            @pl.when(z != f)
            def _(f=f):
                part_copy(sends, recvs, f).start()

        for j in range(1, mp):
            src = place.zahead(j)
            remote(pbuf.at[0], rbuf.at[src], sends.at[0], recvs.at[src], {"mp": src}).wait_recv()

    def wait_parts(sends, recvs):
        for f in range(mp):

            @pl.when(z != f)
            def _(f=f):
                part_copy(sends, recvs, f).wait_send()

    def summed(at):
        value = own[at, :]
        for j in range(1, mp):
            value = value + rbuf[place.zahead(j), at, :].astype(F32)
        return value

    reduce_back(s_r, r_r, s_p, r_p)

    def finish(b, loss):
        at = rows_at(b, TB, TB)
        final = hid[at, mine] + summed(at)
        out_ref[at, :] = final.astype(BF16)
        residue = final - tea_ref[at, :].astype(F32)
        grad = valc[at, :] * residue
        gf[at, mine] = grad.astype(BF16)
        return loss + 0.5 * jnp.sum(grad * residue)

    loss = lax.fori_loop(0, blocks, finish, jnp.float32(0.0))
    whole = pl.ds(0, tokens)
    spread_block(gf, s_g, r_g, whole, 0)

    wait_returns(s_r, r_r)

    def clear(e):
        gg[e] = jnp.zeros((room, 1), F32)

    loop(0, n, clear)

    if mp == 4:
        turns = ((0, 1, 2, 3), (1, 3, 0, 2), (2, 0, 3, 1), (3, 2, 1, 0))
    else:
        turns = tuple(tuple((r + i) % mp for i in range(mp)) for r in range(mp))

    def turn_at(i):
        f = 0
        for r in range(mp):
            f = f + jnp.where(z == r, turns[r][i], 0)
        return f

    def grad_copy(i, f, k):
        e = place.peer(k)
        return remote(
            sbuf.at[rows_at(e, room, unit), lanes(f, share)],
            grows.at[rows_at(me, room, unit), lanes(f, share)],
            s_d2.at[i, k],
            r_d2.at[i, k],
            place.plane(e),
        )

    for i in range(mp):
        f = turn_at(i)
        if i == 1:
            pass_block(gf, s_g, r_g, whole, 0)
        if i > 0:
            wait_block(gf, s_g, r_g, whole, 0, f)

        def grad_rows(k, f=f):
            e = place.peer(k)
            at = rows_at(e, room, unit)
            picked = dot(disp[e], gf[:, lanes(f, share)])
            gg[e] = gg[e] + jnp.sum(
                picked * ret[at, lanes(f, share)].astype(F32), axis=1, keepdims=True
            )
            return at, (gsl[e] * picked).astype(BF16)

        def grad_send(k, i=i, f=f):
            at, out = grad_rows(k)
            sbuf[at, lanes(f, share)] = out

            @pl.when(k >= 2)
            def _():
                grad_copy(i, f, k - 1).start()

        loop(1, n, grad_send)
        at, out = grad_rows(n)
        grows[at, lanes(f, share)] = out
        grad_copy(i, f, n - 1).start()

    def gate_row(e):
        msg[pl.ds(e, 1), :] = jnp.sum(disp[e].astype(F32) * gg[e], axis=0, keepdims=True)

    loop(0, experts, gate_row)
    msg[experts : experts + 8, :] = jnp.full((8, tokens), loss, F32)
    rmsg[z] = msg[...]
    for j in range(1, mp):
        remote(msg, rmsg.at[z], s_m.at[j], r_m.at[z], {"mp": place.zahead(j)}).start()

    def weigh_back(b):
        at = rows_at(b, TB, TB)
        slot = lax.broadcasted_iota(I32, (TB, slots), 1).astype(F32)
        comb[at, :] = jnp.where(
            (sidc[at, 0:1] == slot) | (sidc[at, 1:2] == slot), 1.0, 0.0
        ).astype(BF16)

    loop(0, blocks, weigh_back)

    def expert_back(k):
        s = place.peer(k)

        @pl.when(k > 0)
        def _():
            for i in range(mp):
                f = turn_at(i)
                remote(
                    grows.at[rows_at(s, room, unit), lanes(f, share)],
                    grows.at[rows_at(s, room, unit), lanes(f, share)],
                    s_d2.at[i, k],
                    r_d2.at[i, k],
                    place.plane(s),
                ).wait_recv()

        at = rows_at(s, room, unit)
        gi[at, :] = (dot_nt(grows[at, :], wout_ref[...]) * dgelu[at, :]).astype(BF16)

    loop(0, n, expert_back)

    def wait_grads():
        for i in range(mp):
            f = turn_at(i)

            def wait(k, i=i, f=f):
                grad_copy(i, f, k).wait_send()

            loop(1, n, wait)

    wait_grads()

    for i, f in enumerate(order):
        give_back(
            i,
            f,
            lambda s, f=f: dot_nt(gi[rows_at(s, room, unit), :], win_ref[f * share : (f + 1) * share, :]),
            s_r2,
            r_r2,
        )

    def weight_grads(b):
        at = lanes(b, 128)
        gwin_ref[at, :] = dot_tn(rows[:, at], gi[...])

    loop(0, width // 128, weight_grads)

    def weight_grads_out(b):
        at = lanes(b, 128)
        gwout_ref[at, :] = dot_tn(act[:, at], grows[...])

    loop(0, gwout_ref.shape[0] // 128, weight_grads_out)

    def store_grads():
        return (
            pltpu.make_async_copy(gwin_ref, gwin_hbm, s_h.at[0]),
            pltpu.make_async_copy(gwout_ref, gwout_hbm, s_h.at[1]),
        )


    loop(0, blocks, lambda b: sent_block(mixf, s_a, r_a, rows_at(b, TB, TB), b))
    wait_parts(s_p, r_p)
    reduce_back(s_r2, r_r2, s_p2, r_p2)

    ger = mixf
    for copy in store_grads():
        copy.start()

    def finish_back(b):
        at = rows_at(b, TB, TB)
        ger[at, mine] = summed(at).astype(BF16)

        @pl.when(b >= 1)
        def _():
            spread_block(ger, s_g2, r_g2, rows_at(b - 1, TB, TB), b - 1)

    loop(0, blocks, finish_back)
    spread_block(ger, s_g2, r_g2, rows_at(blocks - 1, TB, TB), blocks - 1)

    for j in range(1, mp):
        src = place.zahead(j)
        remote(msg, rmsg.at[src], s_m.at[0], r_m.at[src], {"mp": src}).wait_recv()
    grad_probs = rmsg[0]
    for j in range(1, mp):
        grad_probs = grad_probs + rmsg[j]
    loss_ref[...] = grad_probs[experts : experts + 8, 0:128] / (tokens * width)
    grad_probs = grad_probs[0:experts]
    gates = grow_t[0:experts, :]
    grow_t[0:experts, :] = gates * (
        grad_probs - jnp.sum(grad_probs * gates, axis=0, keepdims=True)
    )
    vec_ref[...] = jnp.zeros_like(vec_ref)
    gk[...] = jnp.zeros_like(gk)
    gv[...] = jnp.zeros_like(gv)
    gwo_ref[...] = jnp.zeros_like(gwo_ref)

    def back(b):
        at = rows_at(b, TB, TB)
        @pl.when(b == 0)
        def _():
            pass_block(ger, s_g2, r_g2, rows_at(0, TB, TB), 0)

        for j in range(1, mp):
            wait_block(ger, s_g2, r_g2, at, b, place.zahead(j))
        normal, inverse = standardize(hid[at, :])
        normed = normal * g2_ref[...] + b2_ref[...]
        logits = grow_t[0:experts, at]
        vec_ref[8 : 8 + experts, :] += dot(logits, normed, HIGHEST)
        grad = dot_tn(logits, rt_ref[...], HIGHEST) + ger[at, :].astype(F32)
        vec_ref[2:3, :] += jnp.sum(grad * normal, axis=0, keepdims=True)
        vec_ref[3:4, :] += jnp.sum(grad, axis=0, keepdims=True)
        scaled = grad * g2_ref[...]
        out = gf[at, :].astype(F32) + inverse * (
            scaled
            - jnp.mean(scaled, axis=-1, keepdims=True)
            - normal * jnp.mean(scaled * normal, axis=-1, keepdims=True)
        )
        hid[at, :] = out
        attended = out.astype(BF16)

        @pl.when(b + 1 < blocks)
        def _():
            pass_block(ger, s_g2, r_g2, rows_at(b + 1, TB, TB), b + 1)

        gwo_ref[...] += dot(mixt[:, at], attended)
        mix_t = dot_nt(wo_ref[...], attended)
        mix_low = jnp.transpose(mix_t).astype(BF16)
        mix_t = mix_t.astype(BF16)
        query = jnp.transpose(turned[0:share, at].astype(F32)).astype(BF16)
        grad_query = []
        for h in range(heads):
            probs = jnp.exp(masked_scores(at, h) - lse[h : h + 1, at])
            grad_probs = dot(values[...], only(mix_t, head_row, h))
            centre = jnp.sum(grad_probs * probs, axis=0, keepdims=True)
            grad_scores = (probs * (grad_probs - centre)).astype(BF16)
            low = share + h * HEAD_DIM
            grad_query.append(dot(turned[low : low + HEAD_DIM, :], grad_scores))
            gk[...] += dot(grad_scores, only(query, head_lane, h))
            gv[...] += dot(probs.astype(BF16), only(mix_low, head_lane, h))
        flat = jnp.concatenate(grad_query, axis=0)
        gt[0:share, at] = flat.astype(BF16) * 0.125
        gflat[at, 0:share] = jnp.transpose(flat).astype(BF16) * 0.125

    loop(0, blocks, back)

    part = n2b

    def part_z(b, j):
        at = rows_at(b, TB, TB)
        dst = place.zahead(j)
        return remote(
            part.at[at, lanes(dst, share)], rbuf.at[z, at, :], s_z.at[b, j], r_z.at[b, z], {"mp": dst}
        )

    vz[...] = jnp.zeros_like(vz)

    def first_back(b):
        at = rows_at(b, TB, TB)
        gflat[at, share : 2 * share] = gk[at, :].astype(BF16)
        gflat[at, 2 * share : 3 * share] = gv[at, :].astype(BF16)
        grad = dot_nt(gflat[at, :], wcat[...])
        part[at, :] = grad.astype(BF16)
        normal, _ = standardize(x_ref[at, :].astype(F32))
        scaled = grad * g1_ref[...]
        crossed = grad * normal
        lane = lax.broadcasted_iota(I32, (TB, 128), 1)
        sums = jnp.where(
            lane == 0,
            jnp.sum(scaled, axis=1, keepdims=True),
            jnp.where(lane == 1, jnp.sum(scaled * normal, axis=1, keepdims=True), 0.0),
        )
        small[:, at] = jnp.transpose(sums)[0:8]
        vz[0:1, :] += jnp.sum(crossed, axis=0, keepdims=True)
        vz[1:2, :] += jnp.sum(grad, axis=0, keepdims=True)

        @pl.when(b >= 1)
        def _():
            for j in range(1, mp):
                part_z(b - 1, j).start()

    loop(0, blocks, first_back)

    def vz_copy(j):
        return remote(vz, rvz.at[z], s_v.at[j], r_v.at[z], {"mp": place.zahead(j)})

    def small_copy(j):
        return remote(small, rsmall.at[z], s_s.at[j], r_s.at[z], {"mp": place.zahead(j)})

    for j in range(1, mp):
        vz_copy(j).start()
        part_z(blocks - 1, j).start()
        small_copy(j).start()
    rvz[z] = vz[...]
    rsmall[z] = small[...]

    def turn(b):
        at = rows_at(b, TB, TB)
        gt[share : 2 * share, at] = jnp.transpose(gk[at, :]).astype(BF16)
        gt[2 * share : 3 * share, at] = jnp.transpose(gv[at, :]).astype(BF16)

    loop(0, blocks, turn)
    wpk[0 : 3 * share, :] = dot(gt[...], a1[...]).astype(BF16)
    wpk[3 * share : 4 * share, :] = gwo_ref[...].astype(BF16)
    wrows = 4 * share // n

    def w_copy(k):
        p = place.peer(k)
        return remote(
            wpk.at[rows_at(p, wrows, 16)], rw.at[me], s_w.at[k], r_w.at[k], place.plane(p)
        )

    loop(1, n, lambda k: w_copy(k).start())
    rw[me] = wpk[rows_at(me, wrows, 16), :]

    for j in range(1, mp):
        src = place.zahead(j)
        remote(vz, rvz.at[src], s_v.at[0], r_v.at[src], {"mp": src}).wait_recv()
    total_vz = rvz[0]
    for j in range(1, mp):
        total_vz = total_vz + rvz[j]
    vsend[...] = vec_ref[...].astype(BF16)
    vsend[0:2, :] = total_vz[0:2].astype(BF16)

    def v_copy(k):
        return remote(vsend, rvec.at[me], s_c.at[k], r_c.at[k], place.plane(place.peer(k)))

    rvec[me] = vsend[...]
    loop(1, n, lambda k: v_copy(k).start())

    def w_wait(k):
        src = place.peer(k)
        remote(
            wpk.at[rows_at(0, wrows, 16)], rw.at[src], s_w.at[k], r_w.at[k], place.plane(src)
        ).wait_recv()

    loop(1, n, w_wait)
    acc = rw[0].astype(F32)
    for p in range(1, n):
        acc = acc + rw[p].astype(F32)
    wall[rows_at(me, wrows, 16), :] = acc.astype(BF16)

    def e_copy(k):
        at = rows_at(me, wrows, 16)
        return remote(wall.at[at], wall.at[at], s_e.at[k], r_e.at[k], place.plane(place.peer(k)))

    loop(1, n, lambda k: e_copy(k).start())

    def v_wait(k):
        src = place.peer(k)
        remote(vsend, rvec.at[src], s_c.at[k], r_c.at[k], place.plane(src)).wait_recv()

    loop(1, n, v_wait)
    acc = rvec[0].astype(F32)
    for p in range(1, n):
        acc = acc + rvec[p].astype(F32)
    vec_ref[...] = acc

    def e_wait(k):
        src = place.peer(k)
        at = rows_at(src, wrows, 16)
        remote(wall.at[at], wall.at[at], s_e.at[k], r_e.at[k], place.plane(src)).wait_recv()

    loop(1, n, e_wait)
    for j in range(1, mp):
        src = place.zahead(j)
        remote(small, rsmall.at[src], s_s.at[0], r_s.at[src], {"mp": src}).wait_recv()
    means = rsmall[0]
    for j in range(1, mp):
        means = means + rsmall[j]
    small_sum = means / width
    rsmall[z] = small_sum

    def last(b):
        at = rows_at(b, TB, TB)
        for j in range(1, mp):
            src = place.zahead(j)
            remote(
                part.at[at, mine], rbuf.at[src, at, :], s_z.at[0, 0], r_z.at[b, src], {"mp": src}
            ).wait_recv()
        inputs = x_ref[at, :].astype(F32)
        center = jnp.mean(inputs, axis=-1, keepdims=True)
        spread = inputs - center
        inverse = lax.rsqrt(jnp.mean(spread * spread, axis=-1, keepdims=True) + EPSILON)
        normal = (x_ref[at, mine].astype(F32) - center) * inverse
        grad = part[at, mine].astype(F32)
        for j in range(1, mp):
            grad = grad + rbuf[place.zahead(j), at, :].astype(F32)
        flat = jnp.concatenate([rsmall[z, :, at], jnp.zeros((120, TB), F32)], axis=0)
        columns = jnp.transpose(flat)
        gin_ref[at, :] = hid[at, mine] + inverse * (
            grad * g1_ref[:, mine] - columns[:, 0:1] - normal * columns[:, 1:2]
        )

    loop(0, blocks, last)

    for copy in store_grads():
        copy.wait()

    @pl.when(me < pieces)
    def _():
        for j in range(1, mp):
            out_weight_z(j).wait_send()
            src = place.zahead(j)
            loop(1, n, lambda k, src=src: out_weight_plane(src, k).wait_send())

    for j in range(1, mp):
        remote(msg, rmsg.at[z], s_m.at[j], r_m.at[z], {"mp": place.zahead(j)}).wait_send()
        vz_copy(j).wait_send()
        small_copy(j).wait_send()
        for b in range(blocks):
            part_z(b, j).wait_send()
    sent_block(gf, s_g, r_g, whole, 0)
    loop(0, blocks, lambda b: sent_block(ger, s_g2, r_g2, rows_at(b, TB, TB), b))
    wait_returns(s_r2, r_r2)
    wait_parts(s_p2, r_p2)
    loop(1, n, lambda k: w_copy(k).wait_send())
    loop(1, n, lambda k: v_copy(k).wait_send())
    loop(1, n, lambda k: e_copy(k).wait_send())


def layer(dims, capacity, experts, *args):
    x = args[0]
    dp, ex, mp = dims
    n = dp * ex
    tokens, width = x.shape
    share = width // mp
    hidden = args[-1].shape[0]
    room = -(-capacity // 16) * 16
    while (room * n) % 128:
        room += 16
    slots = n * room
    msgs = experts + 8
    blocks = tokens // TB
    dma = pltpu.SemaphoreType.DMA
    vm = pltpu.VMEM
    scratch = [
        vm((width, hidden), F32),
        vm((hidden, width), F32),
        vm((share, width), F32),
        vm((tokens, width), BF16),
        vm((width, 3 * share), BF16),
        vm((tokens, share), BF16),
        vm((tokens, share), BF16),
        vm((3 * share, tokens), BF16),
        vm((share, tokens), BF16),
        vm((8, tokens), F32),
        vm((tokens, 1), F32),
        vm((tokens, share), F32),
        vm((tokens, share), F32),
        vm((3 * share, tokens), BF16),
        vm((tokens, 3 * share), BF16),
        vm((4 * share, width), BF16),
        vm((n, 4 * share // n, width), BF16),
        vm((8, tokens), F32),
        vm((mp, 8, tokens), F32),
        vm((8, width), F32),
        vm((mp, 8, width), F32),
        vm((8 + experts, width), BF16),
        vm((n, 8 + experts, width), BF16),
        vm((tokens, width), BF16),
        vm((width, width), BF16),
        vm((tokens, width), F32),
        vm((tokens, width), BF16),
        vm((tokens, 1), F32),
        vm((tokens, 128), F32),
        vm((tokens, 128), F32),
        vm((8, tokens), F32),
        vm((2, tokens, 1), F32),
        vm((experts, tokens), F32),
        vm((tokens, 1), F32),
        vm((n, room, tokens), BF16),
        vm((tokens, slots), BF16),
        vm((n, room, 1), F32),
        vm((n, room, 1), F32),
        vm((slots, width), BF16),
        vm((slots, width), BF16),
        vm((slots, hidden), F32),
        vm((slots, hidden), BF16),
        vm((slots, width), BF16),
        vm((mp, tokens, share), BF16),
        vm((mp, tokens, share), BF16),
        vm((tokens, share), F32),
        vm((tokens, width), BF16),
        vm((slots, width), BF16),
        vm((slots, hidden), BF16),
        vm((msgs, tokens), F32),
        vm((mp, msgs, tokens), F32),
        dma((blocks, mp)),
        dma((blocks, mp)),
        dma((n,)),
        dma((n,)),
        dma((mp, n)),
        dma((mp, n)),
        dma((mp,)),
        dma((mp,)),
        dma((1, mp)),
        dma((1, mp)),
        dma((mp, n)),
        dma((mp, n)),
        dma((mp, n)),
        dma((mp, n)),
        dma((mp,)),
        dma((mp,)),
        dma((blocks, mp)),
        dma((blocks, mp)),
        dma((mp,)),
        dma((mp,)),
        dma((mp,)),
        dma((mp,)),
        dma((mp, n)),
        dma((mp, n)),
        dma((blocks, mp)),
        dma((blocks, mp)),
        dma((mp,)),
        dma((mp,)),
        dma((mp,)),
        dma((mp,)),
        dma((n,)),
        dma((n,)),
        dma((n,)),
        dma((n,)),
        dma((n,)),
        dma((n,)),
        dma((2,)),
    ]
    shapes = (
        jax.ShapeDtypeStruct((tokens, share), BF16),
        jax.ShapeDtypeStruct((8, 128), F32),
        jax.ShapeDtypeStruct((tokens, share), F32),
        jax.ShapeDtypeStruct((4 * share, width), BF16),
        jax.ShapeDtypeStruct((8 + experts, width), F32),
        jax.ShapeDtypeStruct((width, hidden), F32),
        jax.ShapeDtypeStruct((hidden, width), F32),
    )
    spec = pl.BlockSpec(memory_space=pltpu.VMEM)
    return pl.pallas_call(
        functools.partial(layer_kernel, dims, capacity, experts),
        out_shape=shapes,
        in_specs=[spec] * len(args),
        out_specs=[spec] * 5 + [pl.BlockSpec(memory_space=pl.ANY)] * 2,
        scratch_shapes=scratch,
        compiler_params=pltpu.CompilerParams(
            collective_id=0, has_side_effects=True, vmem_limit_bytes=VMEM_LIMIT
        ),
        name="layer",
    )(*args)


def results_kernel(
    experts,
    share,
    out,
    loss,
    gin,
    wall,
    vec,
    gwin,
    gwout,
    out_o,
    loss_o,
    gin_o,
    gq_o,
    gk_o,
    gv_o,
    go_o,
    router_o,
    gwin_o,
    gwout_o,
    g1_o,
    b1_o,
    g2_o,
    b2_o,
):
    out_o[...] = out[...]
    gin_o[...] = gin[...]
    gwin_o[...] = gwin[...]
    gwout_o[...] = gwout[...]
    sums = wall[...].astype(F32)
    for i, ref in enumerate((gq_o, gk_o, gv_o)):
        ref[...] = jnp.transpose(sums[i * share : (i + 1) * share])
    go_o[...] = sums[3 * share : 4 * share]

    @pl.when(pl.program_id(0) == 0)
    def _():
        loss_o[...] = loss[0:1, :]
        router_o[...] = vec[8 : 8 + experts, :]
        for i, ref in enumerate((g1_o, b1_o, g2_o, b2_o)):
            ref[...] = vec[i]


def results(experts, steps, out, loss, gin, wall, vec, gwin, gwout):
    tokens, share = out.shape
    width = wall.shape[1]
    hidden = gwin.shape[1]

    def across(shape):
        return pl.BlockSpec((shape[0], shape[1] // steps), lambda i: (0, i))

    def down(shape):
        return pl.BlockSpec((shape[0] // steps, shape[1]), lambda i: (i, 0))

    def once(shape):
        return pl.BlockSpec(shape, lambda i: (0,) * len(shape))

    square = (width, share)
    shapes = (
        ((tokens, share), BF16, down),
        ((1, 128), F32, once),
        ((tokens, share), F32, down),
        (square, F32, down),
        (square, F32, down),
        (square, F32, down),
        ((share, width), F32, across),
        ((experts, width), F32, once),
        ((width, hidden), F32, down),
        ((hidden, width), F32, down),
        ((width,), F32, once),
        ((width,), F32, once),
        ((width,), F32, once),
        ((width,), F32, once),
    )
    return pl.pallas_call(
        functools.partial(results_kernel, experts, share),
        grid=(steps,),
        out_shape=[jax.ShapeDtypeStruct(shape, kind) for shape, kind, _ in shapes],
        in_specs=[
            down(out.shape),
            once(loss.shape),
            down(gin.shape),
            across(wall.shape),
            once(vec.shape),
            down(gwin.shape),
            down(gwout.shape),
        ],
        out_specs=[how(shape) for shape, _, how in shapes],
        name="results",
    )(out, loss, gin, wall, vec, gwin, gwout)


def per_device(
    dims,
    inputs,
    teacher,
    top_experts,
    priority,
    valid_mask,
    blocks,
    query_weight,
    key_weight,
    value_weight,
    out_weight,
    router,
    expert_in,
    expert_out,
    first_gain,
    first_bias,
    second_gain,
    second_bias,
):
    experts = router.shape[1]
    capacity = inputs.shape[0] * 2 * 21 // (20 * experts)
    kept = layer(
        dims,
        capacity,
        experts,
        inputs,
        blocks,
        query_weight,
        key_weight,
        value_weight,
        out_weight,
        first_gain[None],
        first_bias[None],
        second_gain[None],
        second_bias[None],
        router.T,
        top_experts.T,
        priority,
        valid_mask[None],
        teacher,
        expert_in[0],
        expert_out[0],
    )
    done = list(results(experts, dims[2], *kept))
    done[1] = done[1][0, 0:1]
    done[7] = done[7].T
    done[8] = done[8][None]
    done[9] = done[9][None]
    return tuple(done)


def solution(mesh):
    dims = (mesh.shape["dp"], mesh.shape["expert"], mesh.shape["mp"])
    both = ("dp", "expert")
    in_specs = (
        P(both, None),
        P(both, "mp"),
        P(both, None),
        P(both, None),
        P(both),
        P(both, None),
        P(None, "mp"),
        P(None, "mp"),
        P(None, "mp"),
        P("mp", None),
        P(),
        P(both, None, "mp"),
        P(both, "mp", None),
        P(),
        P(),
        P(),
        P(),
    )
    out_specs = (
        P(both, "mp"),
        P(both),
        P(both, "mp"),
        P(None, "mp"),
        P(None, "mp"),
        P(None, "mp"),
        P("mp", None),
        P(),
        P(both, None, "mp"),
        P(both, "mp", None),
        P(),
        P(),
        P(),
        P(),
    )
    return jax.shard_map(
        functools.partial(per_device, dims),
        mesh=mesh,
        in_specs=in_specs,
        out_specs=out_specs,
        check_vma=False,
    )
```

```python
import functools

import jax
import jax.numpy as jnp
from jax import lax
from jax.experimental import pallas as pl
from jax.experimental.pallas import tpu as pltpu
from jax.sharding import PartitionSpec as P

HEAD_DIM = 64
EPSILON = 1e-06
HIGHEST = lax.Precision.HIGHEST
MESH = pl.DeviceIdType.MESH
F32 = jnp.float32
BF16 = jnp.bfloat16
I32 = jnp.int32
VMEM_LIMIT = 67043328


def standardize(values):
    center = values - jnp.mean(values, axis=-1, keepdims=True)
    inverse = lax.rsqrt(jnp.mean(center * center, axis=-1, keepdims=True) + EPSILON)
    return (center * inverse, inverse)


def dot(a, b, precision=None):
    return jnp.dot(a, b, preferred_element_type=F32, precision=precision)


def dot_nt(a, b, precision=None):
    return lax.dot_general(
        a, b, (((1,), (1,)), ((), ())), preferred_element_type=F32, precision=precision
    )


def dot_tn(a, b, precision=None):
    return lax.dot_general(
        a, b, (((0,), (0,)), ((), ())), preferred_element_type=F32, precision=precision
    )


def remote(src, dst, send, recv, device):
    return pltpu.make_async_remote_copy(
        src_ref=src, dst_ref=dst, send_sem=send, recv_sem=recv, device_id=device, device_id_type=MESH
    )


def lanes(f, width):
    return pl.ds(pl.multiple_of(f * width, width), width)


def rows_at(s, count, unit):
    return pl.ds(pl.multiple_of(s * count, unit), count)


def loop(low, high, body):
    def step(i, carry):
        body(i)
        return carry

    lax.fori_loop(low, high, step, 0)


def peer_order(n):
    masks = sorted(range(1, n), key=lambda m: (-bin(m // 2).count("1"), m))
    return [0] + masks


def each(n, body):
    if n <= 8:
        for k in range(1, n):
            body(k)
    else:
        loop(1, n, body)


class Place:
    def __init__(self, dims):
        self.dp, self.ex, self.mp = dims
        self.n = self.dp * self.ex
        self.me = lax.axis_index("dp") * self.ex + lax.axis_index("expert")
        self.z = lax.axis_index("mp")
        self.order = peer_order(self.n)
        self.fixed = [self.flip(mask) for mask in self.order] if self.n <= 8 else None

    def flip(self, mask):
        out = 0
        bit = 1
        while bit < self.n:
            mine = lax.rem(lax.div(self.me, bit), 2)
            out = out + bit * (1 - mine if mask & bit else mine)
            bit *= 2
        return out

    def peer(self, k):
        if isinstance(k, int) and self.fixed:
            return self.fixed[k % self.n]
        mask = 0
        for i in range(1, self.n):
            mask = mask + jnp.where(k == i, self.order[i], 0)
        out = 0
        bit = 1
        while bit < self.n:
            out = out + bit * lax.rem(lax.div(self.me, bit) + lax.div(mask, bit), 2)
            bit *= 2
        return out

    def plane(self, p):
        return {"dp": lax.div(p, self.ex), "expert": lax.rem(p, self.ex)}

    def zahead(self, j):
        return lax.rem(self.z + j, self.mp)

    def greet(self):
        sem = pltpu.get_barrier_semaphore()

        def hello(k):
            pl.semaphore_signal(
                sem, inc=1, device_id=self.plane(self.peer(k)), device_id_type=MESH
            )

        each(self.n, hello)
        for j in range(1, self.mp):
            pl.semaphore_signal(
                sem, inc=1, device_id={"mp": self.zahead(j)}, device_id_type=MESH
            )

    def meet(self):
        pl.semaphore_wait(pltpu.get_barrier_semaphore(), self.n - 1 + self.mp - 1)


def feature_order(mp):
    return [i // 2 if i % 2 == 0 else mp - 1 - i // 2 for i in range(mp)]


TB = 256


def layer_kernel(
    dims,
    capacity,
    experts,
    x_ref,
    blk_ref,
    wq_ref,
    wk_ref,
    wv_ref,
    wo_ref,
    g1_ref,
    b1_ref,
    g2_ref,
    b2_ref,
    rt_ref,
    top_ref,
    pri_ref,
    val_ref,
    tea_ref,
    win_ref,
    wout_ref,
    out_ref,
    loss_ref,
    gin_ref,
    wall,
    vec_ref,
    gwin_hbm,
    gwout_hbm,
    gwin_ref,
    gwout_ref,
    gwo_ref,
    a1,
    wcat,
    keys,
    values,
    turned,
    mixt,
    probs,
    gk,
    gv,
    gt,
    gflat,
    wpk,
    rw,
    small,
    rsmall,
    vz,
    rvz,
    vsend,
    rvec,
    mixf,
    wof,
    hid,
    n2b,
    cols,
    sidr,
    grow_t,
    disp,
    comb,
    sbuf,
    rows,
    dgelu,
    act,
    ret,
    ret2,
    pbuf,
    rbuf,
    own,
    half,
    gf,
    grows,
    gi,
    msg,
    rmsg,
    inners,
    s_a,
    r_a,
    s_d,
    r_d,
    s_r,
    r_r,
    s_p,
    r_p,
    s_g,
    r_g,
    s_d2,
    r_d2,
    s_r2,
    r_r2,
    s_p2,
    r_p2,
    s_g2,
    r_g2,
    s_m,
    r_m,
    s_o,
    r_o,
    s_o2,
    r_o2,
    s_z,
    r_z,
    s_s,
    r_s,
    s_v,
    r_v,
    s_w,
    r_w,
    s_c,
    r_c,
    s_e,
    r_e,
    s_h,
):
    place = Place(dims)
    n, mp, me, z = place.n, place.mp, place.me, place.z
    tokens, width = x_ref.shape
    share = width // mp
    heads = share // HEAD_DIM
    blocks = tokens // TB
    slots = ret.shape[0]
    room = slots // n
    unit = 16
    order = feature_order(mp)
    mine = lanes(z, share)

    def near(dst):
        return jnp.abs(dst - z) < mp - 1

    def block_copy(buf, sends, recvs, at, b, j):
        return remote(
            buf.at[at, mine], buf.at[at, mine], sends.at[b, j], recvs.at[b, z], {"mp": place.zahead(j)}
        )

    def for_near(action):
        for j in (1, 3, 2) if mp == 4 else range(1, mp):

            @pl.when(near(place.zahead(j)))
            def _(j=j):
                action(j)

    def spread_block(buf, sends, recvs, at, b):
        for_near(lambda j: block_copy(buf, sends, recvs, at, b, j).start())

    def pass_copy(buf, sends, recvs, at, b, src, dst):
        return remote(
            buf.at[at, lanes(src, share)],
            buf.at[at, lanes(src, share)],
            sends.at[b, 0],
            recvs.at[b, src],
            {"mp": dst},
        )

    def pass_on(buf, sends, recvs, b, src, dst):
        copy = pass_copy(buf, sends, recvs, rows_at(b, TB, TB), b, src, dst)
        copy.wait_recv()
        copy.start()

    passers = ((mp - 2, 0, mp - 1), (1, mp - 1, 0))

    def pass_block(buf, sends, recvs, at, b):
        for rank, src, dst in passers:

            @pl.when(z == rank)
            def _(src=src, dst=dst):
                copy = pass_copy(buf, sends, recvs, at, b, src, dst)
                copy.wait_recv()
                copy.start()

    def passed(src):
        return ((z == mp - 2) & (src == 0)) | ((z == 1) & (src == mp - 1))

    def wait_block(buf, sends, recvs, at, b, src):
        @pl.when(jnp.logical_not(passed(src)))
        def _():
            remote(
                buf.at[at, mine], buf.at[at, lanes(src, share)], sends.at[b, 0], recvs.at[b, src], {"mp": src}
            ).wait_recv()

    def sent_block(buf, sends, recvs, at, b):
        for_near(lambda j: block_copy(buf, sends, recvs, at, b, j).wait_send())
        for rank, src, dst in passers:

            @pl.when(z == rank)
            def _(src=src, dst=dst):
                pass_copy(buf, sends, recvs, at, b, src, dst).wait_send()

    routes = {
        0: ((0, 0), (0, 1), (0, 2), (2, 0)),
        1: ((1, 0), (0, 0), (1, 2), (2, 2)),
        2: ((1, 1), (2, 1), (0, 0), (2, 3)),
        3: ((1, 3), (3, 1), (3, 2), (0, 0)),
    }
    adder = (2, 2, 1, 1)
    add_slot = (0, 2, 1, 3)

    def pick(table):
        value = 0
        for r in range(mp):
            value = value + jnp.where(z == r, table[r], 0)
        return value

    def route(f):
        return pick([routes[f][r][0] for r in range(mp)]), pick([routes[f][r][1] for r in range(mp)])

    sources = (pick((1, 0, 1, 1)), pick((2, 2, 3, 2)))

    place.greet()

    wcat[:, 0:share] = wq_ref[...]
    wcat[:, share : 2 * share] = wk_ref[...]
    wcat[:, 2 * share : 3 * share] = wv_ref[...]

    def project(b):
        at = rows_at(b, TB, TB)
        normal, _ = standardize(x_ref[at, :].astype(F32))
        normed = (normal * g1_ref[...] + b1_ref[...]).astype(BF16)
        a1[at, :] = normed
        out = dot(normed, wcat[...])
        lane = lax.broadcasted_iota(I32, (TB, 3 * share), 1)
        out = out * jnp.where(lane < share, 0.125, 1.0)
        keys[at, :] = out[:, share : 2 * share].astype(BF16)
        values[at, :] = out[:, 2 * share : 3 * share].astype(BF16)
        turned[:, at] = jnp.transpose(out).astype(BF16)
        flat = jnp.concatenate(
            [
                top_ref[:, at].astype(F32),
                jnp.zeros((1, TB), F32),
                val_ref[:, at].astype(F32),
                blk_ref[:, at].astype(F32),
                jnp.zeros((123, TB), F32),
            ],
            axis=0,
        )
        cols[at, :] = jnp.transpose(flat)

    loop(0, blocks, project)
    place.meet()

    piece = max(16, share // n)
    pieces = share // piece

    def own_piece(ref, s):
        return ref.at[rows_at(s * pieces + me, piece, 16), :]

    def out_weight_z(j):
        return remote(
            wo_ref.at[rows_at(me, piece, 16), :],
            own_piece(wof, z),
            s_o.at[j],
            r_o.at[z],
            {"mp": place.zahead(j)},
        )

    def out_weight_plane(s, k):
        return remote(
            own_piece(wof, s), own_piece(wof, s), s_o2.at[s, k], r_o2.at[s, k], place.plane(place.peer(k))
        )

    @pl.when(me < pieces)
    def _():
        for j in range(1, mp):
            out_weight_z(j).start()

    wof[rows_at(z, share, share), :] = wo_ref[...]

    head_row = lax.div(lax.broadcasted_iota(I32, (share, TB), 0), HEAD_DIM)
    head_lane = lax.div(lax.broadcasted_iota(I32, (TB, share), 1), HEAD_DIM)

    def only(value, where, h):
        return jnp.where(where == h, value, jnp.zeros_like(value))

    def attend(b):
        at = rows_at(b, TB, TB)
        mixed = []
        for h in range(heads):
            scores = dot(keys[...], only(turned[0:share, at], head_row, h))
            scores = jnp.where(cols[:, 4:5] <= blk_ref[:, at].astype(F32), scores, -1e30)
            peak = jnp.max(scores, axis=0, keepdims=True)
            raised = jnp.exp(scores - peak)
            total = jnp.sum(raised, axis=0, keepdims=True)
            low_probs = (raised * (1.0 / total)).astype(BF16)
            probs[h, :, at] = low_probs
            low = 2 * share + h * HEAD_DIM
            mixed.append(dot(turned[low : low + HEAD_DIM, :], low_probs))
        flat = jnp.concatenate(mixed, axis=0)
        mixt[:, at] = flat.astype(BF16)
        mixf[at, mine] = jnp.transpose(flat).astype(BF16)

        positions(b)
        spread_block(mixf, s_a, r_a, at, b)

    lane_t = lax.broadcasted_iota(I32, (TB, tokens), 1)
    sub_t = lax.broadcasted_iota(I32, (TB, tokens), 0)
    lane_k = lax.broadcasted_iota(I32, (TB, 128), 1)
    def positions(b):
        at = rows_at(b, TB, TB)
        hit = (sub_t + b * TB) == pri_ref[...]
        pos = jnp.sum(jnp.where(hit, lane_t.astype(F32), 0.0), axis=1, keepdims=True)
        cols[at, 2:3] = pos
        flat = jnp.transpose(jnp.broadcast_to(pos, (TB, 128)))
        sidr[2:3, at] = flat[0:1]


    loop(0, blocks, attend)

    @pl.when(me < pieces)
    def _():
        for j in range(1, mp):
            src = place.zahead(j)
            remote(
                wo_ref.at[rows_at(me, piece, 16), :], own_piece(wof, src), s_o.at[0], r_o.at[src], {"mp": src}
            ).wait_recv()
        for j in range(1, mp):
            src = place.zahead(j)
            loop(1, n, lambda k, src=src: out_weight_plane(src, k).start())

    def out_weight_wait():
        for j in range(1, mp):
            src = place.zahead(j)

            def wait(k, src=src):
                p = place.peer(k)

                @pl.when(p < pieces)
                def _():
                    at = rows_at(src * pieces + p, piece, 16)
                    remote(
                        wof.at[at, :], wof.at[at, :], s_o2.at[src, k], r_o2.at[src, k], place.plane(p)
                    ).wait_recv()

            each(n, wait)

    pass_block(mixf, s_a, r_a, rows_at(0, TB, TB), 0)

    lane_all = lax.broadcasted_iota(I32, (tokens, 128), 1)
    first = cols[:, 0:1].astype(I32)
    second = cols[:, 1:2].astype(I32)
    named = jnp.where(
        ((lane_all < experts) & (first == lane_all))
        | ((lane_all >= experts) & (second == lane_all - experts)),
        1.0,
        0.0,
    ).astype(BF16)
    total = jnp.sum(
        jnp.where(first == lane_all - experts, 1.0, 0.0), axis=0, keepdims=True
    )
    pos_row = sidr[2:3, :]

    def ranks(b):
        at = rows_at(b, TB, TB)
        earlier = jnp.where(pos_row < cols[at, 2:3], 1.0, 0.0).astype(BF16)
        count = dot(earlier, named)
        e0 = cols[at, 0:1].astype(I32)
        e1 = cols[at, 1:2].astype(I32)
        r0 = jnp.sum(jnp.where(lane_k == e0, count, 0.0), axis=1, keepdims=True)
        r1 = jnp.sum(jnp.where(lane_k == e1 + experts, count + total, 0.0), axis=1, keepdims=True)
        id0 = jnp.where(r0 < capacity, e0.astype(F32) * room + r0, -1.0)
        id1 = jnp.where(r1 < capacity, e1.astype(F32) * room + r1, -1.0)
        both = jnp.where(lane_k == 0, id0, jnp.where(lane_k == 1, id1, 0.0))
        cols[at, 7:8] = id0
        cols[at, 8:9] = id1
        flat = jnp.transpose(both)
        sidr[0:2, at] = flat[0:2]

    pass_block(mixf, s_a, r_a, rows_at(1, TB, TB), 1)
    loop(0, blocks, ranks)

    out_weight_wait()
    sub_e = lax.broadcasted_iota(I32, (experts, TB), 0)

    def second_norm(b):
        at = rows_at(b, TB, TB)
        for j in range(1, mp):
            src = place.zahead(j)
            wait_block(mixf, s_a, r_a, at, b, src)
        hidden = x_ref[at, :].astype(F32) + dot(mixf[at, :], wof[...])
        hid[at, :] = hidden
        normal, _ = standardize(hidden)
        normed = normal * g2_ref[...] + b2_ref[...]
        n2b[at, :] = normed.astype(BF16)
        logits = dot_nt(rt_ref[...], normed, HIGHEST)
        logits = jnp.exp(logits - jnp.max(logits, axis=0, keepdims=True))
        gates = logits / jnp.sum(logits, axis=0, keepdims=True)
        grow_t[0:experts, at] = gates
        for j in range(2):
            chosen = top_ref[j : j + 1, at]
            gate = jnp.sum(jnp.where(sub_e == chosen, gates, 0.0), axis=0, keepdims=True)
            gate = jnp.where(sidr[j : j + 1, at] >= 0.0, gate, 0.0)
            sidr[5 + j : 6 + j, at] = gate
            cols[at, 5 + j : 6 + j] = jnp.transpose(jnp.broadcast_to(gate, (128, TB)))[:, 0:1]

        @pl.when(b + 2 < blocks)
        def _():
            pass_block(mixf, s_a, r_a, rows_at(b + 2, TB, TB), b + 2)

    loop(0, blocks, second_norm)

    sub_c = lax.broadcasted_iota(I32, (room, tokens), 0).astype(F32)

    def fill(k):
        e = place.peer(k)
        base = (e * room).astype(F32)
        hit0 = sidr[0:1, :] == sub_c + base
        hit1 = sidr[1:2, :] == sub_c + base
        pick = jnp.where(hit0 | hit1, 1.0, 0.0).astype(BF16)
        disp[rows_at(e, room, unit), :] = jnp.where(
            hit0, sidr[5:6, :], jnp.where(hit1, sidr[6:7, :], 0.0)
        ).astype(BF16)
        return e, dot(pick, n2b[...]).astype(BF16)

    def dispatch_copy(k):
        e = place.peer(k)
        return remote(
            sbuf.at[rows_at(e, room, unit)],
            rows.at[rows_at(me, room, unit)],
            s_d.at[k],
            r_d.at[k],
            place.plane(e),
        )

    def dispatch(k):
        e, out = fill(k)
        sbuf[rows_at(e, room, unit), :] = out

        @pl.when(k >= 2)
        def _():
            dispatch_copy(k - 1).start()

    loop(1, n, dispatch)
    e, out = fill(n)
    rows[rows_at(e, room, unit), :] = out
    dispatch_copy(n - 1).start()

    def weigh(b):
        at = rows_at(b, TB, TB)
        slot = lax.broadcasted_iota(I32, (TB, slots), 1).astype(F32)
        comb[at, :] = jnp.where(
            cols[at, 7:8] == slot,
            cols[at, 5:6],
            jnp.where(cols[at, 8:9] == slot, cols[at, 6:7], 0.0),
        ).astype(BF16)

    loop(0, blocks, weigh)

    def arrived(buf, recv, send, src):
        remote(
            buf.at[rows_at(src, room, unit)],
            buf.at[rows_at(src, room, unit)],
            send,
            recv,
            place.plane(src),
        ).wait_recv()

    root = 0.7978845608028654
    cube = 0.044715

    def expert_in(k):
        s = place.peer(k)

        @pl.when(k > 0)
        def _():
            arrived(rows, r_d.at[k], s_d.at[k], s)

        at = rows_at(s, room, unit)
        inner = dot(rows[at, :], win_ref[...])
        square = inner * inner
        wave = jnp.tanh(root * inner * (1.0 + cube * square))
        half = 0.5 * (1.0 + wave)
        act[at, :] = (inner * half).astype(BF16)
        dgelu[at, :] = (
            half + 0.5 * inner * (1.0 - wave * wave) * (root * (1.0 + 3.0 * cube * square))
        ).astype(BF16)

    loop(0, n, expert_in)

    def return_copy(sends, recvs, into, i, f, k):
        s = place.peer(k)
        return remote(
            sbuf.at[rows_at(s, room, unit), lanes(f, share)],
            into.at[rows_at(me, room, unit), lanes(f, share)],
            sends.at[i, k],
            recvs.at[i, k],
            place.plane(s),
        )

    def give_back(i, f, value, sends, recvs, into):
        cut = lanes(f, share)
        sbuf[:, cut] = value.astype(BF16)
        at = rows_at(me, room, unit)
        into[at, cut] = sbuf[at, cut]
        each(n, lambda k: return_copy(sends, recvs, into, i, f, k).start())

    each(n, lambda k: dispatch_copy(k).wait_send())

    def wait_returns(sends, recvs):
        for i, f in enumerate(order):

            def wait(k, i=i, f=f):
                return_copy(sends, recvs, ret, i, f, k).wait_send()

            each(n, wait)

    for i, f in enumerate(order):
        give_back(
            i,
            f,
            dot(act[...], wout_ref[:, f * share : (f + 1) * share]),
            s_r,
            r_r,
            ret,
        )

    def gather_back(i, f, recvs, sends, into):
        def wait(k):
            src = place.peer(k)
            remote(
                sbuf.at[rows_at(src, room, unit), lanes(f, share)],
                into.at[rows_at(src, room, unit), lanes(f, share)],
                sends.at[i, k],
                recvs.at[i, k],
                place.plane(src),
            ).wait_recv()

        each(n, wait)

    def part_copy(sends, recvs, f, b):
        at = rows_at(b, TB, TB)
        dst, slot = route(f)
        return remote(
            pbuf.at[f, at, :], rbuf.at[slot, at, :], sends.at[f, b], recvs.at[slot, b], {"mp": dst}
        )

    def wait_slot(sends, recvs, slot, b):
        at = rows_at(b, TB, TB)
        remote(
            pbuf.at[0, at, :], rbuf.at[slot, at, :], sends.at[0, 0], recvs.at[slot, b], {"mp": z}
        ).wait_recv()

    def reduce_back(sends_r, recvs_r, sends, recvs, into):
        for i, f in enumerate(order):
            gather_back(i, f, recvs_r, sends_r, into)

            def combine(b, f=f):
                at = rows_at(b, TB, TB)
                part = dot(comb[at, :], into[:, f * share : (f + 1) * share])
                pbuf[f, at, :] = part.astype(BF16)

                @pl.when(z == f)
                def _():
                    own[at, :] = part

                @pl.when(z == adder[f])
                def _():
                    half[at, :] = part

                @pl.when((z != f) & (z != adder[f]) & (b >= 1))
                def _():
                    part_copy(sends, recvs, f, b - 1).start()

            loop(0, blocks, combine)

            @pl.when((z != f) & (z != adder[f]))
            def _(f=f):
                part_copy(sends, recvs, f, blocks - 1).start()

            @pl.when(z == adder[f])
            def _(f=f):
                def add(b):
                    at = rows_at(b, TB, TB)
                    wait_slot(sends, recvs, add_slot[f], b)
                    pbuf[f, at, :] = (half[at, :] + rbuf[add_slot[f], at, :].astype(F32)).astype(BF16)

                    @pl.when(b >= 1)
                    def _():
                        part_copy(sends, recvs, f, b - 1).start()

                loop(0, blocks, add)
                part_copy(sends, recvs, f, blocks - 1).start()

    def wait_sums(sends, recvs, b):
        for src in sources:
            wait_slot(sends, recvs, src, b)

    def wait_parts(sends, recvs):
        for f in range(mp):

            @pl.when(z != f)
            def _(f=f):
                loop(0, blocks, lambda b: part_copy(sends, recvs, f, b).wait_send())

    def summed(at):
        value = own[at, :]
        for src in sources:
            value = value + rbuf[src, at, :].astype(F32)
        return value

    reduce_back(s_r, r_r, s_p, r_p, ret)

    def finish(b, loss):
        at = rows_at(b, TB, TB)
        wait_sums(s_p, r_p, b)
        final = hid[at, mine] + summed(at)
        out_ref[at, :] = final.astype(BF16)
        residue = final - tea_ref[at, :].astype(F32)
        grad = cols[at, 3:4] * residue
        gf[at, mine] = grad.astype(BF16)

        @pl.when(b >= 1)
        def _():
            spread_block(gf, s_g, r_g, rows_at(b - 1, TB, TB), b - 1)

        return loss + 0.5 * jnp.sum(grad * residue)

    def finish_own():
        loss = lax.fori_loop(0, blocks, finish, jnp.float32(0.0))
        msg[experts : experts + 8, :] = jnp.full((8, tokens), loss, F32)
        spread_block(gf, s_g, r_g, rows_at(blocks - 1, TB, TB), blocks - 1)

    wait_returns(s_r, r_r)

    if mp == 4:
        turns = ((0, 1, 2, 3), (1, 0, 3, 2), (2, 3, 0, 1), (3, 2, 1, 0))
    else:
        turns = tuple(tuple((r + i) % mp for i in range(mp)) for r in range(mp))

    def turn_at(i):
        f = 0
        for r in range(mp):
            f = f + jnp.where(z == r, turns[r][i], 0)
        return f

    def grad_copy(i, f, k):
        e = place.peer(k)
        return remote(
            sbuf.at[rows_at(e, room, unit), lanes(f, share)],
            grows.at[rows_at(me, room, unit), lanes(f, share)],
            s_d2.at[i, k],
            r_d2.at[i, k],
            place.plane(e),
        )

    for i in range(mp):
        f = turn_at(i)
        if any(turns[r][i] == r for r in range(mp)):

            @pl.when(f == z)
            def _():
                finish_own()

        for rank, src, dst in passers:
            if i == (0 if rank == mp - 2 else 1):

                @pl.when(z == rank)
                def _(src=src, dst=dst):
                    loop(0, blocks, lambda b: pass_on(gf, s_g, r_g, b, src, dst))

        if any(turns[r][i] != r for r in range(mp)):
            @pl.when(f != z)
            def _(f=f):
                loop(0, blocks, lambda b: wait_block(gf, s_g, r_g, rows_at(b, TB, TB), b, f))

        cut = lanes(f, share)
        sbuf[:, cut] = dot(disp[...], gf[:, cut]).astype(BF16)
        at = rows_at(me, room, unit)
        grows[at, cut] = sbuf[at, cut]

        def grad_send(k, i=i, f=f):
            grad_copy(i, f, k).start()

        each(n, grad_send)

        def gather_inner(e, i=i, cut=cut):
            at = rows_at(e, room, unit)
            part = sbuf[at, cut].astype(F32) * ret[at, cut].astype(F32)
            inners[at, :] = part if i == 0 else inners[at, :] + part

        loop(0, n, gather_inner)

    def expert_back(k):
        s = place.peer(k)

        @pl.when(k > 0)
        def _():
            for i in range(mp):
                f = turn_at(i)
                remote(
                    grows.at[rows_at(s, room, unit), lanes(f, share)],
                    grows.at[rows_at(s, room, unit), lanes(f, share)],
                    s_d2.at[i, k],
                    r_d2.at[i, k],
                    place.plane(s),
                ).wait_recv()

        at = rows_at(s, room, unit)
        gi[at, :] = (dot_nt(grows[at, :], wout_ref[...]) * dgelu[at, :].astype(F32)).astype(BF16)

    loop(0, n, expert_back)

    def wait_grads():
        for i in range(mp):
            f = turn_at(i)

            def wait(k, i=i, f=f):
                grad_copy(i, f, k).wait_send()

            each(n, wait)

    wait_grads()

    for i, f in enumerate(order):
        give_back(
            i,
            f,
            dot_nt(gi[...], win_ref[f * share : (f + 1) * share, :]),
            s_r2,
            r_r2,
            ret2,
        )

    def gate_row(e):
        at = rows_at(e, room, unit)
        inner = jnp.sum(inners[at, :], axis=1, keepdims=True)
        msg[pl.ds(e, 1), :] = jnp.sum(
            jnp.where(disp[at, :].astype(F32) != 0.0, inner, 0.0), axis=0, keepdims=True
        )

    loop(0, experts, gate_row)
    rmsg[z] = msg[...]
    for j in range(1, mp):
        remote(msg, rmsg.at[z], s_m.at[j], r_m.at[z], {"mp": place.zahead(j)}).start()

    def weigh_back(b):
        at = rows_at(b, TB, TB)
        slot = lax.broadcasted_iota(I32, (TB, slots), 1).astype(F32)
        comb[at, :] = jnp.where(
            (cols[at, 7:8] == slot) | (cols[at, 8:9] == slot), 1.0, 0.0
        ).astype(BF16)

    loop(0, blocks, weigh_back)

    def weight_grads(b):
        at = lanes(b, 128)
        gwin_ref[at, :] = dot_tn(rows[:, at], gi[...])

    loop(0, width // 128, weight_grads)

    def weight_grads_out(b):
        at = lanes(b, 128)
        gwout_ref[at, :] = dot_tn(act[:, at], grows[...])

    loop(0, gwout_ref.shape[0] // 128, weight_grads_out)

    def store_grads():
        return (
            pltpu.make_async_copy(gwin_ref, gwin_hbm, s_h.at[0]),
            pltpu.make_async_copy(gwout_ref, gwout_hbm, s_h.at[1]),
        )


    loop(0, blocks, lambda b: sent_block(mixf, s_a, r_a, rows_at(b, TB, TB), b))
    wait_parts(s_p, r_p)
    reduce_back(s_r2, r_r2, s_p2, r_p2, ret2)

    ger = mixf
    for copy in store_grads():
        copy.start()

    def finish_back(b):
        at = rows_at(b, TB, TB)
        wait_sums(s_p2, r_p2, b)
        ger[at, mine] = summed(at).astype(BF16)

        @pl.when(b >= 1)
        def _():
            spread_block(ger, s_g2, r_g2, rows_at(b - 1, TB, TB), b - 1)

    loop(0, blocks, finish_back)
    spread_block(ger, s_g2, r_g2, rows_at(blocks - 1, TB, TB), blocks - 1)

    for j in range(1, mp):
        src = place.zahead(j)
        remote(msg, rmsg.at[src], s_m.at[0], r_m.at[src], {"mp": src}).wait_recv()
    grad_probs = rmsg[0]
    for j in range(1, mp):
        grad_probs = grad_probs + rmsg[j]
    loss_ref[...] = grad_probs[experts : experts + 8, 0:128] / (tokens * width)
    grad_probs = grad_probs[0:experts]
    gates = grow_t[0:experts, :]
    grow_t[0:experts, :] = grad_probs - gates * jnp.sum(grad_probs, axis=0, keepdims=True)
    vec_ref[...] = jnp.zeros_like(vec_ref)
    gk[...] = jnp.zeros_like(gk)
    gv[...] = jnp.zeros_like(gv)
    gwo_ref[...] = jnp.zeros_like(gwo_ref)

    def back(b):
        at = rows_at(b, TB, TB)
        @pl.when(b == 0)
        def _():
            pass_block(ger, s_g2, r_g2, rows_at(0, TB, TB), 0)

        for j in range(1, mp):
            wait_block(ger, s_g2, r_g2, at, b, place.zahead(j))
        normal, inverse = standardize(hid[at, :])
        normed = normal * g2_ref[...] + b2_ref[...]
        logits = grow_t[0:experts, at]
        vec_ref[8 : 8 + experts, :] += dot(logits, normed, HIGHEST)
        grad = dot_tn(logits, rt_ref[...], HIGHEST) + ger[at, :].astype(F32)
        vec_ref[2:3, :] += jnp.sum(grad * normal, axis=0, keepdims=True)
        vec_ref[3:4, :] += jnp.sum(grad, axis=0, keepdims=True)
        scaled = grad * g2_ref[...]
        out = gf[at, :].astype(F32) + inverse * (
            scaled
            - jnp.mean(scaled, axis=-1, keepdims=True)
            - normal * jnp.mean(scaled * normal, axis=-1, keepdims=True)
        )
        hid[at, :] = out
        attended = out.astype(BF16)

        @pl.when(b + 1 < blocks)
        def _():
            pass_block(ger, s_g2, r_g2, rows_at(b + 1, TB, TB), b + 1)

        gwo_ref[...] += dot(mixt[:, at], attended)
        mix_t = dot_nt(wo_ref[...], attended)
        mix_low = jnp.transpose(mix_t).astype(BF16)
        mix_t = mix_t.astype(BF16)
        query = jnp.transpose(turned[0:share, at].astype(F32)).astype(BF16)
        grad_query = []
        for h in range(heads):
            low_probs = probs[h, :, at]
            wide = low_probs.astype(F32)
            grad_probs = dot(values[...], only(mix_t, head_row, h))
            centre = jnp.sum(grad_probs * wide, axis=0, keepdims=True)
            grad_scores = (wide * (grad_probs - centre)).astype(BF16)
            low = share + h * HEAD_DIM
            grad_query.append(dot(turned[low : low + HEAD_DIM, :], grad_scores))
            gk[...] += dot(grad_scores, only(query, head_lane, h))
            gv[...] += dot(low_probs, only(mix_low, head_lane, h))
        flat = jnp.concatenate(grad_query, axis=0)
        gt[0:share, at] = flat.astype(BF16) * 0.125
        gflat[at, 0:share] = jnp.transpose(flat).astype(BF16) * 0.125

    loop(0, blocks, back)

    part = n2b

    def part_z(b, f):
        at = rows_at(b, TB, TB)
        dst, slot = route(f)
        return remote(
            part.at[at, lanes(f, share)], rbuf.at[slot, at, :], s_z.at[b, f], r_z.at[b, slot], {"mp": dst}
        )

    def wait_z(b, slot):
        at = rows_at(b, TB, TB)
        remote(
            part.at[at, mine], rbuf.at[slot, at, :], s_z.at[0, 0], r_z.at[b, slot], {"mp": z}
        ).wait_recv()

    far_first = (3, 0, 2, 1)

    def send_parts(b):
        for f in far_first:

            @pl.when((z != f) & (z != adder[f]))
            def _(f=f):
                part_z(b, f).start()

    def add_parts(b):
        at = rows_at(b, TB, TB)
        for f in far_first:

            @pl.when(z == adder[f])
            def _(f=f):
                wait_z(b, add_slot[f])
                cut = lanes(f, share)
                part[at, cut] = (
                    part[at, cut].astype(F32) + rbuf[add_slot[f], at, :].astype(F32)
                ).astype(BF16)

    def send_added(b):
        for f in far_first:

            @pl.when(z == adder[f])
            def _(f=f):
                part_z(b, f).start()

    vz[...] = jnp.zeros_like(vz)

    def first_back(b):
        at = rows_at(b, TB, TB)
        gflat[at, share : 2 * share] = gk[at, :].astype(BF16)
        gflat[at, 2 * share : 3 * share] = gv[at, :].astype(BF16)
        grad = dot_nt(gflat[at, :], wcat[...])
        part[at, :] = grad.astype(BF16)
        normal, _ = standardize(x_ref[at, :].astype(F32))
        scaled = grad * g1_ref[...]
        crossed = grad * normal
        lane = lax.broadcasted_iota(I32, (TB, 128), 1)
        sums = jnp.where(
            lane == 0,
            jnp.sum(scaled, axis=1, keepdims=True),
            jnp.where(lane == 1, jnp.sum(scaled * normal, axis=1, keepdims=True), 0.0),
        )
        small[:, at] = jnp.transpose(sums)[0:8]
        vz[0:1, :] += jnp.sum(crossed, axis=0, keepdims=True)
        vz[1:2, :] += jnp.sum(grad, axis=0, keepdims=True)

        @pl.when(b >= 1)
        def _():
            send_parts(b - 1)

    loop(0, blocks, first_back)

    def vz_copy(j):
        return remote(vz, rvz.at[z], s_v.at[j], r_v.at[z], {"mp": place.zahead(j)})

    def small_copy(j):
        return remote(small, rsmall.at[z], s_s.at[j], r_s.at[z], {"mp": place.zahead(j)})

    for j in range(1, mp):
        vz_copy(j).start()
    send_parts(blocks - 1)
    for j in range(1, mp):
        small_copy(j).start()
    rvz[z] = vz[...]
    rsmall[z] = small[...]

    def turn(b):
        at = rows_at(b, TB, TB)
        gt[share : 2 * share, at] = jnp.transpose(gk[at, :]).astype(BF16)
        gt[2 * share : 3 * share, at] = jnp.transpose(gv[at, :]).astype(BF16)

    loop(0, blocks, turn)
    wpk[0 : 3 * share, :] = dot(gt[...], a1[...]).astype(BF16)
    wpk[3 * share : 4 * share, :] = gwo_ref[...].astype(BF16)
    wrows = 4 * share // n

    def w_copy(k):
        p = place.peer(k)
        return remote(
            wpk.at[rows_at(p, wrows, 16)], rw.at[me], s_w.at[k], r_w.at[k], place.plane(p)
        )

    each(n, lambda k: w_copy(k).start())
    rw[me] = wpk[rows_at(me, wrows, 16), :]

    add_parts(0)
    add_parts(1)
    send_added(0)

    for j in range(1, mp):
        src = place.zahead(j)
        remote(vz, rvz.at[src], s_v.at[0], r_v.at[src], {"mp": src}).wait_recv()
    total_vz = rvz[0]
    for j in range(1, mp):
        total_vz = total_vz + rvz[j]
    vsend[...] = vec_ref[...].astype(BF16)
    vsend[0:2, :] = total_vz[0:2].astype(BF16)

    def v_copy(k):
        return remote(vsend, rvec.at[me], s_c.at[k], r_c.at[k], place.plane(place.peer(k)))

    rvec[me] = vsend[...]
    each(n, lambda k: v_copy(k).start())

    def w_wait(k):
        src = place.peer(k)
        remote(
            wpk.at[rows_at(0, wrows, 16)], rw.at[src], s_w.at[k], r_w.at[k], place.plane(src)
        ).wait_recv()

    each(n, w_wait)
    acc = rw[0].astype(F32)
    for p in range(1, n):
        acc = acc + rw[p].astype(F32)
    wall[rows_at(me, wrows, 16), :] = acc.astype(BF16)

    def e_copy(k):
        at = rows_at(me, wrows, 16)
        return remote(wall.at[at], wall.at[at], s_e.at[k], r_e.at[k], place.plane(place.peer(k)))

    each(n, lambda k: e_copy(k).start())
    send_added(1)
    add_parts(2)
    add_parts(3)
    send_added(2)

    def v_wait(k):
        src = place.peer(k)
        remote(vsend, rvec.at[src], s_c.at[k], r_c.at[k], place.plane(src)).wait_recv()

    each(n, v_wait)
    acc = rvec[0].astype(F32)
    for p in range(1, n):
        acc = acc + rvec[p].astype(F32)
    vec_ref[...] = acc
    send_added(3)

    def e_wait(k):
        src = place.peer(k)
        at = rows_at(src, wrows, 16)
        remote(wall.at[at], wall.at[at], s_e.at[k], r_e.at[k], place.plane(src)).wait_recv()

    each(n, e_wait)
    for j in range(1, mp):
        src = place.zahead(j)
        remote(small, rsmall.at[src], s_s.at[0], r_s.at[src], {"mp": src}).wait_recv()
    means = rsmall[0]
    for j in range(1, mp):
        means = means + rsmall[j]
    small_sum = means / width
    rsmall[z] = small_sum

    def last(b):
        at = rows_at(b, TB, TB)
        for src in sources:
            wait_z(b, src)
        inputs = x_ref[at, :].astype(F32)
        center = jnp.mean(inputs, axis=-1, keepdims=True)
        spread = inputs - center
        inverse = lax.rsqrt(jnp.mean(spread * spread, axis=-1, keepdims=True) + EPSILON)
        normal = (x_ref[at, mine].astype(F32) - center) * inverse
        grad = part[at, mine].astype(F32)
        for src in sources:
            grad = grad + rbuf[src, at, :].astype(F32)
        flat = jnp.concatenate([rsmall[z, :, at], jnp.zeros((120, TB), F32)], axis=0)
        columns = jnp.transpose(flat)
        gin_ref[at, :] = hid[at, mine] + inverse * (
            grad * g1_ref[:, mine] - columns[:, 0:1] - normal * columns[:, 1:2]
        )

    loop(0, blocks, last)

    for copy in store_grads():
        copy.wait()

    @pl.when(me < pieces)
    def _():
        for j in range(1, mp):
            out_weight_z(j).wait_send()
            src = place.zahead(j)
            loop(1, n, lambda k, src=src: out_weight_plane(src, k).wait_send())

    for j in range(1, mp):
        remote(msg, rmsg.at[z], s_m.at[j], r_m.at[z], {"mp": place.zahead(j)}).wait_send()
        vz_copy(j).wait_send()
        small_copy(j).wait_send()
    for f in range(mp):

        @pl.when(z != f)
        def _(f=f):
            loop(0, blocks, lambda b: part_z(b, f).wait_send())

    loop(0, blocks, lambda b: sent_block(gf, s_g, r_g, rows_at(b, TB, TB), b))
    loop(0, blocks, lambda b: sent_block(ger, s_g2, r_g2, rows_at(b, TB, TB), b))
    wait_returns(s_r2, r_r2)
    wait_parts(s_p2, r_p2)
    each(n, lambda k: w_copy(k).wait_send())
    each(n, lambda k: v_copy(k).wait_send())
    each(n, lambda k: e_copy(k).wait_send())


def layer(dims, capacity, experts, *args):
    x = args[0]
    dp, ex, mp = dims
    n = dp * ex
    tokens, width = x.shape
    share = width // mp
    hidden = args[-1].shape[0]
    room = -(-capacity // 16) * 16
    while (room * n) % 128:
        room += 16
    slots = n * room
    msgs = experts + 8
    blocks = tokens // TB
    heads = share // HEAD_DIM
    dma = pltpu.SemaphoreType.DMA
    vm = pltpu.VMEM
    scratch = [
        vm((width, hidden), F32),
        vm((hidden, width), F32),
        vm((share, width), F32),
        vm((tokens, width), BF16),
        vm((width, 3 * share), BF16),
        vm((tokens, share), BF16),
        vm((tokens, share), BF16),
        vm((3 * share, tokens), BF16),
        vm((share, tokens), BF16),
        vm((heads, tokens, tokens), BF16),
        vm((tokens, share), F32),
        vm((tokens, share), F32),
        vm((3 * share, tokens), BF16),
        vm((tokens, 3 * share), BF16),
        vm((4 * share, width), BF16),
        vm((n, 4 * share // n, width), BF16),
        vm((8, tokens), F32),
        vm((mp, 8, tokens), F32),
        vm((8, width), F32),
        vm((mp, 8, width), F32),
        vm((8 + experts, width), BF16),
        vm((n, 8 + experts, width), BF16),
        vm((tokens, width), BF16),
        vm((width, width), BF16),
        vm((tokens, width), F32),
        vm((tokens, width), BF16),
        vm((tokens, 128), F32),
        vm((8, tokens), F32),
        vm((experts, tokens), F32),
        vm((slots, tokens), BF16),
        vm((tokens, slots), BF16),
        vm((slots, width), BF16),
        vm((slots, width), BF16),
        vm((slots, hidden), BF16),
        vm((slots, hidden), BF16),
        vm((slots, width), BF16),
        vm((slots, width), BF16),
        vm((mp, tokens, share), BF16),
        vm((mp, tokens, share), BF16),
        vm((tokens, share), F32),
        vm((tokens, share), F32),
        vm((tokens, width), BF16),
        vm((slots, width), BF16),
        vm((slots, hidden), BF16),
        vm((msgs, tokens), F32),
        vm((mp, msgs, tokens), F32),
        vm((slots, share), F32),
        dma((blocks, mp)),
        dma((blocks, mp)),
        dma((n,)),
        dma((n,)),
        dma((mp, n)),
        dma((mp, n)),
        dma((mp, blocks)),
        dma((mp, blocks)),
        dma((blocks, mp)),
        dma((blocks, mp)),
        dma((mp, n)),
        dma((mp, n)),
        dma((mp, n)),
        dma((mp, n)),
        dma((mp, blocks)),
        dma((mp, blocks)),
        dma((blocks, mp)),
        dma((blocks, mp)),
        dma((mp,)),
        dma((mp,)),
        dma((mp,)),
        dma((mp,)),
        dma((mp, n)),
        dma((mp, n)),
        dma((blocks, mp)),
        dma((blocks, mp)),
        dma((mp,)),
        dma((mp,)),
        dma((mp,)),
        dma((mp,)),
        dma((n,)),
        dma((n,)),
        dma((n,)),
        dma((n,)),
        dma((n,)),
        dma((n,)),
        dma((2,)),
    ]
    shapes = (
        jax.ShapeDtypeStruct((tokens, share), BF16),
        jax.ShapeDtypeStruct((8, 128), F32),
        jax.ShapeDtypeStruct((tokens, share), F32),
        jax.ShapeDtypeStruct((4 * share, width), BF16),
        jax.ShapeDtypeStruct((8 + experts, width), F32),
        jax.ShapeDtypeStruct((width, hidden), F32),
        jax.ShapeDtypeStruct((hidden, width), F32),
    )
    spec = pl.BlockSpec(memory_space=pltpu.VMEM)
    return pl.pallas_call(
        functools.partial(layer_kernel, dims, capacity, experts),
        out_shape=shapes,
        in_specs=[spec] * len(args),
        out_specs=[spec] * 5 + [pl.BlockSpec(memory_space=pl.ANY)] * 2,
        scratch_shapes=scratch,
        compiler_params=pltpu.CompilerParams(
            collective_id=0, has_side_effects=True, vmem_limit_bytes=VMEM_LIMIT
        ),
        name="layer",
    )(*args)


def results_kernel(
    experts,
    share,
    out,
    loss,
    gin,
    wall,
    vec,
    gwin,
    gwout,
    out_o,
    loss_o,
    gin_o,
    gq_o,
    gk_o,
    gv_o,
    go_o,
    router_o,
    gwin_o,
    gwout_o,
    g1_o,
    b1_o,
    g2_o,
    b2_o,
):
    out_o[...] = out[...]
    gin_o[...] = gin[...]
    gwin_o[...] = gwin[...]
    gwout_o[...] = gwout[...]
    sums = wall[...].astype(F32)
    for i, ref in enumerate((gq_o, gk_o, gv_o)):
        ref[...] = jnp.transpose(sums[i * share : (i + 1) * share])
    go_o[...] = sums[3 * share : 4 * share]

    @pl.when(pl.program_id(0) == 0)
    def _():
        loss_o[...] = loss[0:1, :]
        router_o[...] = vec[8 : 8 + experts, :]
        for i, ref in enumerate((g1_o, b1_o, g2_o, b2_o)):
            ref[...] = vec[i]


def results(experts, steps, out, loss, gin, wall, vec, gwin, gwout):
    tokens, share = out.shape
    width = wall.shape[1]
    hidden = gwin.shape[1]

    def across(shape):
        return pl.BlockSpec((shape[0], shape[1] // steps), lambda i: (0, i))

    def down(shape):
        return pl.BlockSpec((shape[0] // steps, shape[1]), lambda i: (i, 0))

    def once(shape):
        return pl.BlockSpec(shape, lambda i: (0,) * len(shape))

    square = (width, share)
    shapes = (
        ((tokens, share), BF16, down),
        ((1, 128), F32, once),
        ((tokens, share), F32, down),
        (square, F32, down),
        (square, F32, down),
        (square, F32, down),
        ((share, width), F32, across),
        ((experts, width), F32, once),
        ((width, hidden), F32, down),
        ((hidden, width), F32, down),
        ((width,), F32, once),
        ((width,), F32, once),
        ((width,), F32, once),
        ((width,), F32, once),
    )
    return pl.pallas_call(
        functools.partial(results_kernel, experts, share),
        grid=(steps,),
        out_shape=[jax.ShapeDtypeStruct(shape, kind) for shape, kind, _ in shapes],
        in_specs=[
            down(out.shape),
            once(loss.shape),
            down(gin.shape),
            across(wall.shape),
            once(vec.shape),
            down(gwin.shape),
            down(gwout.shape),
        ],
        out_specs=[how(shape) for shape, _, how in shapes],
        name="results",
    )(out, loss, gin, wall, vec, gwin, gwout)


def per_device(
    dims,
    inputs,
    teacher,
    top_experts,
    priority,
    valid_mask,
    blocks,
    query_weight,
    key_weight,
    value_weight,
    out_weight,
    router,
    expert_in,
    expert_out,
    first_gain,
    first_bias,
    second_gain,
    second_bias,
):
    experts = router.shape[1]
    capacity = inputs.shape[0] * 2 * 21 // (20 * experts)
    kept = layer(
        dims,
        capacity,
        experts,
        inputs,
        blocks,
        query_weight,
        key_weight,
        value_weight,
        out_weight,
        first_gain[None],
        first_bias[None],
        second_gain[None],
        second_bias[None],
        router.T,
        top_experts.T,
        priority,
        valid_mask[None],
        teacher,
        expert_in[0],
        expert_out[0],
    )
    done = list(results(experts, dims[2], *kept))
    done[1] = done[1][0, 0:1]
    done[7] = done[7].T
    done[8] = done[8][None]
    done[9] = done[9][None]
    return tuple(done)


def solution(mesh):
    dims = (mesh.shape["dp"], mesh.shape["expert"], mesh.shape["mp"])
    both = ("dp", "expert")
    in_specs = (
        P(both, None),
        P(both, "mp"),
        P(both, None),
        P(both, None),
        P(both),
        P(both, None),
        P(None, "mp"),
        P(None, "mp"),
        P(None, "mp"),
        P("mp", None),
        P(),
        P(both, None, "mp"),
        P(both, "mp", None),
        P(),
        P(),
        P(),
        P(),
    )
    out_specs = (
        P(both, "mp"),
        P(both),
        P(both, "mp"),
        P(None, "mp"),
        P(None, "mp"),
        P(None, "mp"),
        P("mp", None),
        P(),
        P(both, None, "mp"),
        P(both, "mp", None),
        P(),
        P(),
        P(),
        P(),
    )
    return jax.shard_map(
        functools.partial(per_device, dims),
        mesh=mesh,
        in_specs=in_specs,
        out_specs=out_specs,
        check_vma=False,
    )
```

```python
import functools

import jax
import jax.numpy as jnp
from jax import lax
from jax.experimental import pallas as pl
from jax.experimental.pallas import tpu as pltpu
from jax.sharding import PartitionSpec as P

HEAD_DIM = 64
EPSILON = 1e-06
HIGHEST = lax.Precision.HIGHEST
MESH = pl.DeviceIdType.MESH
F32 = jnp.float32
BF16 = jnp.bfloat16
I32 = jnp.int32
VMEM_LIMIT = 67043328


def standardize(values):
    center = values - jnp.mean(values, axis=-1, keepdims=True)
    inverse = lax.rsqrt(jnp.mean(center * center, axis=-1, keepdims=True) + EPSILON)
    return (center * inverse, inverse)


def dot(a, b, precision=None):
    return jnp.dot(a, b, preferred_element_type=F32, precision=precision)


def dot_nt(a, b, precision=None):
    return lax.dot_general(
        a, b, (((1,), (1,)), ((), ())), preferred_element_type=F32, precision=precision
    )


def dot_tn(a, b, precision=None):
    return lax.dot_general(
        a, b, (((0,), (0,)), ((), ())), preferred_element_type=F32, precision=precision
    )


def remote(src, dst, send, recv, device):
    return pltpu.make_async_remote_copy(
        src_ref=src, dst_ref=dst, send_sem=send, recv_sem=recv, device_id=device, device_id_type=MESH
    )


def lanes(f, width):
    return pl.ds(pl.multiple_of(f * width, width), width)


def rows_at(s, count, unit):
    return pl.ds(pl.multiple_of(s * count, unit), count)


def loop(low, high, body):
    def step(i, carry):
        body(i)
        return carry

    lax.fori_loop(low, high, step, 0)


def peer_order(n):
    masks = sorted(range(1, n), key=lambda m: (-bin(m // 2).count("1"), m))
    return [0] + masks


def each(n, body):
    if n <= 8:
        for k in range(1, n):
            body(k)
    else:
        loop(1, n, body)


class Place:
    def __init__(self, dims):
        self.dp, self.ex, self.mp = dims
        self.n = self.dp * self.ex
        self.me = lax.axis_index("dp") * self.ex + lax.axis_index("expert")
        self.z = lax.axis_index("mp")
        self.order = peer_order(self.n)
        self.fixed = [self.flip(mask) for mask in self.order] if self.n <= 8 else None

    def flip(self, mask):
        out = 0
        bit = 1
        while bit < self.n:
            mine = lax.rem(lax.div(self.me, bit), 2)
            out = out + bit * (1 - mine if mask & bit else mine)
            bit *= 2
        return out

    def peer(self, k):
        if isinstance(k, int) and self.fixed:
            return self.fixed[k % self.n]
        mask = 0
        for i in range(1, self.n):
            mask = mask + jnp.where(k == i, self.order[i], 0)
        out = 0
        bit = 1
        while bit < self.n:
            out = out + bit * lax.rem(lax.div(self.me, bit) + lax.div(mask, bit), 2)
            bit *= 2
        return out

    def plane(self, p):
        return {"dp": lax.div(p, self.ex), "expert": lax.rem(p, self.ex)}

    def zahead(self, j):
        return lax.rem(self.z + j, self.mp)

    def greet(self):
        sem = pltpu.get_barrier_semaphore()

        def hello(k):
            pl.semaphore_signal(
                sem, inc=1, device_id=self.plane(self.peer(k)), device_id_type=MESH
            )

        each(self.n, hello)
        for j in range(1, self.mp):
            pl.semaphore_signal(
                sem, inc=1, device_id={"mp": self.zahead(j)}, device_id_type=MESH
            )

    def meet(self):
        pl.semaphore_wait(pltpu.get_barrier_semaphore(), self.n - 1 + self.mp - 1)


def feature_order(mp):
    return [i // 2 if i % 2 == 0 else mp - 1 - i // 2 for i in range(mp)]


TB = 256


def layer_kernel(
    dims,
    capacity,
    experts,
    x_ref,
    blk_ref,
    wq_ref,
    wk_ref,
    wv_ref,
    wo_ref,
    g1_ref,
    b1_ref,
    g2_ref,
    b2_ref,
    rt_ref,
    top_ref,
    pri_ref,
    val_ref,
    tea_ref,
    win_ref,
    wout_ref,
    out_ref,
    loss_ref,
    gin_ref,
    wall,
    vec_ref,
    gwin_hbm,
    gwout_hbm,
    gwin_ref,
    gwout_ref,
    gwo_ref,
    a1,
    wcat,
    keys,
    values,
    turned,
    mixt,
    probs,
    gk,
    gv,
    gt,
    gflat,
    wpk,
    rw,
    small,
    rsmall,
    vz,
    rvz,
    vsend,
    rvec,
    mixf,
    wof,
    hid,
    n2b,
    cols,
    sidr,
    grow_t,
    disp,
    comb,
    sbuf,
    rows,
    dgelu,
    act,
    ret,
    ret2,
    pbuf,
    rbuf,
    own,
    half,
    gf,
    grows,
    gi,
    msg,
    rmsg,
    inners,
    s_a,
    r_a,
    s_d,
    r_d,
    s_r,
    r_r,
    s_p,
    r_p,
    s_g,
    r_g,
    s_d2,
    r_d2,
    s_r2,
    r_r2,
    s_p2,
    r_p2,
    s_g2,
    r_g2,
    s_m,
    r_m,
    s_o,
    r_o,
    s_o2,
    r_o2,
    s_z,
    r_z,
    s_s,
    r_s,
    s_v,
    r_v,
    s_w,
    r_w,
    s_c,
    r_c,
    s_e,
    r_e,
    s_h,
):
    place = Place(dims)
    n, mp, me, z = place.n, place.mp, place.me, place.z
    tokens, width = x_ref.shape
    share = width // mp
    heads = share // HEAD_DIM
    blocks = tokens // TB
    slots = ret.shape[0]
    room = slots // n
    unit = 16
    order = feature_order(mp)
    mine = lanes(z, share)

    def near(dst):
        return jnp.abs(dst - z) < mp - 1

    def block_copy(buf, sends, recvs, at, b, j):
        return remote(
            buf.at[at, mine], buf.at[at, mine], sends.at[b, j], recvs.at[b, z], {"mp": place.zahead(j)}
        )

    def for_near(action):
        for j in (1, 3, 2) if mp == 4 else range(1, mp):

            @pl.when(near(place.zahead(j)))
            def _(j=j):
                action(j)

    def spread_block(buf, sends, recvs, at, b):
        for_near(lambda j: block_copy(buf, sends, recvs, at, b, j).start())

    def pass_copy(buf, sends, recvs, at, b, src, dst):
        return remote(
            buf.at[at, lanes(src, share)],
            buf.at[at, lanes(src, share)],
            sends.at[b, 0],
            recvs.at[b, src],
            {"mp": dst},
        )

    def pass_on(buf, sends, recvs, b, src, dst):
        copy = pass_copy(buf, sends, recvs, rows_at(b, TB, TB), b, src, dst)
        copy.wait_recv()
        copy.start()

    passers = ((mp - 2, 0, mp - 1), (1, mp - 1, 0))

    def pass_block(buf, sends, recvs, at, b):
        for rank, src, dst in passers:

            @pl.when(z == rank)
            def _(src=src, dst=dst):
                copy = pass_copy(buf, sends, recvs, at, b, src, dst)
                copy.wait_recv()
                copy.start()

    def passed(src):
        return ((z == mp - 2) & (src == 0)) | ((z == 1) & (src == mp - 1))

    def wait_block(buf, sends, recvs, at, b, src):
        @pl.when(jnp.logical_not(passed(src)))
        def _():
            remote(
                buf.at[at, mine], buf.at[at, lanes(src, share)], sends.at[b, 0], recvs.at[b, src], {"mp": src}
            ).wait_recv()

    def sent_block(buf, sends, recvs, at, b):
        for_near(lambda j: block_copy(buf, sends, recvs, at, b, j).wait_send())
        for rank, src, dst in passers:

            @pl.when(z == rank)
            def _(src=src, dst=dst):
                pass_copy(buf, sends, recvs, at, b, src, dst).wait_send()

    routes = {
        0: ((0, 0), (0, 1), (0, 2), (2, 0)),
        1: ((1, 0), (0, 0), (1, 2), (2, 2)),
        2: ((1, 1), (2, 1), (0, 0), (2, 3)),
        3: ((1, 3), (3, 1), (3, 2), (0, 0)),
    }
    adder = (2, 2, 1, 1)
    add_slot = (0, 2, 1, 3)

    def pick(table):
        value = 0
        for r in range(mp):
            value = value + jnp.where(z == r, table[r], 0)
        return value

    def route(f):
        return pick([routes[f][r][0] for r in range(mp)]), pick([routes[f][r][1] for r in range(mp)])

    sources = (pick((1, 0, 1, 1)), pick((2, 2, 3, 2)))

    place.greet()

    wcat[:, 0:share] = wq_ref[...]
    wcat[:, share : 2 * share] = wk_ref[...]
    wcat[:, 2 * share : 3 * share] = wv_ref[...]

    def project(b):
        at = rows_at(b, TB, TB)
        normal, _ = standardize(x_ref[at, :].astype(F32))
        normed = (normal * g1_ref[...] + b1_ref[...]).astype(BF16)
        a1[at, :] = normed
        out = dot(normed, wcat[...])
        lane = lax.broadcasted_iota(I32, (TB, 3 * share), 1)
        out = out * jnp.where(lane < share, 0.125, 1.0)
        keys[at, :] = out[:, share : 2 * share].astype(BF16)
        values[at, :] = out[:, 2 * share : 3 * share].astype(BF16)
        turned[:, at] = jnp.transpose(out).astype(BF16)
        flat = jnp.concatenate(
            [
                top_ref[:, at].astype(F32),
                jnp.zeros((1, TB), F32),
                val_ref[:, at].astype(F32),
                blk_ref[:, at].astype(F32),
                jnp.zeros((123, TB), F32),
            ],
            axis=0,
        )
        cols[at, :] = jnp.transpose(flat)

    loop(0, blocks, project)
    place.meet()

    piece = max(16, share // n)
    pieces = share // piece

    def own_piece(ref, s):
        return ref.at[rows_at(s * pieces + me, piece, 16), :]

    def out_weight_z(j):
        return remote(
            wo_ref.at[rows_at(me, piece, 16), :],
            own_piece(wof, z),
            s_o.at[j],
            r_o.at[z],
            {"mp": place.zahead(j)},
        )

    def out_weight_plane(s, k):
        return remote(
            own_piece(wof, s), own_piece(wof, s), s_o2.at[s, k], r_o2.at[s, k], place.plane(place.peer(k))
        )

    @pl.when(me < pieces)
    def _():
        for j in range(1, mp):
            out_weight_z(j).start()

    wof[rows_at(z, share, share), :] = wo_ref[...]

    head_row = lax.div(lax.broadcasted_iota(I32, (share, TB), 0), HEAD_DIM)
    head_lane = lax.div(lax.broadcasted_iota(I32, (TB, share), 1), HEAD_DIM)

    def only(value, where, h):
        return jnp.where(where == h, value, jnp.zeros_like(value))

    def attend(b):
        at = rows_at(b, TB, TB)
        mixed = []
        for h in range(heads):
            scores = dot(keys[...], only(turned[0:share, at], head_row, h))
            scores = jnp.where(cols[:, 4:5] <= blk_ref[:, at].astype(F32), scores, -1e30)
            peak = jnp.max(scores, axis=0, keepdims=True)
            raised = jnp.exp(scores - peak)
            total = jnp.sum(raised, axis=0, keepdims=True)
            low_probs = (raised * (1.0 / total)).astype(BF16)
            probs[h, :, at] = low_probs
            low = 2 * share + h * HEAD_DIM
            mixed.append(dot(turned[low : low + HEAD_DIM, :], low_probs))
        flat = jnp.concatenate(mixed, axis=0)
        mixt[:, at] = flat.astype(BF16)
        mixf[at, mine] = jnp.transpose(flat).astype(BF16)

        positions(b)
        spread_block(mixf, s_a, r_a, at, b)

    lane_t = lax.broadcasted_iota(I32, (TB, tokens), 1)
    sub_t = lax.broadcasted_iota(I32, (TB, tokens), 0)
    lane_k = lax.broadcasted_iota(I32, (TB, 128), 1)
    def positions(b):
        at = rows_at(b, TB, TB)
        hit = (sub_t + b * TB) == pri_ref[...]
        pos = jnp.sum(jnp.where(hit, lane_t.astype(F32), 0.0), axis=1, keepdims=True)
        cols[at, 2:3] = pos
        flat = jnp.transpose(jnp.broadcast_to(pos, (TB, 128)))
        sidr[2:3, at] = flat[0:1]


    loop(0, blocks, attend)

    @pl.when(me < pieces)
    def _():
        for j in range(1, mp):
            src = place.zahead(j)
            remote(
                wo_ref.at[rows_at(me, piece, 16), :], own_piece(wof, src), s_o.at[0], r_o.at[src], {"mp": src}
            ).wait_recv()
        for j in range(1, mp):
            src = place.zahead(j)
            loop(1, n, lambda k, src=src: out_weight_plane(src, k).start())

    def out_weight_wait():
        for j in range(1, mp):
            src = place.zahead(j)

            def wait(k, src=src):
                p = place.peer(k)

                @pl.when(p < pieces)
                def _():
                    at = rows_at(src * pieces + p, piece, 16)
                    remote(
                        wof.at[at, :], wof.at[at, :], s_o2.at[src, k], r_o2.at[src, k], place.plane(p)
                    ).wait_recv()

            each(n, wait)

    pass_block(mixf, s_a, r_a, rows_at(0, TB, TB), 0)

    lane_all = lax.broadcasted_iota(I32, (tokens, 128), 1)
    first = cols[:, 0:1].astype(I32)
    second = cols[:, 1:2].astype(I32)
    named = jnp.where(
        ((lane_all < experts) & (first == lane_all))
        | ((lane_all >= experts) & (second == lane_all - experts)),
        1.0,
        0.0,
    ).astype(BF16)
    total = jnp.sum(
        jnp.where(first == lane_all - experts, 1.0, 0.0), axis=0, keepdims=True
    )
    pos_row = sidr[2:3, :]

    def ranks(b):
        at = rows_at(b, TB, TB)
        earlier = jnp.where(pos_row < cols[at, 2:3], 1.0, 0.0).astype(BF16)
        count = dot(earlier, named)
        e0 = cols[at, 0:1].astype(I32)
        e1 = cols[at, 1:2].astype(I32)
        r0 = jnp.sum(jnp.where(lane_k == e0, count, 0.0), axis=1, keepdims=True)
        r1 = jnp.sum(jnp.where(lane_k == e1 + experts, count + total, 0.0), axis=1, keepdims=True)
        id0 = jnp.where(r0 < capacity, e0.astype(F32) * room + r0, -1.0)
        id1 = jnp.where(r1 < capacity, e1.astype(F32) * room + r1, -1.0)
        both = jnp.where(lane_k == 0, id0, jnp.where(lane_k == 1, id1, 0.0))
        cols[at, 7:8] = id0
        cols[at, 8:9] = id1
        flat = jnp.transpose(both)
        sidr[0:2, at] = flat[0:2]

    pass_block(mixf, s_a, r_a, rows_at(1, TB, TB), 1)
    loop(0, blocks, ranks)

    out_weight_wait()
    sub_e = lax.broadcasted_iota(I32, (experts, TB), 0)

    def second_norm(b):
        at = rows_at(b, TB, TB)
        for j in range(1, mp):
            src = place.zahead(j)
            wait_block(mixf, s_a, r_a, at, b, src)
        hidden = x_ref[at, :].astype(F32) + dot(mixf[at, :], wof[...])
        hid[at, :] = hidden
        normal, _ = standardize(hidden)
        normed = normal * g2_ref[...] + b2_ref[...]
        n2b[at, :] = normed.astype(BF16)
        logits = dot_nt(rt_ref[...], normed, HIGHEST)
        logits = jnp.exp(logits - jnp.max(logits, axis=0, keepdims=True))
        gates = logits / jnp.sum(logits, axis=0, keepdims=True)
        grow_t[0:experts, at] = gates
        for j in range(2):
            chosen = top_ref[j : j + 1, at]
            gate = jnp.sum(jnp.where(sub_e == chosen, gates, 0.0), axis=0, keepdims=True)
            gate = jnp.where(sidr[j : j + 1, at] >= 0.0, gate, 0.0)
            sidr[5 + j : 6 + j, at] = gate
            cols[at, 5 + j : 6 + j] = jnp.transpose(jnp.broadcast_to(gate, (128, TB)))[:, 0:1]

        @pl.when(b + 2 < blocks)
        def _():
            pass_block(mixf, s_a, r_a, rows_at(b + 2, TB, TB), b + 2)

    loop(0, blocks, second_norm)

    sub_c = lax.broadcasted_iota(I32, (room, tokens), 0).astype(F32)

    def fill(k):
        e = place.peer(k)
        base = (e * room).astype(F32)
        hit0 = sidr[0:1, :] == sub_c + base
        hit1 = sidr[1:2, :] == sub_c + base
        pick = jnp.where(hit0 | hit1, 1.0, 0.0).astype(BF16)
        disp[rows_at(e, room, unit), :] = jnp.where(
            hit0, sidr[5:6, :], jnp.where(hit1, sidr[6:7, :], 0.0)
        ).astype(BF16)
        return e, dot(pick, n2b[...]).astype(BF16)

    def dispatch_copy(k):
        e = place.peer(k)
        return remote(
            sbuf.at[rows_at(e, room, unit)],
            rows.at[rows_at(me, room, unit)],
            s_d.at[k],
            r_d.at[k],
            place.plane(e),
        )

    def dispatch(k):
        e, out = fill(k)
        sbuf[rows_at(e, room, unit), :] = out

        @pl.when(k >= 2)
        def _():
            dispatch_copy(k - 1).start()

    loop(1, n, dispatch)
    e, out = fill(n)
    rows[rows_at(e, room, unit), :] = out
    dispatch_copy(n - 1).start()

    def weigh(b):
        at = rows_at(b, TB, TB)
        slot = lax.broadcasted_iota(I32, (TB, slots), 1).astype(F32)
        comb[at, :] = jnp.where(
            cols[at, 7:8] == slot,
            cols[at, 5:6],
            jnp.where(cols[at, 8:9] == slot, cols[at, 6:7], 0.0),
        ).astype(BF16)

    loop(0, blocks, weigh)

    def arrived(buf, recv, send, src):
        remote(
            buf.at[rows_at(src, room, unit)],
            buf.at[rows_at(src, room, unit)],
            send,
            recv,
            place.plane(src),
        ).wait_recv()

    root = 0.7978845608028654
    cube = 0.044715

    def expert_in(k):
        s = place.peer(k)

        @pl.when(k > 0)
        def _():
            arrived(rows, r_d.at[k], s_d.at[k], s)

        at = rows_at(s, room, unit)
        inner = dot(rows[at, :], win_ref[...])
        square = inner * inner
        wave = jnp.tanh(root * inner * (1.0 + cube * square))
        half = 0.5 * (1.0 + wave)
        act[at, :] = (inner * half).astype(BF16)
        dgelu[at, :] = (
            half + 0.5 * inner * (1.0 - wave * wave) * (root * (1.0 + 3.0 * cube * square))
        ).astype(BF16)

    loop(0, n, expert_in)

    def return_copy(sends, recvs, into, i, f, k):
        s = place.peer(k)
        return remote(
            sbuf.at[rows_at(s, room, unit), lanes(f, share)],
            into.at[rows_at(me, room, unit), lanes(f, share)],
            sends.at[i, k],
            recvs.at[i, k],
            place.plane(s),
        )

    def give_back(i, f, value, sends, recvs, into):
        cut = lanes(f, share)
        sbuf[:, cut] = value.astype(BF16)
        at = rows_at(me, room, unit)
        into[at, cut] = sbuf[at, cut]
        each(n, lambda k: return_copy(sends, recvs, into, i, f, k).start())

    each(n, lambda k: dispatch_copy(k).wait_send())

    def wait_returns(sends, recvs):
        for i, f in enumerate(order):

            def wait(k, i=i, f=f):
                return_copy(sends, recvs, ret, i, f, k).wait_send()

            each(n, wait)

    for i, f in enumerate(order):
        give_back(
            i,
            f,
            dot(act[...], wout_ref[:, f * share : (f + 1) * share]),
            s_r,
            r_r,
            ret,
        )

    def gather_back(i, f, recvs, sends, into):
        def wait(k):
            src = place.peer(k)
            remote(
                sbuf.at[rows_at(src, room, unit), lanes(f, share)],
                into.at[rows_at(src, room, unit), lanes(f, share)],
                sends.at[i, k],
                recvs.at[i, k],
                place.plane(src),
            ).wait_recv()

        each(n, wait)

    def part_copy(sends, recvs, f, b):
        at = rows_at(b, TB, TB)
        dst, slot = route(f)
        return remote(
            pbuf.at[f, at, :], rbuf.at[slot, at, :], sends.at[f, b], recvs.at[slot, b], {"mp": dst}
        )

    def wait_slot(sends, recvs, slot, b):
        at = rows_at(b, TB, TB)
        remote(
            pbuf.at[0, at, :], rbuf.at[slot, at, :], sends.at[0, 0], recvs.at[slot, b], {"mp": z}
        ).wait_recv()

    def reduce_back(sends_r, recvs_r, sends, recvs, into):
        for i, f in enumerate(order):
            gather_back(i, f, recvs_r, sends_r, into)

            def combine(b, f=f):
                at = rows_at(b, TB, TB)
                part = dot(comb[at, :], into[:, f * share : (f + 1) * share])
                pbuf[f, at, :] = part.astype(BF16)

                @pl.when(z == f)
                def _():
                    own[at, :] = part

                @pl.when(z == adder[f])
                def _():
                    half[at, :] = part

                @pl.when((z != f) & (z != adder[f]) & (b >= 1))
                def _():
                    part_copy(sends, recvs, f, b - 1).start()

            loop(0, blocks, combine)

            @pl.when((z != f) & (z != adder[f]))
            def _(f=f):
                part_copy(sends, recvs, f, blocks - 1).start()

            @pl.when(z == adder[f])
            def _(f=f):
                def add(b):
                    at = rows_at(b, TB, TB)
                    wait_slot(sends, recvs, add_slot[f], b)
                    pbuf[f, at, :] = (half[at, :] + rbuf[add_slot[f], at, :].astype(F32)).astype(BF16)

                    @pl.when(b >= 1)
                    def _():
                        part_copy(sends, recvs, f, b - 1).start()

                loop(0, blocks, add)
                part_copy(sends, recvs, f, blocks - 1).start()

    def wait_sums(sends, recvs, b):
        for src in sources:
            wait_slot(sends, recvs, src, b)

    def wait_parts(sends, recvs):
        for f in range(mp):

            @pl.when(z != f)
            def _(f=f):
                loop(0, blocks, lambda b: part_copy(sends, recvs, f, b).wait_send())

    def summed(at):
        value = own[at, :]
        for src in sources:
            value = value + rbuf[src, at, :].astype(F32)
        return value

    reduce_back(s_r, r_r, s_p, r_p, ret)

    def finish(b, loss):
        at = rows_at(b, TB, TB)
        wait_sums(s_p, r_p, b)
        final = hid[at, mine] + summed(at)
        out_ref[at, :] = final.astype(BF16)
        residue = final - tea_ref[at, :].astype(F32)
        grad = cols[at, 3:4] * residue
        gf[at, mine] = grad.astype(BF16)

        @pl.when(b >= 1)
        def _():
            spread_block(gf, s_g, r_g, rows_at(b - 1, TB, TB), b - 1)

        return loss + 0.5 * jnp.sum(grad * residue)

    def finish_own():
        loss = lax.fori_loop(0, blocks, finish, jnp.float32(0.0))
        msg[experts : experts + 8, :] = jnp.full((8, tokens), loss, F32)
        spread_block(gf, s_g, r_g, rows_at(blocks - 1, TB, TB), blocks - 1)

    wait_returns(s_r, r_r)

    if mp == 4:
        turns = ((0, 1, 2, 3), (1, 0, 3, 2), (2, 3, 0, 1), (3, 2, 1, 0))
    else:
        turns = tuple(tuple((r + i) % mp for i in range(mp)) for r in range(mp))

    def turn_at(i):
        f = 0
        for r in range(mp):
            f = f + jnp.where(z == r, turns[r][i], 0)
        return f

    def grad_copy(i, f, k):
        e = place.peer(k)
        return remote(
            sbuf.at[rows_at(e, room, unit), lanes(f, share)],
            grows.at[rows_at(me, room, unit), lanes(f, share)],
            s_d2.at[i, k],
            r_d2.at[i, k],
            place.plane(e),
        )

    for i in range(mp):
        f = turn_at(i)
        if any(turns[r][i] == r for r in range(mp)):

            @pl.when(f == z)
            def _():
                finish_own()

        for rank, src, dst in passers:
            if i == (0 if rank == mp - 2 else 1):

                @pl.when(z == rank)
                def _(src=src, dst=dst):
                    loop(0, blocks, lambda b: pass_on(gf, s_g, r_g, b, src, dst))

        if any(turns[r][i] != r for r in range(mp)):
            @pl.when(f != z)
            def _(f=f):
                loop(0, blocks, lambda b: wait_block(gf, s_g, r_g, rows_at(b, TB, TB), b, f))

        cut = lanes(f, share)
        sbuf[:, cut] = dot(disp[...], gf[:, cut]).astype(BF16)
        at = rows_at(me, room, unit)
        grows[at, cut] = sbuf[at, cut]

        def grad_send(k, i=i, f=f):
            grad_copy(i, f, k).start()

        each(n, grad_send)

        def gather_inner(e, i=i, cut=cut):
            at = rows_at(e, room, unit)
            part = sbuf[at, cut].astype(F32) * ret[at, cut].astype(F32)
            inners[at, :] = part if i == 0 else inners[at, :] + part

        loop(0, n, gather_inner)

    def expert_back(k):
        s = place.peer(k)

        @pl.when(k > 0)
        def _():
            for i in range(mp):
                f = turn_at(i)
                remote(
                    grows.at[rows_at(s, room, unit), lanes(f, share)],
                    grows.at[rows_at(s, room, unit), lanes(f, share)],
                    s_d2.at[i, k],
                    r_d2.at[i, k],
                    place.plane(s),
                ).wait_recv()

        at = rows_at(s, room, unit)
        gi[at, :] = (dot_nt(grows[at, :], wout_ref[...]) * dgelu[at, :].astype(F32)).astype(BF16)

    loop(0, n, expert_back)

    def wait_grads():
        for i in range(mp):
            f = turn_at(i)

            def wait(k, i=i, f=f):
                grad_copy(i, f, k).wait_send()

            each(n, wait)

    wait_grads()

    for i, f in enumerate(order):
        give_back(
            i,
            f,
            dot_nt(gi[...], win_ref[f * share : (f + 1) * share, :]),
            s_r2,
            r_r2,
            ret2,
        )

    def gate_row(e):
        at = rows_at(e, room, unit)
        inner = jnp.sum(inners[at, :], axis=1, keepdims=True)
        msg[pl.ds(e, 1), :] = jnp.sum(
            jnp.where(disp[at, :].astype(F32) != 0.0, inner, 0.0), axis=0, keepdims=True
        )

    loop(0, experts, gate_row)
    rmsg[z] = msg[...]
    for j in range(1, mp):
        remote(msg, rmsg.at[z], s_m.at[j], r_m.at[z], {"mp": place.zahead(j)}).start()

    def weigh_back(b):
        at = rows_at(b, TB, TB)
        slot = lax.broadcasted_iota(I32, (TB, slots), 1).astype(F32)
        comb[at, :] = jnp.where(
            (cols[at, 7:8] == slot) | (cols[at, 8:9] == slot), 1.0, 0.0
        ).astype(BF16)

    loop(0, blocks, weigh_back)

    def weight_grads(b):
        at = lanes(b, 128)
        gwin_ref[at, :] = dot_tn(rows[:, at], gi[...])

    loop(0, width // 128, weight_grads)

    def weight_grads_out(b):
        at = lanes(b, 128)
        gwout_ref[at, :] = dot_tn(act[:, at], grows[...])

    loop(0, gwout_ref.shape[0] // 128, weight_grads_out)

    def store_grads():
        return (
            pltpu.make_async_copy(gwin_ref, gwin_hbm, s_h.at[0]),
            pltpu.make_async_copy(gwout_ref, gwout_hbm, s_h.at[1]),
        )


    loop(0, blocks, lambda b: sent_block(mixf, s_a, r_a, rows_at(b, TB, TB), b))
    wait_parts(s_p, r_p)
    reduce_back(s_r2, r_r2, s_p2, r_p2, ret2)

    ger = mixf
    for copy in store_grads():
        copy.start()

    def finish_back(b):
        at = rows_at(b, TB, TB)
        wait_sums(s_p2, r_p2, b)
        ger[at, mine] = summed(at).astype(BF16)

        @pl.when(b >= 1)
        def _():
            spread_block(ger, s_g2, r_g2, rows_at(b - 1, TB, TB), b - 1)

    loop(0, blocks, finish_back)
    spread_block(ger, s_g2, r_g2, rows_at(blocks - 1, TB, TB), blocks - 1)

    for j in range(1, mp):
        src = place.zahead(j)
        remote(msg, rmsg.at[src], s_m.at[0], r_m.at[src], {"mp": src}).wait_recv()
    grad_probs = rmsg[0]
    for j in range(1, mp):
        grad_probs = grad_probs + rmsg[j]
    loss_ref[...] = grad_probs[experts : experts + 8, 0:128] / (tokens * width)
    grad_probs = grad_probs[0:experts]
    gates = grow_t[0:experts, :]
    grow_t[0:experts, :] = grad_probs - gates * jnp.sum(grad_probs, axis=0, keepdims=True)
    vec_ref[...] = jnp.zeros_like(vec_ref)
    gk[...] = jnp.zeros_like(gk)
    gv[...] = jnp.zeros_like(gv)
    gwo_ref[...] = jnp.zeros_like(gwo_ref)

    def back(b):
        at = rows_at(b, TB, TB)
        @pl.when(b == 0)
        def _():
            pass_block(ger, s_g2, r_g2, rows_at(0, TB, TB), 0)

        for j in range(1, mp):
            wait_block(ger, s_g2, r_g2, at, b, place.zahead(j))
        normal, inverse = standardize(hid[at, :])
        normed = normal * g2_ref[...] + b2_ref[...]
        logits = grow_t[0:experts, at]
        vec_ref[8 : 8 + experts, :] += dot(logits, normed, HIGHEST)
        grad = dot_tn(logits, rt_ref[...], HIGHEST) + ger[at, :].astype(F32)
        vec_ref[2:3, :] += jnp.sum(grad * normal, axis=0, keepdims=True)
        vec_ref[3:4, :] += jnp.sum(grad, axis=0, keepdims=True)
        scaled = grad * g2_ref[...]
        out = gf[at, :].astype(F32) + inverse * (
            scaled
            - jnp.mean(scaled, axis=-1, keepdims=True)
            - normal * jnp.mean(scaled * normal, axis=-1, keepdims=True)
        )
        hid[at, :] = out
        attended = out.astype(BF16)

        @pl.when(b + 1 < blocks)
        def _():
            pass_block(ger, s_g2, r_g2, rows_at(b + 1, TB, TB), b + 1)

        gwo_ref[...] += dot(mixt[:, at], attended)
        mix_t = dot_nt(wo_ref[...], attended)
        mix_low = jnp.transpose(mix_t).astype(BF16)
        mix_t = mix_t.astype(BF16)
        query = jnp.transpose(turned[0:share, at].astype(F32)).astype(BF16)
        grad_query = []
        for h in range(heads):
            low_probs = probs[h, :, at]
            wide = low_probs.astype(F32)
            grad_probs = dot(values[...], only(mix_t, head_row, h))
            centre = jnp.sum(grad_probs * wide, axis=0, keepdims=True)
            grad_scores = (wide * (grad_probs - centre)).astype(BF16)
            low = share + h * HEAD_DIM
            grad_query.append(dot(turned[low : low + HEAD_DIM, :], grad_scores))
            gk[...] += dot(grad_scores, only(query, head_lane, h))
            gv[...] += dot(low_probs, only(mix_low, head_lane, h))
        flat = jnp.concatenate(grad_query, axis=0)
        gt[0:share, at] = flat.astype(BF16) * 0.125
        gflat[at, 0:share] = jnp.transpose(flat).astype(BF16) * 0.125

    loop(0, blocks, back)

    part = n2b

    def part_z(b, f):
        at = rows_at(b, TB, TB)
        dst, slot = route(f)
        return remote(
            part.at[at, lanes(f, share)], rbuf.at[slot, at, :], s_z.at[b, f], r_z.at[b, slot], {"mp": dst}
        )

    def wait_z(b, slot):
        at = rows_at(b, TB, TB)
        remote(
            part.at[at, mine], rbuf.at[slot, at, :], s_z.at[0, 0], r_z.at[b, slot], {"mp": z}
        ).wait_recv()

    far_first = (3, 0, 2, 1)

    def send_parts(b):
        for f in far_first:

            @pl.when((z != f) & (z != adder[f]))
            def _(f=f):
                part_z(b, f).start()

    def add_parts(b):
        at = rows_at(b, TB, TB)
        for f in far_first:

            @pl.when(z == adder[f])
            def _(f=f):
                wait_z(b, add_slot[f])
                cut = lanes(f, share)
                part[at, cut] = (
                    part[at, cut].astype(F32) + rbuf[add_slot[f], at, :].astype(F32)
                ).astype(BF16)

    def send_added(b):
        for f in far_first:

            @pl.when(z == adder[f])
            def _(f=f):
                part_z(b, f).start()

    vz[...] = jnp.zeros_like(vz)

    def first_back(b):
        at = rows_at(b, TB, TB)
        gflat[at, share : 2 * share] = gk[at, :].astype(BF16)
        gflat[at, 2 * share : 3 * share] = gv[at, :].astype(BF16)
        grad = dot_nt(gflat[at, :], wcat[...])
        part[at, :] = grad.astype(BF16)
        normal, _ = standardize(x_ref[at, :].astype(F32))
        scaled = grad * g1_ref[...]
        crossed = grad * normal
        lane = lax.broadcasted_iota(I32, (TB, 128), 1)
        sums = jnp.where(
            lane == 0,
            jnp.sum(scaled, axis=1, keepdims=True),
            jnp.where(lane == 1, jnp.sum(scaled * normal, axis=1, keepdims=True), 0.0),
        )
        small[:, at] = jnp.transpose(sums)[0:8]
        vz[0:1, :] += jnp.sum(crossed, axis=0, keepdims=True)
        vz[1:2, :] += jnp.sum(grad, axis=0, keepdims=True)

        @pl.when(b >= 1)
        def _():
            send_parts(b - 1)

    loop(0, blocks, first_back)

    def vz_copy(j):
        return remote(vz, rvz.at[z], s_v.at[j], r_v.at[z], {"mp": place.zahead(j)})

    def small_copy(j):
        return remote(small, rsmall.at[z], s_s.at[j], r_s.at[z], {"mp": place.zahead(j)})

    for j in range(1, mp):
        vz_copy(j).start()
    send_parts(blocks - 1)
    for j in range(1, mp):
        small_copy(j).start()
    rvz[z] = vz[...]
    rsmall[z] = small[...]

    def turn(b):
        at = rows_at(b, TB, TB)
        gt[share : 2 * share, at] = jnp.transpose(gk[at, :]).astype(BF16)
        gt[2 * share : 3 * share, at] = jnp.transpose(gv[at, :]).astype(BF16)

    loop(0, blocks, turn)
    wpk[0 : 3 * share, :] = dot(gt[...], a1[...]).astype(BF16)
    wpk[3 * share : 4 * share, :] = gwo_ref[...].astype(BF16)
    wrows = 4 * share // n

    def w_copy(k):
        p = place.peer(k)
        return remote(
            wpk.at[rows_at(p, wrows, 16)], rw.at[me], s_w.at[k], r_w.at[k], place.plane(p)
        )

    each(n, lambda k: w_copy(k).start())
    rw[me] = wpk[rows_at(me, wrows, 16), :]

    add_parts(0)
    add_parts(1)
    send_added(0)

    for j in range(1, mp):
        src = place.zahead(j)
        remote(vz, rvz.at[src], s_v.at[0], r_v.at[src], {"mp": src}).wait_recv()
    total_vz = rvz[0]
    for j in range(1, mp):
        total_vz = total_vz + rvz[j]
    vsend[...] = vec_ref[...].astype(BF16)
    vsend[0:2, :] = total_vz[0:2].astype(BF16)

    def v_copy(k):
        return remote(vsend, rvec.at[me], s_c.at[k], r_c.at[k], place.plane(place.peer(k)))

    rvec[me] = vsend[...]
    each(n, lambda k: v_copy(k).start())

    def w_wait(k):
        src = place.peer(k)
        remote(
            wpk.at[rows_at(0, wrows, 16)], rw.at[src], s_w.at[k], r_w.at[k], place.plane(src)
        ).wait_recv()

    each(n, w_wait)
    acc = rw[0].astype(F32)
    for p in range(1, n):
        acc = acc + rw[p].astype(F32)
    wall[rows_at(me, wrows, 16), :] = acc.astype(BF16)

    def e_copy(k):
        at = rows_at(me, wrows, 16)
        return remote(wall.at[at], wall.at[at], s_e.at[k], r_e.at[k], place.plane(place.peer(k)))

    each(n, lambda k: e_copy(k).start())
    send_added(1)
    add_parts(2)
    add_parts(3)
    send_added(2)

    def v_wait(k):
        src = place.peer(k)
        remote(vsend, rvec.at[src], s_c.at[k], r_c.at[k], place.plane(src)).wait_recv()

    each(n, v_wait)
    acc = rvec[0].astype(F32)
    for p in range(1, n):
        acc = acc + rvec[p].astype(F32)
    vec_ref[...] = acc
    send_added(3)

    def e_wait(k):
        src = place.peer(k)
        at = rows_at(src, wrows, 16)
        remote(wall.at[at], wall.at[at], s_e.at[k], r_e.at[k], place.plane(src)).wait_recv()

    each(n, e_wait)
    for j in range(1, mp):
        src = place.zahead(j)
        remote(small, rsmall.at[src], s_s.at[0], r_s.at[src], {"mp": src}).wait_recv()
    means = rsmall[0]
    for j in range(1, mp):
        means = means + rsmall[j]
    small_sum = means / width
    rsmall[z] = small_sum

    def last(b):
        at = rows_at(b, TB, TB)
        for src in sources:
            wait_z(b, src)
        inputs = x_ref[at, :].astype(F32)
        center = jnp.mean(inputs, axis=-1, keepdims=True)
        spread = inputs - center
        inverse = lax.rsqrt(jnp.mean(spread * spread, axis=-1, keepdims=True) + EPSILON)
        normal = (x_ref[at, mine].astype(F32) - center) * inverse
        grad = part[at, mine].astype(F32)
        for src in sources:
            grad = grad + rbuf[src, at, :].astype(F32)
        flat = jnp.concatenate([rsmall[z, :, at], jnp.zeros((120, TB), F32)], axis=0)
        columns = jnp.transpose(flat)
        gin_ref[at, :] = hid[at, mine] + inverse * (
            grad * g1_ref[:, mine] - columns[:, 0:1] - normal * columns[:, 1:2]
        )

    loop(0, blocks, last)

    for copy in store_grads():
        copy.wait()

    @pl.when(me < pieces)
    def _():
        for j in range(1, mp):
            out_weight_z(j).wait_send()
            src = place.zahead(j)
            loop(1, n, lambda k, src=src: out_weight_plane(src, k).wait_send())

    for j in range(1, mp):
        remote(msg, rmsg.at[z], s_m.at[j], r_m.at[z], {"mp": place.zahead(j)}).wait_send()
        vz_copy(j).wait_send()
        small_copy(j).wait_send()
    for f in range(mp):

        @pl.when(z != f)
        def _(f=f):
            loop(0, blocks, lambda b: part_z(b, f).wait_send())

    loop(0, blocks, lambda b: sent_block(gf, s_g, r_g, rows_at(b, TB, TB), b))
    loop(0, blocks, lambda b: sent_block(ger, s_g2, r_g2, rows_at(b, TB, TB), b))
    wait_returns(s_r2, r_r2)
    wait_parts(s_p2, r_p2)
    each(n, lambda k: w_copy(k).wait_send())
    each(n, lambda k: v_copy(k).wait_send())
    each(n, lambda k: e_copy(k).wait_send())


def layer(dims, capacity, experts, *args):
    x = args[0]
    dp, ex, mp = dims
    n = dp * ex
    tokens, width = x.shape
    share = width // mp
    hidden = args[-1].shape[0]
    room = -(-capacity // 16) * 16
    while (room * n) % 128:
        room += 16
    slots = n * room
    msgs = experts + 8
    blocks = tokens // TB
    heads = share // HEAD_DIM
    dma = pltpu.SemaphoreType.DMA
    vm = pltpu.VMEM
    scratch = [
        vm((width, hidden), F32),
        vm((hidden, width), F32),
        vm((share, width), F32),
        vm((tokens, width), BF16),
        vm((width, 3 * share), BF16),
        vm((tokens, share), BF16),
        vm((tokens, share), BF16),
        vm((3 * share, tokens), BF16),
        vm((share, tokens), BF16),
        vm((heads, tokens, tokens), BF16),
        vm((tokens, share), F32),
        vm((tokens, share), F32),
        vm((3 * share, tokens), BF16),
        vm((tokens, 3 * share), BF16),
        vm((4 * share, width), BF16),
        vm((n, 4 * share // n, width), BF16),
        vm((8, tokens), F32),
        vm((mp, 8, tokens), F32),
        vm((8, width), F32),
        vm((mp, 8, width), F32),
        vm((8 + experts, width), BF16),
        vm((n, 8 + experts, width), BF16),
        vm((tokens, width), BF16),
        vm((width, width), BF16),
        vm((tokens, width), F32),
        vm((tokens, width), BF16),
        vm((tokens, 128), F32),
        vm((8, tokens), F32),
        vm((experts, tokens), F32),
        vm((slots, tokens), BF16),
        vm((tokens, slots), BF16),
        vm((slots, width), BF16),
        vm((slots, width), BF16),
        vm((slots, hidden), BF16),
        vm((slots, hidden), BF16),
        vm((slots, width), BF16),
        vm((slots, width), BF16),
        vm((mp, tokens, share), BF16),
        vm((mp, tokens, share), BF16),
        vm((tokens, share), F32),
        vm((tokens, share), F32),
        vm((tokens, width), BF16),
        vm((slots, width), BF16),
        vm((slots, hidden), BF16),
        vm((msgs, tokens), F32),
        vm((mp, msgs, tokens), F32),
        vm((slots, share), F32),
        dma((blocks, mp)),
        dma((blocks, mp)),
        dma((n,)),
        dma((n,)),
        dma((mp, n)),
        dma((mp, n)),
        dma((mp, blocks)),
        dma((mp, blocks)),
        dma((blocks, mp)),
        dma((blocks, mp)),
        dma((mp, n)),
        dma((mp, n)),
        dma((mp, n)),
        dma((mp, n)),
        dma((mp, blocks)),
        dma((mp, blocks)),
        dma((blocks, mp)),
        dma((blocks, mp)),
        dma((mp,)),
        dma((mp,)),
        dma((mp,)),
        dma((mp,)),
        dma((mp, n)),
        dma((mp, n)),
        dma((blocks, mp)),
        dma((blocks, mp)),
        dma((mp,)),
        dma((mp,)),
        dma((mp,)),
        dma((mp,)),
        dma((n,)),
        dma((n,)),
        dma((n,)),
        dma((n,)),
        dma((n,)),
        dma((n,)),
        dma((2,)),
    ]
    shapes = (
        jax.ShapeDtypeStruct((tokens, share), BF16),
        jax.ShapeDtypeStruct((8, 128), F32),
        jax.ShapeDtypeStruct((tokens, share), F32),
        jax.ShapeDtypeStruct((4 * share, width), BF16),
        jax.ShapeDtypeStruct((8 + experts, width), F32),
        jax.ShapeDtypeStruct((width, hidden), F32),
        jax.ShapeDtypeStruct((hidden, width), F32),
    )
    spec = pl.BlockSpec(memory_space=pltpu.VMEM)
    return pl.pallas_call(
        functools.partial(layer_kernel, dims, capacity, experts),
        out_shape=shapes,
        in_specs=[spec] * len(args),
        out_specs=[spec] * 5 + [pl.BlockSpec(memory_space=pl.ANY)] * 2,
        scratch_shapes=scratch,
        compiler_params=pltpu.CompilerParams(
            collective_id=0, has_side_effects=True, vmem_limit_bytes=VMEM_LIMIT
        ),
        name="layer",
    )(*args)


def results_kernel(
    experts,
    share,
    out,
    loss,
    gin,
    wall,
    vec,
    gwin,
    gwout,
    out_o,
    loss_o,
    gin_o,
    gq_o,
    gk_o,
    gv_o,
    go_o,
    router_o,
    gwin_o,
    gwout_o,
    g1_o,
    b1_o,
    g2_o,
    b2_o,
):
    out_o[...] = out[...]
    gin_o[...] = gin[...]
    gwin_o[...] = gwin[...]
    gwout_o[...] = gwout[...]
    sums = wall[...].astype(F32)
    for i, ref in enumerate((gq_o, gk_o, gv_o)):
        ref[...] = jnp.transpose(sums[i * share : (i + 1) * share])
    go_o[...] = sums[3 * share : 4 * share]

    @pl.when(pl.program_id(0) == 0)
    def _():
        loss_o[...] = loss[0:1, :]
        router_o[...] = vec[8 : 8 + experts, :]
        for i, ref in enumerate((g1_o, b1_o, g2_o, b2_o)):
            ref[...] = vec[i]


def results(experts, steps, out, loss, gin, wall, vec, gwin, gwout):
    tokens, share = out.shape
    width = wall.shape[1]
    hidden = gwin.shape[1]

    def across(shape):
        return pl.BlockSpec((shape[0], shape[1] // steps), lambda i: (0, i))

    def down(shape):
        return pl.BlockSpec((shape[0] // steps, shape[1]), lambda i: (i, 0))

    def once(shape):
        return pl.BlockSpec(shape, lambda i: (0,) * len(shape))

    square = (width, share)
    shapes = (
        ((tokens, share), BF16, down),
        ((1, 128), F32, once),
        ((tokens, share), F32, down),
        (square, F32, down),
        (square, F32, down),
        (square, F32, down),
        ((share, width), F32, across),
        ((experts, width), F32, once),
        ((width, hidden), F32, down),
        ((hidden, width), F32, down),
        ((width,), F32, once),
        ((width,), F32, once),
        ((width,), F32, once),
        ((width,), F32, once),
    )
    return pl.pallas_call(
        functools.partial(results_kernel, experts, share),
        grid=(steps,),
        out_shape=[jax.ShapeDtypeStruct(shape, kind) for shape, kind, _ in shapes],
        in_specs=[
            down(out.shape),
            once(loss.shape),
            down(gin.shape),
            across(wall.shape),
            once(vec.shape),
            down(gwin.shape),
            down(gwout.shape),
        ],
        out_specs=[how(shape) for shape, _, how in shapes],
        name="results",
    )(out, loss, gin, wall, vec, gwin, gwout)


def per_device(
    dims,
    inputs,
    teacher,
    top_experts,
    priority,
    valid_mask,
    blocks,
    query_weight,
    key_weight,
    value_weight,
    out_weight,
    router,
    expert_in,
    expert_out,
    first_gain,
    first_bias,
    second_gain,
    second_bias,
):
    experts = router.shape[1]
    capacity = inputs.shape[0] * 2 * 21 // (20 * experts)
    kept = layer(
        dims,
        capacity,
        experts,
        inputs,
        blocks,
        query_weight,
        key_weight,
        value_weight,
        out_weight,
        first_gain[None],
        first_bias[None],
        second_gain[None],
        second_bias[None],
        router.T,
        top_experts.T,
        priority,
        valid_mask[None],
        teacher,
        expert_in[0],
        expert_out[0],
    )
    done = list(results(experts, 2, *kept))
    done[1] = done[1][0, 0:1]
    done[7] = done[7].T
    done[8] = done[8][None]
    done[9] = done[9][None]
    return tuple(done)


def solution(mesh):
    dims = (mesh.shape["dp"], mesh.shape["expert"], mesh.shape["mp"])
    both = ("dp", "expert")
    in_specs = (
        P(both, None),
        P(both, "mp"),
        P(both, None),
        P(both, None),
        P(both),
        P(both, None),
        P(None, "mp"),
        P(None, "mp"),
        P(None, "mp"),
        P("mp", None),
        P(),
        P(both, None, "mp"),
        P(both, "mp", None),
        P(),
        P(),
        P(),
        P(),
    )
    out_specs = (
        P(both, "mp"),
        P(both),
        P(both, "mp"),
        P(None, "mp"),
        P(None, "mp"),
        P(None, "mp"),
        P("mp", None),
        P(),
        P(both, None, "mp"),
        P(both, "mp", None),
        P(),
        P(),
        P(),
        P(),
    )
    return jax.shard_map(
        functools.partial(per_device, dims),
        mesh=mesh,
        in_specs=in_specs,
        out_specs=out_specs,
        check_vma=False,
    )
```

```python
import functools

import jax
import jax.numpy as jnp
from jax import lax
from jax.experimental import pallas as pl
from jax.experimental.pallas import tpu as pltpu
from jax.sharding import PartitionSpec as P

HEAD_DIM = 64
EPSILON = 1e-06
HIGHEST = lax.Precision.HIGHEST
MESH = pl.DeviceIdType.MESH
F32 = jnp.float32
BF16 = jnp.bfloat16
I32 = jnp.int32
VMEM_LIMIT = 67043328


def standardize(values):
    center = values - jnp.mean(values, axis=-1, keepdims=True)
    inverse = lax.rsqrt(jnp.mean(center * center, axis=-1, keepdims=True) + EPSILON)
    return (center * inverse, inverse)


def dot(a, b, precision=None):
    return jnp.dot(a, b, preferred_element_type=F32, precision=precision)


def dot_nt(a, b, precision=None):
    return lax.dot_general(
        a, b, (((1,), (1,)), ((), ())), preferred_element_type=F32, precision=precision
    )


def dot_tn(a, b, precision=None):
    return lax.dot_general(
        a, b, (((0,), (0,)), ((), ())), preferred_element_type=F32, precision=precision
    )


def remote(src, dst, send, recv, device):
    return pltpu.make_async_remote_copy(
        src_ref=src, dst_ref=dst, send_sem=send, recv_sem=recv, device_id=device, device_id_type=MESH
    )


def lanes(f, width):
    return pl.ds(pl.multiple_of(f * width, width), width)


def rows_at(s, count, unit):
    return pl.ds(pl.multiple_of(s * count, unit), count)


def loop(low, high, body):
    def step(i, carry):
        body(i)
        return carry

    lax.fori_loop(low, high, step, 0)


def peer_order(n):
    masks = sorted(range(1, n), key=lambda m: (-bin(m // 2).count("1"), m))
    return [0] + masks


def each(n, body):
    if n <= 8:
        for k in range(1, n):
            body(k)
    else:
        loop(1, n, body)


class Place:
    def __init__(self, dims):
        self.dp, self.ex, self.mp = dims
        self.n = self.dp * self.ex
        self.me = lax.axis_index("dp") * self.ex + lax.axis_index("expert")
        self.z = lax.axis_index("mp")
        self.order = peer_order(self.n)
        self.fixed = [self.flip(mask) for mask in self.order] if self.n <= 8 else None

    def flip(self, mask):
        out = 0
        bit = 1
        while bit < self.n:
            mine = lax.rem(lax.div(self.me, bit), 2)
            out = out + bit * (1 - mine if mask & bit else mine)
            bit *= 2
        return out

    def peer(self, k):
        if isinstance(k, int) and self.fixed:
            return self.fixed[k % self.n]
        mask = 0
        for i in range(1, self.n):
            mask = mask + jnp.where(k == i, self.order[i], 0)
        out = 0
        bit = 1
        while bit < self.n:
            out = out + bit * lax.rem(lax.div(self.me, bit) + lax.div(mask, bit), 2)
            bit *= 2
        return out

    def plane(self, p):
        return {"dp": lax.div(p, self.ex), "expert": lax.rem(p, self.ex)}

    def zahead(self, j):
        return lax.rem(self.z + j, self.mp)

    def greet(self):
        sem = pltpu.get_barrier_semaphore()

        def hello(k):
            pl.semaphore_signal(
                sem, inc=1, device_id=self.plane(self.peer(k)), device_id_type=MESH
            )

        each(self.n, hello)
        for j in range(1, self.mp):
            pl.semaphore_signal(
                sem, inc=1, device_id={"mp": self.zahead(j)}, device_id_type=MESH
            )

    def meet(self):
        pl.semaphore_wait(pltpu.get_barrier_semaphore(), self.n - 1 + self.mp - 1)


def feature_order(mp):
    return [i // 2 if i % 2 == 0 else mp - 1 - i // 2 for i in range(mp)]


TB = 256


def layer_kernel(
    dims,
    capacity,
    experts,
    x_ref,
    blk_ref,
    wq_ref,
    wk_ref,
    wv_ref,
    wo_ref,
    g1_ref,
    b1_ref,
    g2_ref,
    b2_ref,
    rt_ref,
    top_ref,
    pri_ref,
    val_ref,
    tea_ref,
    win_ref,
    wout_ref,
    out_ref,
    loss_ref,
    gin_ref,
    wall,
    vec_ref,
    gwin_hbm,
    gwout_hbm,
    gwin_ref,
    gwout_ref,
    gwo_ref,
    a1,
    wcat,
    keys,
    values,
    turned,
    mixt,
    probs,
    gk,
    gv,
    gt,
    gflat,
    wpk,
    rw,
    small,
    rsmall,
    vz,
    rvz,
    vsend,
    rvec,
    mixf,
    wof,
    hid,
    n2b,
    cols,
    sidr,
    grow_t,
    disp,
    comb,
    sbuf,
    rows,
    dgelu,
    act,
    ret,
    ret2,
    pbuf,
    rbuf,
    own,
    half,
    gf,
    grows,
    gi,
    msg,
    rmsg,
    inners,
    s_a,
    r_a,
    s_d,
    r_d,
    s_r,
    r_r,
    s_p,
    r_p,
    s_g,
    r_g,
    s_d2,
    r_d2,
    s_r2,
    r_r2,
    s_p2,
    r_p2,
    s_g2,
    r_g2,
    s_m,
    r_m,
    s_o,
    r_o,
    s_o2,
    r_o2,
    s_z,
    r_z,
    s_s,
    r_s,
    s_v,
    r_v,
    s_w,
    r_w,
    s_c,
    r_c,
    s_e,
    r_e,
    s_h,
):
    place = Place(dims)
    n, mp, me, z = place.n, place.mp, place.me, place.z
    tokens, width = x_ref.shape
    share = width // mp
    heads = share // HEAD_DIM
    blocks = tokens // TB
    slots = ret.shape[0]
    room = slots // n
    unit = 16
    order = feature_order(mp)
    mine = lanes(z, share)

    def near(dst):
        return jnp.abs(dst - z) < mp - 1

    def block_copy(buf, sends, recvs, at, b, j):
        return remote(
            buf.at[at, mine], buf.at[at, mine], sends.at[b, j], recvs.at[b, z], {"mp": place.zahead(j)}
        )

    def for_near(action):
        for j in (1, 3, 2) if mp == 4 else range(1, mp):

            @pl.when(near(place.zahead(j)))
            def _(j=j):
                action(j)

    def spread_block(buf, sends, recvs, at, b):
        for_near(lambda j: block_copy(buf, sends, recvs, at, b, j).start())

    def pass_copy(buf, sends, recvs, at, b, src, dst):
        return remote(
            buf.at[at, lanes(src, share)],
            buf.at[at, lanes(src, share)],
            sends.at[b, 0],
            recvs.at[b, src],
            {"mp": dst},
        )

    def pass_on(buf, sends, recvs, b, src, dst):
        copy = pass_copy(buf, sends, recvs, rows_at(b, TB, TB), b, src, dst)
        copy.wait_recv()
        copy.start()

    passers = ((mp - 2, 0, mp - 1), (1, mp - 1, 0))

    def pass_block(buf, sends, recvs, at, b):
        for rank, src, dst in passers:

            @pl.when(z == rank)
            def _(src=src, dst=dst):
                copy = pass_copy(buf, sends, recvs, at, b, src, dst)
                copy.wait_recv()
                copy.start()

    def passed(src):
        return ((z == mp - 2) & (src == 0)) | ((z == 1) & (src == mp - 1))

    def wait_block(buf, sends, recvs, at, b, src):
        @pl.when(jnp.logical_not(passed(src)))
        def _():
            remote(
                buf.at[at, mine], buf.at[at, lanes(src, share)], sends.at[b, 0], recvs.at[b, src], {"mp": src}
            ).wait_recv()

    def sent_block(buf, sends, recvs, at, b):
        for_near(lambda j: block_copy(buf, sends, recvs, at, b, j).wait_send())
        for rank, src, dst in passers:

            @pl.when(z == rank)
            def _(src=src, dst=dst):
                pass_copy(buf, sends, recvs, at, b, src, dst).wait_send()

    routes = {
        0: ((0, 0), (0, 1), (0, 2), (2, 0)),
        1: ((1, 0), (0, 0), (1, 2), (2, 2)),
        2: ((1, 1), (2, 1), (0, 0), (2, 3)),
        3: ((1, 3), (3, 1), (3, 2), (0, 0)),
    }
    adder = (2, 2, 1, 1)
    add_slot = (0, 2, 1, 3)

    def pick(table):
        value = 0
        for r in range(mp):
            value = value + jnp.where(z == r, table[r], 0)
        return value

    def route(f):
        return pick([routes[f][r][0] for r in range(mp)]), pick([routes[f][r][1] for r in range(mp)])

    sources = (pick((1, 0, 1, 1)), pick((2, 2, 3, 2)))

    place.greet()

    wcat[:, 0:share] = wq_ref[...]
    wcat[:, share : 2 * share] = wk_ref[...]
    wcat[:, 2 * share : 3 * share] = wv_ref[...]

    def project(b):
        at = rows_at(b, TB, TB)
        normal, _ = standardize(x_ref[at, :].astype(F32))
        normed = (normal * g1_ref[...] + b1_ref[...]).astype(BF16)
        a1[at, :] = normed
        out = dot(normed, wcat[...])
        lane = lax.broadcasted_iota(I32, (TB, 3 * share), 1)
        out = out * jnp.where(lane < share, 0.125, 1.0)
        keys[at, :] = out[:, share : 2 * share].astype(BF16)
        values[at, :] = out[:, 2 * share : 3 * share].astype(BF16)
        turned[:, at] = jnp.transpose(out).astype(BF16)
        flat = jnp.concatenate(
            [
                top_ref[:, at].astype(F32),
                jnp.zeros((1, TB), F32),
                val_ref[:, at].astype(F32),
                blk_ref[:, at].astype(F32),
                jnp.zeros((123, TB), F32),
            ],
            axis=0,
        )
        cols[at, :] = jnp.transpose(flat)

    loop(0, blocks, project)
    place.meet()

    piece = max(16, share // n)
    pieces = share // piece

    def own_piece(ref, s):
        return ref.at[rows_at(s * pieces + me, piece, 16), :]

    def out_weight_z(j):
        return remote(
            wo_ref.at[rows_at(me, piece, 16), :],
            own_piece(wof, z),
            s_o.at[j],
            r_o.at[z],
            {"mp": place.zahead(j)},
        )

    def out_weight_plane(s, k):
        return remote(
            own_piece(wof, s), own_piece(wof, s), s_o2.at[s, k], r_o2.at[s, k], place.plane(place.peer(k))
        )

    @pl.when(me < pieces)
    def _():
        for j in range(1, mp):
            out_weight_z(j).start()

    wof[rows_at(z, share, share), :] = wo_ref[...]

    head_row = lax.div(lax.broadcasted_iota(I32, (share, TB), 0), HEAD_DIM)
    head_lane = lax.div(lax.broadcasted_iota(I32, (TB, share), 1), HEAD_DIM)

    def only(value, where, h):
        return jnp.where(where == h, value, jnp.zeros_like(value))

    def attend(b):
        at = rows_at(b, TB, TB)
        mixed = []
        for h in range(heads):
            scores = dot(keys[...], only(turned[0:share, at], head_row, h))
            scores = jnp.where(cols[:, 4:5] <= blk_ref[:, at].astype(F32), scores, -1e30)
            peak = jnp.max(scores, axis=0, keepdims=True)
            raised = jnp.exp(scores - peak)
            total = jnp.sum(raised, axis=0, keepdims=True)
            low_probs = (raised * (1.0 / total)).astype(BF16)
            probs[h, :, at] = low_probs
            low = 2 * share + h * HEAD_DIM
            mixed.append(dot(turned[low : low + HEAD_DIM, :], low_probs))
        flat = jnp.concatenate(mixed, axis=0)
        mixt[:, at] = flat.astype(BF16)
        mixf[at, mine] = jnp.transpose(flat).astype(BF16)

        positions(b)
        spread_block(mixf, s_a, r_a, at, b)

    lane_t = lax.broadcasted_iota(I32, (TB, tokens), 1)
    sub_t = lax.broadcasted_iota(I32, (TB, tokens), 0)
    lane_k = lax.broadcasted_iota(I32, (TB, 128), 1)
    def positions(b):
        at = rows_at(b, TB, TB)
        hit = (sub_t + b * TB) == pri_ref[...]
        pos = jnp.sum(jnp.where(hit, lane_t.astype(F32), 0.0), axis=1, keepdims=True)
        cols[at, 2:3] = pos
        flat = jnp.transpose(jnp.broadcast_to(pos, (TB, 128)))
        sidr[2:3, at] = flat[0:1]


    loop(0, blocks, attend)

    @pl.when(me < pieces)
    def _():
        for j in range(1, mp):
            src = place.zahead(j)
            remote(
                wo_ref.at[rows_at(me, piece, 16), :], own_piece(wof, src), s_o.at[0], r_o.at[src], {"mp": src}
            ).wait_recv()
        for j in range(1, mp):
            src = place.zahead(j)
            loop(1, n, lambda k, src=src: out_weight_plane(src, k).start())

    def out_weight_wait():
        for j in range(1, mp):
            src = place.zahead(j)

            def wait(k, src=src):
                p = place.peer(k)

                @pl.when(p < pieces)
                def _():
                    at = rows_at(src * pieces + p, piece, 16)
                    remote(
                        wof.at[at, :], wof.at[at, :], s_o2.at[src, k], r_o2.at[src, k], place.plane(p)
                    ).wait_recv()

            each(n, wait)

    pass_block(mixf, s_a, r_a, rows_at(0, TB, TB), 0)

    lane_all = lax.broadcasted_iota(I32, (tokens, 128), 1)
    first = cols[:, 0:1].astype(I32)
    second = cols[:, 1:2].astype(I32)
    named = jnp.where(
        ((lane_all < experts) & (first == lane_all))
        | ((lane_all >= experts) & (second == lane_all - experts)),
        1.0,
        0.0,
    ).astype(BF16)
    total = jnp.sum(
        jnp.where(first == lane_all - experts, 1.0, 0.0), axis=0, keepdims=True
    )
    pos_row = sidr[2:3, :]

    def ranks(b):
        at = rows_at(b, TB, TB)
        earlier = jnp.where(pos_row < cols[at, 2:3], 1.0, 0.0).astype(BF16)
        count = dot(earlier, named)
        e0 = cols[at, 0:1].astype(I32)
        e1 = cols[at, 1:2].astype(I32)
        r0 = jnp.sum(jnp.where(lane_k == e0, count, 0.0), axis=1, keepdims=True)
        r1 = jnp.sum(jnp.where(lane_k == e1 + experts, count + total, 0.0), axis=1, keepdims=True)
        id0 = jnp.where(r0 < capacity, e0.astype(F32) * room + r0, -1.0)
        id1 = jnp.where(r1 < capacity, e1.astype(F32) * room + r1, -1.0)
        both = jnp.where(lane_k == 0, id0, jnp.where(lane_k == 1, id1, 0.0))
        cols[at, 7:8] = id0
        cols[at, 8:9] = id1
        flat = jnp.transpose(both)
        sidr[0:2, at] = flat[0:2]

    pass_block(mixf, s_a, r_a, rows_at(1, TB, TB), 1)
    loop(0, blocks, ranks)

    out_weight_wait()
    sub_e = lax.broadcasted_iota(I32, (experts, TB), 0)

    def second_norm(b):
        at = rows_at(b, TB, TB)
        for j in range(1, mp):
            src = place.zahead(j)
            wait_block(mixf, s_a, r_a, at, b, src)
        hidden = x_ref[at, :].astype(F32) + dot(mixf[at, :], wof[...])
        hid[at, :] = hidden
        normal, _ = standardize(hidden)
        normed = normal * g2_ref[...] + b2_ref[...]
        n2b[at, :] = normed.astype(BF16)
        logits = dot_nt(rt_ref[...], normed, HIGHEST)
        logits = jnp.exp(logits - jnp.max(logits, axis=0, keepdims=True))
        gates = logits / jnp.sum(logits, axis=0, keepdims=True)
        grow_t[0:experts, at] = gates
        for j in range(2):
            chosen = top_ref[j : j + 1, at]
            gate = jnp.sum(jnp.where(sub_e == chosen, gates, 0.0), axis=0, keepdims=True)
            gate = jnp.where(sidr[j : j + 1, at] >= 0.0, gate, 0.0)
            sidr[5 + j : 6 + j, at] = gate
            cols[at, 5 + j : 6 + j] = jnp.transpose(jnp.broadcast_to(gate, (128, TB)))[:, 0:1]

        @pl.when(b + 2 < blocks)
        def _():
            pass_block(mixf, s_a, r_a, rows_at(b + 2, TB, TB), b + 2)

    loop(0, blocks, second_norm)

    sub_c = lax.broadcasted_iota(I32, (room, tokens), 0).astype(F32)

    def fill(k):
        e = place.peer(k)
        base = (e * room).astype(F32)
        hit0 = sidr[0:1, :] == sub_c + base
        hit1 = sidr[1:2, :] == sub_c + base
        pick = jnp.where(hit0 | hit1, 1.0, 0.0).astype(BF16)
        disp[rows_at(e, room, unit), :] = jnp.where(
            hit0, sidr[5:6, :], jnp.where(hit1, sidr[6:7, :], 0.0)
        ).astype(BF16)
        return e, dot(pick, n2b[...]).astype(BF16)

    def dispatch_copy(k):
        e = place.peer(k)
        return remote(
            sbuf.at[rows_at(e, room, unit)],
            rows.at[rows_at(me, room, unit)],
            s_d.at[k],
            r_d.at[k],
            place.plane(e),
        )

    def dispatch(k):
        e, out = fill(k)
        sbuf[rows_at(e, room, unit), :] = out

        @pl.when(k >= 2)
        def _():
            dispatch_copy(k - 1).start()

    loop(1, n, dispatch)
    e, out = fill(n)
    rows[rows_at(e, room, unit), :] = out
    dispatch_copy(n - 1).start()

    def weigh(b):
        at = rows_at(b, TB, TB)
        slot = lax.broadcasted_iota(I32, (TB, slots), 1).astype(F32)
        comb[at, :] = jnp.where(
            cols[at, 7:8] == slot,
            cols[at, 5:6],
            jnp.where(cols[at, 8:9] == slot, cols[at, 6:7], 0.0),
        ).astype(BF16)

    loop(0, blocks, weigh)

    def arrived(buf, recv, send, src):
        remote(
            buf.at[rows_at(src, room, unit)],
            buf.at[rows_at(src, room, unit)],
            send,
            recv,
            place.plane(src),
        ).wait_recv()

    root = 0.7978845608028654
    cube = 0.044715

    def expert_in(k):
        s = place.peer(k)

        @pl.when(k > 0)
        def _():
            arrived(rows, r_d.at[k], s_d.at[k], s)

        at = rows_at(s, room, unit)
        inner = dot(rows[at, :], win_ref[...])
        square = inner * inner
        wave = jnp.tanh(root * inner * (1.0 + cube * square))
        half = 0.5 * (1.0 + wave)
        act[at, :] = (inner * half).astype(BF16)
        dgelu[at, :] = (
            half + 0.5 * inner * (1.0 - wave * wave) * (root * (1.0 + 3.0 * cube * square))
        ).astype(BF16)

    loop(0, n, expert_in)

    def return_copy(sends, recvs, into, i, f, k):
        s = place.peer(k)
        return remote(
            sbuf.at[rows_at(s, room, unit), lanes(f, share)],
            into.at[rows_at(me, room, unit), lanes(f, share)],
            sends.at[i, k],
            recvs.at[i, k],
            place.plane(s),
        )

    def give_back(i, f, value, sends, recvs, into):
        cut = lanes(f, share)
        sbuf[:, cut] = value.astype(BF16)
        at = rows_at(me, room, unit)
        into[at, cut] = sbuf[at, cut]
        each(n, lambda k: return_copy(sends, recvs, into, i, f, k).start())

    each(n, lambda k: dispatch_copy(k).wait_send())

    def wait_returns(sends, recvs):
        for i, f in enumerate(order):

            def wait(k, i=i, f=f):
                return_copy(sends, recvs, ret, i, f, k).wait_send()

            each(n, wait)

    for i, f in enumerate(order):
        give_back(
            i,
            f,
            dot(act[...], wout_ref[:, f * share : (f + 1) * share]),
            s_r,
            r_r,
            ret,
        )

    def gather_back(i, f, recvs, sends, into):
        def wait(k):
            src = place.peer(k)
            remote(
                sbuf.at[rows_at(src, room, unit), lanes(f, share)],
                into.at[rows_at(src, room, unit), lanes(f, share)],
                sends.at[i, k],
                recvs.at[i, k],
                place.plane(src),
            ).wait_recv()

        each(n, wait)

    def part_copy(sends, recvs, f, b):
        at = rows_at(b, TB, TB)
        dst, slot = route(f)
        return remote(
            pbuf.at[f, at, :], rbuf.at[slot, at, :], sends.at[f, b], recvs.at[slot, b], {"mp": dst}
        )

    def wait_slot(sends, recvs, slot, b):
        at = rows_at(b, TB, TB)
        remote(
            pbuf.at[0, at, :], rbuf.at[slot, at, :], sends.at[0, 0], recvs.at[slot, b], {"mp": z}
        ).wait_recv()

    def reduce_back(sends_r, recvs_r, sends, recvs, into):
        for i, f in enumerate(order):
            gather_back(i, f, recvs_r, sends_r, into)

            def combine(b, f=f):
                at = rows_at(b, TB, TB)
                part = dot(comb[at, :], into[:, f * share : (f + 1) * share])
                pbuf[f, at, :] = part.astype(BF16)

                @pl.when(z == f)
                def _():
                    own[at, :] = part

                @pl.when(z == adder[f])
                def _():
                    half[at, :] = part

                @pl.when((z != f) & (z != adder[f]) & (b >= 1))
                def _():
                    part_copy(sends, recvs, f, b - 1).start()

            loop(0, blocks, combine)

            @pl.when((z != f) & (z != adder[f]))
            def _(f=f):
                part_copy(sends, recvs, f, blocks - 1).start()

            @pl.when(z == adder[f])
            def _(f=f):
                def add(b):
                    at = rows_at(b, TB, TB)
                    wait_slot(sends, recvs, add_slot[f], b)
                    pbuf[f, at, :] = (half[at, :] + rbuf[add_slot[f], at, :].astype(F32)).astype(BF16)

                    @pl.when(b >= 1)
                    def _():
                        part_copy(sends, recvs, f, b - 1).start()

                loop(0, blocks, add)
                part_copy(sends, recvs, f, blocks - 1).start()

    def wait_sums(sends, recvs, b):
        for src in sources:
            wait_slot(sends, recvs, src, b)

    def wait_parts(sends, recvs):
        for f in range(mp):

            @pl.when(z != f)
            def _(f=f):
                loop(0, blocks, lambda b: part_copy(sends, recvs, f, b).wait_send())

    def summed(at):
        value = own[at, :]
        for src in sources:
            value = value + rbuf[src, at, :].astype(F32)
        return value

    reduce_back(s_r, r_r, s_p, r_p, ret)

    def finish(b, loss):
        at = rows_at(b, TB, TB)
        wait_sums(s_p, r_p, b)
        final = hid[at, mine] + summed(at)
        out_ref[at, :] = final.astype(BF16)
        residue = final - tea_ref[at, :].astype(F32)
        grad = cols[at, 3:4] * residue
        gf[at, mine] = grad.astype(BF16)

        @pl.when(b >= 1)
        def _():
            spread_block(gf, s_g, r_g, rows_at(b - 1, TB, TB), b - 1)

        return loss + 0.5 * jnp.sum(grad * residue)

    def finish_own():
        loss = lax.fori_loop(0, blocks, finish, jnp.float32(0.0))
        msg[experts : experts + 8, :] = jnp.full((8, tokens), loss, F32)
        spread_block(gf, s_g, r_g, rows_at(blocks - 1, TB, TB), blocks - 1)

    wait_returns(s_r, r_r)

    if mp == 4:
        turns = ((0, 1, 2, 3), (1, 0, 3, 2), (2, 3, 0, 1), (3, 2, 1, 0))
    else:
        turns = tuple(tuple((r + i) % mp for i in range(mp)) for r in range(mp))

    def turn_at(i):
        f = 0
        for r in range(mp):
            f = f + jnp.where(z == r, turns[r][i], 0)
        return f

    def grad_copy(i, f, k):
        e = place.peer(k)
        return remote(
            sbuf.at[rows_at(e, room, unit), lanes(f, share)],
            grows.at[rows_at(me, room, unit), lanes(f, share)],
            s_d2.at[i, k],
            r_d2.at[i, k],
            place.plane(e),
        )

    for i in range(mp):
        f = turn_at(i)
        if any(turns[r][i] == r for r in range(mp)):

            @pl.when(f == z)
            def _():
                finish_own()

        for rank, src, dst in passers:
            if i == (0 if rank == mp - 2 else 1):

                @pl.when(z == rank)
                def _(src=src, dst=dst):
                    loop(0, blocks, lambda b: pass_on(gf, s_g, r_g, b, src, dst))

        if any(turns[r][i] != r for r in range(mp)):
            @pl.when(f != z)
            def _(f=f):
                loop(0, blocks, lambda b: wait_block(gf, s_g, r_g, rows_at(b, TB, TB), b, f))

        cut = lanes(f, share)
        sbuf[:, cut] = dot(disp[...], gf[:, cut]).astype(BF16)
        at = rows_at(me, room, unit)
        grows[at, cut] = sbuf[at, cut]

        def grad_send(k, i=i, f=f):
            grad_copy(i, f, k).start()

        each(n, grad_send)

        def gather_inner(e, i=i, cut=cut):
            at = rows_at(e, room, unit)
            part = sbuf[at, cut].astype(F32) * ret[at, cut].astype(F32)
            inners[at, :] = part if i == 0 else inners[at, :] + part

        loop(0, n, gather_inner)

    def expert_back(k):
        s = place.peer(k)

        @pl.when(k > 0)
        def _():
            for i in range(mp):
                f = turn_at(i)
                remote(
                    grows.at[rows_at(s, room, unit), lanes(f, share)],
                    grows.at[rows_at(s, room, unit), lanes(f, share)],
                    s_d2.at[i, k],
                    r_d2.at[i, k],
                    place.plane(s),
                ).wait_recv()

        at = rows_at(s, room, unit)
        gi[at, :] = (dot_nt(grows[at, :], wout_ref[...]) * dgelu[at, :].astype(F32)).astype(BF16)

    loop(0, n, expert_back)

    def wait_grads():
        for i in range(mp):
            f = turn_at(i)

            def wait(k, i=i, f=f):
                grad_copy(i, f, k).wait_send()

            each(n, wait)

    wait_grads()

    for i, f in enumerate(order):
        give_back(
            i,
            f,
            dot_nt(gi[...], win_ref[f * share : (f + 1) * share, :]),
            s_r2,
            r_r2,
            ret2,
        )

    def gate_row(e):
        at = rows_at(e, room, unit)
        inner = jnp.sum(inners[at, :], axis=1, keepdims=True)
        msg[pl.ds(e, 1), :] = jnp.sum(
            jnp.where(disp[at, :].astype(F32) != 0.0, inner, 0.0), axis=0, keepdims=True
        )

    loop(0, experts, gate_row)
    rmsg[z] = msg[...]
    for j in range(1, mp):
        remote(msg, rmsg.at[z], s_m.at[j], r_m.at[z], {"mp": place.zahead(j)}).start()

    def weigh_back(b):
        at = rows_at(b, TB, TB)
        slot = lax.broadcasted_iota(I32, (TB, slots), 1).astype(F32)
        comb[at, :] = jnp.where(
            (cols[at, 7:8] == slot) | (cols[at, 8:9] == slot), 1.0, 0.0
        ).astype(BF16)

    loop(0, blocks, weigh_back)

    def weight_grads(b):
        at = lanes(b, 128)
        gwin_ref[at, :] = dot_tn(rows[:, at], gi[...])

    loop(0, width // 128, weight_grads)

    def weight_grads_out(b):
        at = lanes(b, 128)
        gwout_ref[at, :] = dot_tn(act[:, at], grows[...])

    loop(0, gwout_ref.shape[0] // 128, weight_grads_out)

    def store_grads():
        return (
            pltpu.make_async_copy(gwin_ref, gwin_hbm, s_h.at[0]),
            pltpu.make_async_copy(gwout_ref, gwout_hbm, s_h.at[1]),
        )


    loop(0, blocks, lambda b: sent_block(mixf, s_a, r_a, rows_at(b, TB, TB), b))
    wait_parts(s_p, r_p)
    reduce_back(s_r2, r_r2, s_p2, r_p2, ret2)

    ger = mixf
    for copy in store_grads():
        copy.start()

    def finish_back(b):
        at = rows_at(b, TB, TB)
        wait_sums(s_p2, r_p2, b)
        ger[at, mine] = summed(at).astype(BF16)

        @pl.when(b >= 1)
        def _():
            spread_block(ger, s_g2, r_g2, rows_at(b - 1, TB, TB), b - 1)

    loop(0, blocks, finish_back)
    spread_block(ger, s_g2, r_g2, rows_at(blocks - 1, TB, TB), blocks - 1)

    for j in range(1, mp):
        src = place.zahead(j)
        remote(msg, rmsg.at[src], s_m.at[0], r_m.at[src], {"mp": src}).wait_recv()
    grad_probs = rmsg[0]
    for j in range(1, mp):
        grad_probs = grad_probs + rmsg[j]
    loss_ref[...] = grad_probs[experts : experts + 8, 0:128] / (tokens * width)
    grad_probs = grad_probs[0:experts]
    gates = grow_t[0:experts, :]
    grow_t[0:experts, :] = grad_probs - gates * jnp.sum(grad_probs, axis=0, keepdims=True)
    vec_ref[...] = jnp.zeros_like(vec_ref)
    gk[...] = jnp.zeros_like(gk)
    gv[...] = jnp.zeros_like(gv)
    gwo_ref[...] = jnp.zeros_like(gwo_ref)

    def back(b):
        at = rows_at(b, TB, TB)
        @pl.when(b == 0)
        def _():
            pass_block(ger, s_g2, r_g2, rows_at(0, TB, TB), 0)

        for j in range(1, mp):
            wait_block(ger, s_g2, r_g2, at, b, place.zahead(j))
        @pl.when(b + 1 < blocks)
        def _():
            pass_block(ger, s_g2, r_g2, rows_at(b + 1, TB, TB), b + 1)

        normal, inverse = standardize(hid[at, :])
        normed = normal * g2_ref[...] + b2_ref[...]
        logits = grow_t[0:experts, at]
        vec_ref[8 : 8 + experts, :] += dot(logits, normed, HIGHEST)
        grad = dot_tn(logits, rt_ref[...], HIGHEST) + ger[at, :].astype(F32)
        vec_ref[2:3, :] += jnp.sum(grad * normal, axis=0, keepdims=True)
        vec_ref[3:4, :] += jnp.sum(grad, axis=0, keepdims=True)
        scaled = grad * g2_ref[...]
        out = gf[at, :].astype(F32) + inverse * (
            scaled
            - jnp.mean(scaled, axis=-1, keepdims=True)
            - normal * jnp.mean(scaled * normal, axis=-1, keepdims=True)
        )
        hid[at, :] = out
        attended = out.astype(BF16)

        gwo_ref[...] += dot(mixt[:, at], attended)
        mix_t = dot_nt(wo_ref[...], attended)
        mix_low = jnp.transpose(mix_t).astype(BF16)
        mix_t = mix_t.astype(BF16)
        query = jnp.transpose(turned[0:share, at].astype(F32)).astype(BF16)
        grad_query = []
        for h in range(heads):
            low_probs = probs[h, :, at]
            wide = low_probs.astype(F32)
            grad_probs = dot(values[...], only(mix_t, head_row, h))
            centre = jnp.sum(grad_probs * wide, axis=0, keepdims=True)
            grad_scores = (wide * (grad_probs - centre)).astype(BF16)
            low = share + h * HEAD_DIM
            grad_query.append(dot(turned[low : low + HEAD_DIM, :], grad_scores))
            gk[...] += dot(grad_scores, only(query, head_lane, h))
            gv[...] += dot(low_probs, only(mix_low, head_lane, h))
        flat = jnp.concatenate(grad_query, axis=0)
        gt[0:share, at] = flat.astype(BF16) * 0.125
        gflat[at, 0:share] = jnp.transpose(flat).astype(BF16) * 0.125

    loop(0, blocks, back)

    part = n2b

    def part_z(b, f):
        at = rows_at(b, TB, TB)
        dst, slot = route(f)
        return remote(
            part.at[at, lanes(f, share)], rbuf.at[slot, at, :], s_z.at[b, f], r_z.at[b, slot], {"mp": dst}
        )

    def wait_z(b, slot):
        at = rows_at(b, TB, TB)
        remote(
            part.at[at, mine], rbuf.at[slot, at, :], s_z.at[0, 0], r_z.at[b, slot], {"mp": z}
        ).wait_recv()

    far_first = (3, 0, 2, 1)

    def send_parts(b):
        for f in far_first:

            @pl.when((z != f) & (z != adder[f]))
            def _(f=f):
                part_z(b, f).start()

    def add_parts(b):
        at = rows_at(b, TB, TB)
        for f in far_first:

            @pl.when(z == adder[f])
            def _(f=f):
                wait_z(b, add_slot[f])
                cut = lanes(f, share)
                part[at, cut] = (
                    part[at, cut].astype(F32) + rbuf[add_slot[f], at, :].astype(F32)
                ).astype(BF16)

    def send_added(b):
        for f in far_first:

            @pl.when(z == adder[f])
            def _(f=f):
                part_z(b, f).start()

    vz[...] = jnp.zeros_like(vz)

    def first_back(b):
        at = rows_at(b, TB, TB)
        gflat[at, share : 2 * share] = gk[at, :].astype(BF16)
        gflat[at, 2 * share : 3 * share] = gv[at, :].astype(BF16)
        grad = dot_nt(gflat[at, :], wcat[...])
        part[at, :] = grad.astype(BF16)
        normal, _ = standardize(x_ref[at, :].astype(F32))
        scaled = grad * g1_ref[...]
        crossed = grad * normal
        lane = lax.broadcasted_iota(I32, (TB, 128), 1)
        sums = jnp.where(
            lane == 0,
            jnp.sum(scaled, axis=1, keepdims=True),
            jnp.where(lane == 1, jnp.sum(scaled * normal, axis=1, keepdims=True), 0.0),
        )
        small[:, at] = jnp.transpose(sums)[0:8]
        vz[0:1, :] += jnp.sum(crossed, axis=0, keepdims=True)
        vz[1:2, :] += jnp.sum(grad, axis=0, keepdims=True)

        @pl.when(b >= 1)
        def _():
            send_parts(b - 1)

    loop(0, blocks, first_back)

    def vz_copy(j):
        return remote(vz, rvz.at[z], s_v.at[j], r_v.at[z], {"mp": place.zahead(j)})

    def small_copy(j):
        return remote(small, rsmall.at[z], s_s.at[j], r_s.at[z], {"mp": place.zahead(j)})

    for j in range(1, mp):
        vz_copy(j).start()
    send_parts(blocks - 1)
    for j in range(1, mp):
        small_copy(j).start()
    rvz[z] = vz[...]
    rsmall[z] = small[...]

    def turn(b):
        at = rows_at(b, TB, TB)
        gt[share : 2 * share, at] = jnp.transpose(gk[at, :]).astype(BF16)
        gt[2 * share : 3 * share, at] = jnp.transpose(gv[at, :]).astype(BF16)

    loop(0, blocks, turn)
    wpk[0 : 3 * share, :] = dot(gt[...], a1[...]).astype(BF16)
    wpk[3 * share : 4 * share, :] = gwo_ref[...].astype(BF16)
    wrows = 4 * share // n

    def w_copy(k):
        p = place.peer(k)
        return remote(
            wpk.at[rows_at(p, wrows, 16)], rw.at[me], s_w.at[k], r_w.at[k], place.plane(p)
        )

    each(n, lambda k: w_copy(k).start())
    rw[me] = wpk[rows_at(me, wrows, 16), :]

    add_parts(0)
    add_parts(1)
    send_added(0)

    for j in range(1, mp):
        src = place.zahead(j)
        remote(vz, rvz.at[src], s_v.at[0], r_v.at[src], {"mp": src}).wait_recv()
    total_vz = rvz[0]
    for j in range(1, mp):
        total_vz = total_vz + rvz[j]
    vsend[...] = vec_ref[...].astype(BF16)
    vsend[0:2, :] = total_vz[0:2].astype(BF16)

    def v_copy(k):
        return remote(vsend, rvec.at[me], s_c.at[k], r_c.at[k], place.plane(place.peer(k)))

    rvec[me] = vsend[...]
    each(n, lambda k: v_copy(k).start())

    def w_wait(k):
        src = place.peer(k)
        remote(
            wpk.at[rows_at(0, wrows, 16)], rw.at[src], s_w.at[k], r_w.at[k], place.plane(src)
        ).wait_recv()

    each(n, w_wait)
    acc = rw[0].astype(F32)
    for p in range(1, n):
        acc = acc + rw[p].astype(F32)
    wall[rows_at(me, wrows, 16), :] = acc.astype(BF16)

    def e_copy(k):
        at = rows_at(me, wrows, 16)
        return remote(wall.at[at], wall.at[at], s_e.at[k], r_e.at[k], place.plane(place.peer(k)))

    each(n, lambda k: e_copy(k).start())
    send_added(1)
    add_parts(2)
    add_parts(3)
    send_added(2)

    def v_wait(k):
        src = place.peer(k)
        remote(vsend, rvec.at[src], s_c.at[k], r_c.at[k], place.plane(src)).wait_recv()

    each(n, v_wait)
    acc = rvec[0].astype(F32)
    for p in range(1, n):
        acc = acc + rvec[p].astype(F32)
    vec_ref[...] = acc
    send_added(3)

    def e_wait(k):
        src = place.peer(k)
        at = rows_at(src, wrows, 16)
        remote(wall.at[at], wall.at[at], s_e.at[k], r_e.at[k], place.plane(src)).wait_recv()

    each(n, e_wait)
    for j in range(1, mp):
        src = place.zahead(j)
        remote(small, rsmall.at[src], s_s.at[0], r_s.at[src], {"mp": src}).wait_recv()
    means = rsmall[0]
    for j in range(1, mp):
        means = means + rsmall[j]
    small_sum = means / width
    rsmall[z] = small_sum

    def last(b):
        at = rows_at(b, TB, TB)
        for src in sources:
            wait_z(b, src)
        inputs = x_ref[at, :].astype(F32)
        center = jnp.mean(inputs, axis=-1, keepdims=True)
        spread = inputs - center
        inverse = lax.rsqrt(jnp.mean(spread * spread, axis=-1, keepdims=True) + EPSILON)
        normal = (x_ref[at, mine].astype(F32) - center) * inverse
        grad = part[at, mine].astype(F32)
        for src in sources:
            grad = grad + rbuf[src, at, :].astype(F32)
        flat = jnp.concatenate([rsmall[z, :, at], jnp.zeros((120, TB), F32)], axis=0)
        columns = jnp.transpose(flat)
        gin_ref[at, :] = hid[at, mine] + inverse * (
            grad * g1_ref[:, mine] - columns[:, 0:1] - normal * columns[:, 1:2]
        )

    loop(0, blocks, last)

    for copy in store_grads():
        copy.wait()

    @pl.when(me < pieces)
    def _():
        for j in range(1, mp):
            out_weight_z(j).wait_send()
            src = place.zahead(j)
            loop(1, n, lambda k, src=src: out_weight_plane(src, k).wait_send())

    for j in range(1, mp):
        remote(msg, rmsg.at[z], s_m.at[j], r_m.at[z], {"mp": place.zahead(j)}).wait_send()
        vz_copy(j).wait_send()
        small_copy(j).wait_send()
    for f in range(mp):

        @pl.when(z != f)
        def _(f=f):
            loop(0, blocks, lambda b: part_z(b, f).wait_send())

    loop(0, blocks, lambda b: sent_block(gf, s_g, r_g, rows_at(b, TB, TB), b))
    loop(0, blocks, lambda b: sent_block(ger, s_g2, r_g2, rows_at(b, TB, TB), b))
    wait_returns(s_r2, r_r2)
    wait_parts(s_p2, r_p2)
    each(n, lambda k: w_copy(k).wait_send())
    each(n, lambda k: v_copy(k).wait_send())
    each(n, lambda k: e_copy(k).wait_send())


def layer(dims, capacity, experts, *args):
    x = args[0]
    dp, ex, mp = dims
    n = dp * ex
    tokens, width = x.shape
    share = width // mp
    hidden = args[-1].shape[0]
    room = -(-capacity // 16) * 16
    while (room * n) % 128:
        room += 16
    slots = n * room
    msgs = experts + 8
    blocks = tokens // TB
    heads = share // HEAD_DIM
    dma = pltpu.SemaphoreType.DMA
    vm = pltpu.VMEM
    scratch = [
        vm((width, hidden), F32),
        vm((hidden, width), F32),
        vm((share, width), F32),
        vm((tokens, width), BF16),
        vm((width, 3 * share), BF16),
        vm((tokens, share), BF16),
        vm((tokens, share), BF16),
        vm((3 * share, tokens), BF16),
        vm((share, tokens), BF16),
        vm((heads, tokens, tokens), BF16),
        vm((tokens, share), F32),
        vm((tokens, share), F32),
        vm((3 * share, tokens), BF16),
        vm((tokens, 3 * share), BF16),
        vm((4 * share, width), BF16),
        vm((n, 4 * share // n, width), BF16),
        vm((8, tokens), F32),
        vm((mp, 8, tokens), F32),
        vm((8, width), F32),
        vm((mp, 8, width), F32),
        vm((8 + experts, width), BF16),
        vm((n, 8 + experts, width), BF16),
        vm((tokens, width), BF16),
        vm((width, width), BF16),
        vm((tokens, width), F32),
        vm((tokens, width), BF16),
        vm((tokens, 128), F32),
        vm((8, tokens), F32),
        vm((experts, tokens), F32),
        vm((slots, tokens), BF16),
        vm((tokens, slots), BF16),
        vm((slots, width), BF16),
        vm((slots, width), BF16),
        vm((slots, hidden), BF16),
        vm((slots, hidden), BF16),
        vm((slots, width), BF16),
        vm((slots, width), BF16),
        vm((mp, tokens, share), BF16),
        vm((mp, tokens, share), BF16),
        vm((tokens, share), F32),
        vm((tokens, share), F32),
        vm((tokens, width), BF16),
        vm((slots, width), BF16),
        vm((slots, hidden), BF16),
        vm((msgs, tokens), F32),
        vm((mp, msgs, tokens), F32),
        vm((slots, share), F32),
        dma((blocks, mp)),
        dma((blocks, mp)),
        dma((n,)),
        dma((n,)),
        dma((mp, n)),
        dma((mp, n)),
        dma((mp, blocks)),
        dma((mp, blocks)),
        dma((blocks, mp)),
        dma((blocks, mp)),
        dma((mp, n)),
        dma((mp, n)),
        dma((mp, n)),
        dma((mp, n)),
        dma((mp, blocks)),
        dma((mp, blocks)),
        dma((blocks, mp)),
        dma((blocks, mp)),
        dma((mp,)),
        dma((mp,)),
        dma((mp,)),
        dma((mp,)),
        dma((mp, n)),
        dma((mp, n)),
        dma((blocks, mp)),
        dma((blocks, mp)),
        dma((mp,)),
        dma((mp,)),
        dma((mp,)),
        dma((mp,)),
        dma((n,)),
        dma((n,)),
        dma((n,)),
        dma((n,)),
        dma((n,)),
        dma((n,)),
        dma((2,)),
    ]
    shapes = (
        jax.ShapeDtypeStruct((tokens, share), BF16),
        jax.ShapeDtypeStruct((8, 128), F32),
        jax.ShapeDtypeStruct((tokens, share), F32),
        jax.ShapeDtypeStruct((4 * share, width), BF16),
        jax.ShapeDtypeStruct((8 + experts, width), F32),
        jax.ShapeDtypeStruct((width, hidden), F32),
        jax.ShapeDtypeStruct((hidden, width), F32),
    )
    spec = pl.BlockSpec(memory_space=pltpu.VMEM)
    return pl.pallas_call(
        functools.partial(layer_kernel, dims, capacity, experts),
        out_shape=shapes,
        in_specs=[spec] * len(args),
        out_specs=[spec] * 5 + [pl.BlockSpec(memory_space=pl.ANY)] * 2,
        scratch_shapes=scratch,
        compiler_params=pltpu.CompilerParams(
            collective_id=0, has_side_effects=True, vmem_limit_bytes=VMEM_LIMIT
        ),
        name="layer",
    )(*args)


def results_kernel(
    experts,
    share,
    out,
    loss,
    gin,
    wall,
    vec,
    gwin,
    gwout,
    out_o,
    loss_o,
    gin_o,
    gq_o,
    gk_o,
    gv_o,
    go_o,
    router_o,
    gwin_o,
    gwout_o,
    g1_o,
    b1_o,
    g2_o,
    b2_o,
):
    out_o[...] = out[...]
    gin_o[...] = gin[...]
    gwin_o[...] = gwin[...]
    gwout_o[...] = gwout[...]
    sums = wall[...].astype(F32)
    for i, ref in enumerate((gq_o, gk_o, gv_o)):
        ref[...] = jnp.transpose(sums[i * share : (i + 1) * share])
    go_o[...] = sums[3 * share : 4 * share]

    @pl.when(pl.program_id(0) == 0)
    def _():
        loss_o[...] = loss[0:1, :]
        router_o[...] = vec[8 : 8 + experts, :]
        for i, ref in enumerate((g1_o, b1_o, g2_o, b2_o)):
            ref[...] = vec[i]


def results(experts, steps, out, loss, gin, wall, vec, gwin, gwout):
    tokens, share = out.shape
    width = wall.shape[1]
    hidden = gwin.shape[1]

    def across(shape):
        return pl.BlockSpec((shape[0], shape[1] // steps), lambda i: (0, i))

    def down(shape):
        return pl.BlockSpec((shape[0] // steps, shape[1]), lambda i: (i, 0))

    def once(shape):
        return pl.BlockSpec(shape, lambda i: (0,) * len(shape))

    square = (width, share)
    shapes = (
        ((tokens, share), BF16, down),
        ((1, 128), F32, once),
        ((tokens, share), F32, down),
        (square, F32, down),
        (square, F32, down),
        (square, F32, down),
        ((share, width), F32, across),
        ((experts, width), F32, once),
        ((width, hidden), F32, down),
        ((hidden, width), F32, down),
        ((width,), F32, once),
        ((width,), F32, once),
        ((width,), F32, once),
        ((width,), F32, once),
    )
    return pl.pallas_call(
        functools.partial(results_kernel, experts, share),
        grid=(steps,),
        out_shape=[jax.ShapeDtypeStruct(shape, kind) for shape, kind, _ in shapes],
        in_specs=[
            down(out.shape),
            once(loss.shape),
            down(gin.shape),
            across(wall.shape),
            once(vec.shape),
            down(gwin.shape),
            down(gwout.shape),
        ],
        out_specs=[how(shape) for shape, _, how in shapes],
        name="results",
    )(out, loss, gin, wall, vec, gwin, gwout)


def per_device(
    dims,
    inputs,
    teacher,
    top_experts,
    priority,
    valid_mask,
    blocks,
    query_weight,
    key_weight,
    value_weight,
    out_weight,
    router,
    expert_in,
    expert_out,
    first_gain,
    first_bias,
    second_gain,
    second_bias,
):
    experts = router.shape[1]
    capacity = inputs.shape[0] * 2 * 21 // (20 * experts)
    kept = layer(
        dims,
        capacity,
        experts,
        inputs,
        blocks,
        query_weight,
        key_weight,
        value_weight,
        out_weight,
        first_gain[None],
        first_bias[None],
        second_gain[None],
        second_bias[None],
        router.T,
        top_experts.T,
        priority,
        valid_mask[None],
        teacher,
        expert_in[0],
        expert_out[0],
    )
    done = list(results(experts, 2, *kept))
    done[1] = done[1][0, 0:1]
    done[7] = done[7].T
    done[8] = done[8][None]
    done[9] = done[9][None]
    return tuple(done)


def solution(mesh):
    dims = (mesh.shape["dp"], mesh.shape["expert"], mesh.shape["mp"])
    both = ("dp", "expert")
    in_specs = (
        P(both, None),
        P(both, "mp"),
        P(both, None),
        P(both, None),
        P(both),
        P(both, None),
        P(None, "mp"),
        P(None, "mp"),
        P(None, "mp"),
        P("mp", None),
        P(),
        P(both, None, "mp"),
        P(both, "mp", None),
        P(),
        P(),
        P(),
        P(),
    )
    out_specs = (
        P(both, "mp"),
        P(both),
        P(both, "mp"),
        P(None, "mp"),
        P(None, "mp"),
        P(None, "mp"),
        P("mp", None),
        P(),
        P(both, None, "mp"),
        P(both, "mp", None),
        P(),
        P(),
        P(),
        P(),
    )
    return jax.shard_map(
        functools.partial(per_device, dims),
        mesh=mesh,
        in_specs=in_specs,
        out_specs=out_specs,
        check_vma=False,
    )
```
